32 devices in a mesh: dp: 2 (over y), ctx: 4 (over x, core), exp: 4 (over z).
Axes of the slice: x: 2, y: 2, z: 4, core: 2. Of those that a mesh axis runs over, the one named last changes fastest.
Arguments:
- tokens: bfloat16 [2, 2048, 768], P('dp', ('ctx', 'exp')), may hold values from -6 to 6
- lengths: int32 [2], P('dp'), may hold values from 512 to 2048, as said below
- routes: int32 [2, 2048, 2], P('dp', ('ctx', 'exp')), may hold values from 0 to 3, all different within a row; in each aligned block of 128 rows (0 to 127, 128 to 255, ..., all dimensions but the last counted through in order) at most 80 rows name the same one
- buckets: int32 [2048], replicated, may hold values from 0 to 31, never falling along the last dimension, each value on 1 to 128 neighbouring positions
- cotangent: bfloat16 [2, 2048, 768], P('dp', ('ctx', 'exp')), may hold values from -6 to 6
- attn_gain: float32 [768], replicated, may hold values from 0.5 to 1.5
- w_qkv: bfloat16 [768, 2304], replicated, may hold values from -0.21875 to 0.21875
- w_attn_out: bfloat16 [768, 768], replicated, may hold values from -6 to 6
- rel_bias: float32 [32, 12], replicated, may hold values from -4 to 4
- ffn_gain: float32 [768], replicated, may hold values from 0.5 to 1.5
- w_router: float32 [768, 4], replicated, may hold values from -0.4375 to 0.4375
- w_up: bfloat16 [4, 768, 3072], P('exp'), may hold values from -0.21875 to 0.21875
- w_down: bfloat16 [4, 3072, 768], P('exp'), may hold values from -0.109375 to 0.109375
Outputs:
- output: bfloat16 [2, 2048, 768], P('dp', ('ctx', 'exp'))
- grad_tokens: float32 [2, 2048, 768], P('dp', ('ctx', 'exp'))
- grad_attn_gain: float32 [768], replicated
- grad_qkv: float32 [768, 2304], replicated
- grad_attn_out: float32 [768, 768], replicated
- grad_rel_bias: float32 [32, 12], replicated
- grad_ffn_gain: float32 [768], replicated
- grad_router: float32 [768, 4], replicated
- grad_up: float32 [4, 768, 3072], P('exp')
- grad_down: float32 [4, 3072, 768], P('exp')
The draws below stay inside these ranges and needn't reach their ends.
Inputs may be any that keep to these rules, and one draw needn't show every extreme that they name: `lengths`: the valid tokens of a slot are its first positions, at least a quarter of the slot; some slot is always full. `routes`: each token names two different experts; among the 128 rows of one device no expert is named more than 80 times. `buckets`: never falls as the distance grows, starting at 0.
All inputs are finite; a program needn't handle non-finite values.
Results may differ from the reference program's by a relative error of at most 0.035.
Values may be sent and summed in bfloat16 or wider, within the bound.
No kernel may reach another device: no remote copies, remote signals or barrier semaphores. Data moves between devices by JAX's collectives and lax.ppermute only.
A program may use at most 256 MiB of HBM per device.

```python
import math
import jax
import jax.numpy as jnp
import numpy as np
from jax import lax

D = 768
H = 12
FF = 3072
NB = 32
TOK_DEV = 128
EXPERTS = 4
SEQ = 2048
SLOTS = 2
CAP = 80


def draw_lengths(key, part):
    first_key, second_key = jax.random.split(jax.random.fold_in(key, 11))
    counts = jax.random.randint(first_key, (SLOTS,), SEQ // 4, SEQ + 1)
    full_slot = jax.random.randint(second_key, (), 0, SLOTS)
    return jnp.where(jnp.arange(SLOTS) == full_slot, SEQ, counts).astype(jnp.int32)


def block_levels(stream_key, shape, pieces, low, high):
    level = 1.0
    for position, parts in pieces:
        draws = jax.random.uniform(jax.random.fold_in(jax.random.fold_in(stream_key, 6), position), (parts,), jnp.float32, low / len(pieces), high / len(pieces))
        level = level * jnp.repeat(jnp.exp(draws), shape[position] // parts).reshape((-1,) + (1,) * (len(shape) - 1 - position))
    return level


def profile(count, total, reach, lean):
    portions = [(1 << 20) // math.isqrt(standing ** lean) + 1 for standing in range(2, count + 1)]
    spare, given = total - reach - (count - 1), [1] * (count - 1)
    while spare > 0:
        free = [i for i in range(count - 1) if given[i] < reach]
        mass, remaining = sum([portions[i] for i in free]), spare
        for i in free:
            addition = min(reach - given[i], max(1, remaining * portions[i] // mass), spare)
            given[i] = given[i] + addition
            spare = spare - addition
    return np.array([reach] + given)


def ragged_sizes(rng, number_of, total, limit, lean):
    if number_of == 2:
        one = jax.random.randint(rng, (), max(1, total - limit), min(limit, total - 1) + 1)
        return jnp.stack([one, total - one])
    sizes = jnp.asarray(profile(number_of, total, limit, lean), jnp.int32)
    couples = (number_of - 1) // 2
    giver, sink = sizes[1:1 + 2 * couples:2], sizes[2:2 + 2 * couples:2]
    slack = jnp.minimum(giver - 1, limit - sink)
    shifted = jax.random.randint(jax.random.fold_in(rng, 1), (couples,), 0, 1 << 20) % (slack + 1)
    sizes = sizes.at[1:1 + 2 * couples:2].set(giver - shifted).at[2:2 + 2 * couples:2].set(sink + shifted)
    return sizes[jax.random.permutation(jax.random.fold_in(rng, 2), number_of)]


def assign_block(rng, own, number, rows, amount, top, reach, lean):
    order = jax.random.permutation(rng, amount)
    heavy_load, usual = shares(amount, rows * top, reach, lean, True), shares(amount, rows * top, reach, lean, False)
    places = jnp.arange(amount)

    def named(sizes, rotation):
        used = int((sizes > 0).sum())
        fixed = max(1, used // 4)
        shifted = fixed + (places - fixed + rotation * (used - fixed)) % max(1, amount - fixed)
        return jnp.zeros((amount,), jnp.int32).at[order[jnp.where(places < fixed, places, shifted)]].set(jnp.asarray(sizes, jnp.int32))

    sizes = jnp.where(number % 4 == 0, named(heavy_load, number // 4), named(usual, number - number // 4 - 1))
    mixed = jax.random.permutation(jax.random.fold_in(own, 3), amount)
    giver, sink = mixed[0:amount // 2 * 2:2], mixed[1:amount // 2 * 2:2]
    slack = jnp.minimum(sizes[giver] - 1, reach - sizes[sink]) // 2
    slack = jnp.where((giver == order[0]) | (sink == order[0]) | (sizes[sink] == 0), 0, jnp.maximum(slack, 0))
    shifted = jax.random.randint(jax.random.fold_in(own, 4), (amount // 2,), 0, 1 << 20) % (slack + 1)
    sizes = sizes.at[giver].add(-shifted).at[sink].add(shifted)
    members = jnp.searchsorted(jnp.cumsum(sizes), jnp.arange(rows * top), side="right").astype(jnp.int32)
    table = members.reshape(top, rows).T
    table = table[jax.random.permutation(jax.random.fold_in(own, 1), rows)]
    rotation = jax.random.randint(jax.random.fold_in(own, 2), (rows, 1), 0, top)
    return jnp.take_along_axis(table, (jnp.arange(top)[None, :] + rotation) % top, axis=1)


def shares(count, total, most, slope, full):
    weights = [(1 << 20) // math.isqrt(grade ** slope) + 1 for grade in range(1, count + 1)]
    largest = most if full else min(most, max(-(-total // count), total * weights[0] // sum(weights)))
    least = 1 if total - largest >= count - 1 else 0
    given, spare = [largest] + [least] * (count - 1), total - largest - least * (count - 1)
    while spare > 0:
        candidates = [i for i in range(1, count) if given[i] < largest] or [i for i in range(1, count) if given[i] < most]
        whole, budget = sum([weights[i] for i in candidates]), spare
        for i in candidates:
            more = min(most - given[i], max(1, budget * weights[i] // whole), spare)
            given[i] = given[i] + more
            spare = spare - more
    return np.array(given)


def centred(own_key, extent, scale, bound, pieces=(), held_as=jnp.bfloat16):
    values = scale * jax.random.normal(own_key, extent, jnp.float32)
    if pieces:
        values = values * block_levels(own_key, extent, pieces, -0.22, 0.18)
    return jnp.clip(values, -bound, bound).astype(held_as)


def setup_inputs(seed: int = 0) -> dict:
    keys = jax.random.split(jax.random.key(seed), 14)
    tokens = centred(keys[0], (SLOTS, SEQ, D), 1.0, 6.0, ((0, 2), (1, 16)))
    lengths = draw_lengths(jax.random.fold_in(keys[13], 71), 0)
    routes_keys = jax.random.split(jax.random.fold_in(keys[2], 1), SLOTS * SEQ // TOK_DEV)
    routes_turns = jax.random.permutation(jax.random.fold_in(keys[2], 3), SLOTS * SEQ // TOK_DEV)
    routes = jax.vmap(lambda own, number: assign_block(jax.random.fold_in(keys[2], 2), own, number, TOK_DEV, EXPERTS, 2, CAP, 1))(routes_keys, routes_turns).reshape((SLOTS, SEQ, 2))
    buckets = jnp.searchsorted(jnp.cumsum(ragged_sizes(keys[3], NB, SEQ, 2 * SEQ // NB, 0)), jnp.arange(SEQ), side="right").astype(jnp.int32)
    cotangent = centred(keys[4], (SLOTS, SEQ, D), 1.0, 6.0, ((0, 2), (1, 16)))
    attn_gain = jnp.clip(1.0 + 0.1 * jax.random.normal(keys[5], (D,), jnp.float32), 0.5, 1.5)
    w_qkv = centred(keys[6], (D, 3 * D), D ** -0.5, 0.21875)
    w_attn_out = centred(keys[7], (D, D), 1 ** -0.5, 6.0)
    rel_bias = centred(keys[8], (NB, H), 1.0, 4.0, (), jnp.float32)
    ffn_gain = jnp.clip(1.0 + 0.1 * jax.random.normal(keys[9], (D,), jnp.float32), 0.5, 1.5)
    w_router = centred(keys[10], (D, EXPERTS), (D // 4) ** -0.5, 0.4375, (), jnp.float32)
    w_up = centred(keys[11], (EXPERTS, D, FF), D ** -0.5, 0.21875, ((0, 4),))
    w_down = centred(keys[12], (EXPERTS, FF, D), FF ** -0.5, 0.109375, ((0, 4),))
    return dict(tokens=tokens, lengths=lengths, routes=routes, buckets=buckets, cotangent=cotangent, attn_gain=attn_gain, w_qkv=w_qkv, w_attn_out=w_attn_out, rel_bias=rel_bias, ffn_gain=ffn_gain, w_router=w_router, w_up=w_up, w_down=w_down)


epsilon = 1e-06

@jax.custom_vjp
def low(v):
    return lax.optimization_barrier(v.astype(jnp.bfloat16)).astype(jnp.float32)

@jax.custom_vjp
def low_back(v):
    return v

def low_keep(v):
    return (low(v), None)

def low_pass(kept, grad):
    return (grad,)

def back_keep(v):
    return (v, None)

def back_low(kept, grad):
    return (low(grad),)
low.defvjp(low_keep, low_pass)
low_back.defvjp(back_keep, back_low)

def normed(values, gain):
    return values * lax.rsqrt(lax.optimization_barrier(jnp.mean(values * values, axis=-1, keepdims=True)) + epsilon) * gain

def gelu_tanh(values):
    return jax.nn.gelu(values, approximate=True)

def attention_slot(queries, key_rows, value_rows, rel_bias, buckets, length):
    seq_len = queries.shape[0]
    q_block = math.gcd(seq_len, 512)
    key_pos = jnp.arange(seq_len, dtype=jnp.int32)

    def one_block(index):
        first_row = index * q_block
        block_q = lax.dynamic_slice_in_dim(queries, first_row, q_block, 0)
        query_pos = first_row + jnp.arange(q_block, dtype=jnp.int32)
        distance = query_pos[:, None] - key_pos[None, :]
        bucket_ids = jnp.take(buckets, jnp.clip(distance, 0, seq_len - 1))
        biases = jnp.transpose(jnp.take(rel_bias, bucket_ids, axis=0), (2, 0, 1))
        scores = jnp.einsum('qhd,khd->hqk', block_q, key_rows, precision=lax.Precision.HIGHEST) * 0.125 + biases
        scores = low_back(scores)
        allowed = (distance >= 0) & (key_pos[None, :] < length)
        scores = jnp.where(allowed[None], scores, -1e+30)
        attn_probs = jax.nn.softmax(scores, axis=-1)
        return jnp.einsum('hqk,khd->qhd', low(attn_probs), value_rows, precision=lax.Precision.HIGHEST)
    blocks = lax.map(jax.checkpoint(one_block), jnp.arange(seq_len // q_block, dtype=jnp.int32))
    return blocks.reshape(seq_len, queries.shape[1], queries.shape[2])

def expert_layer(first_rows, second_rows, expert_ids, w_up, w_down):

    def one_expert(inputs, up_weight, down_weight):
        up_proj = low_back(jnp.dot(inputs, up_weight, precision=lax.Precision.HIGHEST))
        hidden = low(gelu_tanh(up_proj))
        return jnp.dot(hidden, down_weight, precision=lax.Precision.HIGHEST)
    run_expert = jax.checkpoint(one_expert)
    first_out = jnp.zeros_like(first_rows)
    second_out = jnp.zeros_like(second_rows)
    for expert in range(w_up.shape[0]):
        first_pick = (expert_ids[:, 0] == expert)[:, None]
        second_pick = (expert_ids[:, 1] == expert)[:, None]
        inputs = jnp.where(first_pick, first_rows, jnp.where(second_pick, second_rows, 0.0))
        result = run_expert(inputs, w_up[expert], w_down[expert])
        first_out = first_out + jnp.where(first_pick, result, 0.0)
        second_out = second_out + jnp.where(second_pick, result, 0.0)
    return (first_out, second_out)

def forward(inputs, attn_gain, w_qkv, w_attn_out, rel_bias, ffn_gain, w_router, w_up, w_down, lengths, routes, buckets):
    seq_len, model_width = (inputs.shape[1], inputs.shape[2])
    heads_all = rel_bias.shape[1]
    head_dim = model_width // heads_all
    results = []
    for slot_index in range(inputs.shape[0]):
        slot_rows = inputs[slot_index]
        length = lengths[slot_index]
        expert_ids = routes[slot_index]
        valid_rows = (jnp.arange(seq_len, dtype=jnp.int32) < length).astype(slot_rows.dtype)[:, None]
        first_norm = low(normed(slot_rows, attn_gain))
        qkv = low_back(low(jnp.dot(first_norm, w_qkv, precision=lax.Precision.HIGHEST)))
        qkv = qkv.reshape(seq_len, heads_all, 3, head_dim)
        attn_heads = attention_slot(qkv[:, :, 0], qkv[:, :, 1], qkv[:, :, 2], rel_bias, buckets, length)
        attn_heads = low_back(low(attn_heads.reshape(seq_len, model_width)))
        branch = low_back(jnp.dot(attn_heads, w_attn_out, precision=lax.Precision.HIGHEST))
        middle = slot_rows + valid_rows * branch
        second_norm = low(normed(middle, ffn_gain))
        logits = jnp.dot(second_norm, w_router, precision=lax.Precision.HIGHEST)
        chosen = jnp.take_along_axis(logits, expert_ids, axis=1)
        gate_probs = jax.nn.softmax(chosen, axis=-1)
        first_out, second_out = expert_layer(low_back(second_norm), low_back(second_norm), expert_ids, w_up, w_down)
        first_out = low_back(low(first_out))
        second_out = low_back(low(second_out))
        expert_mix = gate_probs[:, 0:1] * first_out + gate_probs[:, 1:2] * second_out
        results.append(middle + valid_rows * expert_mix)
    return jnp.stack(results)

def reference(tokens, lengths, routes, buckets, cotangent, attn_gain, w_qkv, w_attn_out, rel_bias, ffn_gain, w_router, w_up, w_down):
    params = (tokens.astype(jnp.float32), attn_gain, w_qkv.astype(jnp.float32), w_attn_out.astype(jnp.float32), rel_bias, ffn_gain, w_router, w_up.astype(jnp.float32), w_down.astype(jnp.float32))

    def closed(*weights):
        return forward(*weights, lengths, routes, buckets)
    output, pullback = jax.vjp(closed, *params)
    grads = pullback(cotangent.astype(jnp.float32))
    return (output.astype(jnp.bfloat16), grads[0], grads[1], grads[2], grads[3], grads[4], grads[5], grads[6], grads[7], grads[8])
```

```python
import functools

import jax
import jax.numpy as jnp
from jax import lax
from jax.experimental import pallas as pl
from jax.experimental.pallas import tpu as pltpu
from jax.sharding import PartitionSpec as P

CAP = 80
EPS = 1e-06
NEG = -1e30
VMEM_LIMIT = 58 << 20
bf16 = jnp.bfloat16
f32 = jnp.float32
NN = ((1,), (0,))
NT = ((1,), (1,))
TN = ((0,), (0,))
GELU_C = 0.7978845608028654
GELU_A = 0.044715


def dot(left, right, dims):
    return lax.dot_general(left, right, (dims, ((), ())), preferred_element_type=f32)


def iota(shape, axis):
    return lax.broadcasted_iota(jnp.int32, shape, axis)


def norm_scale(values):
    return lax.rsqrt(jnp.mean(values * values, axis=-1, keepdims=True) + EPS)


def norm_back(values, gain, grad):
    scale = norm_scale(values)
    xhat = values * scale
    gxhat = grad * gain
    grad_in = scale * (gxhat - xhat * jnp.mean(gxhat * xhat, axis=-1, keepdims=True))
    return grad_in, xhat


def gelu_parts(u):
    square = u * u
    t = jnp.tanh(u * (GELU_C + (GELU_C * GELU_A) * square))
    half = 0.5 * (1.0 + t)
    slope = half + (0.5 * u) * (1.0 - t * t) * (GELU_C + (3.0 * GELU_C * GELU_A) * square)
    return u * half, slope


def split2(values):
    high = values.astype(bf16)
    return high, (values - high.astype(f32)).astype(bf16)


def params(limit=VMEM_LIMIT):
    return pltpu.CompilerParams(vmem_limit_bytes=limit)


def vmem():
    return pl.BlockSpec(memory_space=pltpu.VMEM)


def smem():
    return pl.BlockSpec(memory_space=pltpu.SMEM)


def call(kernel, outs, ins, scratch=(), cost=None, name=None):
    flops, size = cost if cost else (1 << 20, 1 << 20)
    return pl.pallas_call(
        kernel,
        out_shape=outs,
        in_specs=ins,
        out_specs=jax.tree.map(lambda _: vmem(), outs),
        scratch_shapes=list(scratch),
        compiler_params=params(),
        cost_estimate=pl.CostEstimate(flops=flops, bytes_accessed=size, transcendentals=0),
        name=name,
    )


def sds(shape, dtype):
    return jax.ShapeDtypeStruct(shape, dtype)


def route_kernel(n_experts, sc, routes, routes_t, dy, pick, pay):
    rows = dy.shape[0]
    width = dy.shape[1]
    first, second = routes_t[0:1, :], routes_t[1:2, :]
    eight = iota((8, rows), 0)
    named = jnp.where((first == eight) | (second == eight), 1.0, 0.0)
    upper = jnp.where(iota((rows, rows), 0) < iota((rows, rows), 1), 1.0, 0.0)
    rank = dot(named.astype(bf16), upper.astype(bf16), NN)
    slot = iota((CAP, rows), 0).astype(f32)
    for e in range(n_experts):
        hit = (named[e : e + 1] > 0.5) & (rank[e : e + 1] == slot)
        pick[e * CAP : (e + 1) * CAP, :] = jnp.where(hit, 1.0, 0.0).astype(bf16)
    all_pick = pick[...].astype(f32)
    valid = iota((1, rows), 1) < sc[0]
    live = jnp.where(valid, all_pick, 0.0).astype(bf16)
    pay[:, :width] = dot(live, dy[...], NN).astype(bf16)
    lane = iota((rows, 128), 1)
    kind = jnp.where(lane < 3 * n_experts, lane % n_experts, -1)
    pair = (routes[:, 0:1] == kind) | (routes[:, 1:2] == kind)
    pair = jnp.where(pair, 1.0, 0.0).astype(bf16)
    pay[:, width:] = dot(pick[...], pair, NN).astype(bf16)


def bias_tiles(rel, buckets, brow, tiles, n_buckets):
    n_tiles, side, _ = tiles.shape
    ids = buckets[...]
    row = jnp.zeros(ids.shape, f32)
    for b in range(n_buckets):
        row = jnp.where(ids == b, rel[b], row)
    brow[:, :side] = jnp.zeros((1, side), f32)
    brow[:, side:] = row
    for o in range(n_tiles):
        wide = jnp.broadcast_to(brow[:, o * side : (o + 2) * side], (side, 2 * side))
        tiles[o] = pltpu.roll(wide, 0, axis=1, stride=1, stride_axis=0)[:, side:]


def attn_kernel(n_pieces, n_buckets, head_dim, sc, rel, *refs):
    pieces = refs[:n_pieces]
    gain, weight, buckets = refs[n_pieces : n_pieces + 3]
    h1, qa, ka, va, qt, kt, out_t, lse = refs[n_pieces + 3 : n_pieces + 11]
    vt, brow, tiles = refs[n_pieces + 11 :]
    n_tiles, side, _ = tiles.shape
    length = sc[0]
    lane = iota((128, 128), 1)

    def rows_in(x, start):
        x = x.astype(f32)
        h = (x * norm_scale(x) * gain[...]).astype(bf16)
        h1[pl.ds(start, 128), :] = h
        qkv = dot(h, weight[...], NN).astype(bf16).astype(f32)
        q, k, v = qkv[:, :128] * 0.125, qkv[:, 128:256], qkv[:, 256:]
        live = jnp.where(start + iota((128, 128), 0) < length, 0.0, NEG)
        qa[pl.ds(start, 128), :] = jnp.where(lane == head_dim, 1.0, q).astype(bf16)
        ka[pl.ds(start, 128), :] = jnp.where(lane == head_dim, live, k).astype(bf16)
        va[pl.ds(start, 128), :] = v.astype(bf16)
        qt[:, pl.ds(start, 128)] = q.T[:head_dim].astype(bf16)
        kt[:, pl.ds(start, 128)] = k.T[:head_dim].astype(bf16)
        vt[:, pl.ds(start, 128)] = v.T[:head_dim].astype(bf16)

    for i, piece in enumerate(pieces):
        if piece.shape[0] == 128:
            rows_in(piece[...], pl.multiple_of(sc[1 + i], 128))
        else:

            def step(j, carry, piece=piece, i=i):
                part = piece[pl.ds(pl.multiple_of(j * 128, 128), 128), :]
                rows_in(part, pl.multiple_of(sc[1 + i] + j * 128, 128))
                return carry

            lax.fori_loop(0, piece.shape[0] // 128, step, 0)
    bias_tiles(rel, buckets, brow, tiles, n_buckets)
    blocks = side // 128

    def one_query_tile(qi, carry):
        q_start = pl.multiple_of(qi * side, side)
        q = qa[pl.ds(q_start, side), :]

        def fold(k_start, offset, state, diagonal):
            top, total, acc = state
            scores = dot(ka[pl.ds(k_start, side), :], q, NT) + tiles[offset]
            if diagonal:
                scores = jnp.where(iota((side, side), 0) <= iota((side, side), 1), scores, NEG)
            new_top = jnp.maximum(top, jnp.max(scores, axis=0, keepdims=True))
            probs = jnp.exp(scores - new_top)
            scale = jnp.exp(top - new_top)
            total = total * scale + jnp.sum(probs, axis=0, keepdims=True)
            acc = acc * scale + dot(vt[:, pl.ds(k_start, side)], probs.astype(bf16), NN)
            return new_top, total, acc

        state = (
            jnp.full((1, side), NEG, f32),
            jnp.zeros((1, side), f32),
            jnp.zeros((head_dim, side), f32),
        )
        state = fold(q_start, 0, state, True)

        def earlier(kj, state):
            return fold(pl.multiple_of(kj * side, side), qi - kj, state, False)

        top, total, acc = lax.fori_loop(0, qi, earlier, state)
        result = (acc / total).astype(bf16)
        lse[:, pl.ds(q_start, side)] = top + jnp.log(total)
        for b in range(blocks):
            out_t[qi * blocks + b] = result[:, b * 128 : (b + 1) * 128]
        return carry

    lax.fori_loop(0, n_tiles, one_query_tile, 0)


def attn_back_kernel(n_buckets, head_dim, n_dp, sc, rel, *refs):
    qa, ka, va, qt, kt, out_t, grad_t, lse, h1, buckets, shifted = refs[:11]
    pay, weight_pay = refs[11:13]
    dots, dq, dk, dv, full, brow, tiles, sums, diag = refs[13:]
    n_tiles, side, _ = tiles.shape
    blocks = side // 128
    bias_tiles(rel, buckets, brow, tiles, n_buckets)
    sums[...] = jnp.zeros_like(sums)
    dk[...] = jnp.zeros_like(dk)
    dv[...] = jnp.zeros_like(dv)

    def one_query_tile(qi, carry):
        q_start = pl.multiple_of(qi * side, side)
        q = qa[pl.ds(q_start, side), :]
        q_t = qt[:, pl.ds(q_start, side)]
        g_t = jnp.concatenate([grad_t[qi * blocks + b] for b in range(blocks)], axis=1)
        o_t = jnp.concatenate([out_t[qi * blocks + b] for b in range(blocks)], axis=1)
        row_dots = jnp.sum(g_t.astype(f32) * o_t.astype(f32), axis=0, keepdims=True)
        norm = lse[:, pl.ds(q_start, side)]

        def fold(k_start, offset, acc, diagonal):
            where_k = pl.ds(k_start, side)
            scores = dot(ka[where_k, :], q, NT) + tiles[offset]
            probs = jnp.exp(scores - norm)
            if diagonal:
                probs = jnp.where(iota((side, side), 0) <= iota((side, side), 1), probs, 0.0)
            grad_prob = dot(va[where_k, :][:, :head_dim], g_t, NN)
            grad_score = probs * (grad_prob - row_dots)
            low = grad_score.astype(bf16)
            sums[offset] = sums[offset] + grad_score
            dv[:, where_k] = dv[:, where_k] + dot(g_t, probs.astype(bf16), NT)
            dk[:, where_k] = dk[:, where_k] + dot(q_t, low, NT)
            return acc + dot(kt[:, where_k], low, NN)

        acc = fold(q_start, 0, jnp.zeros((head_dim, side), f32), True)

        def earlier(kj, acc):
            return fold(pl.multiple_of(kj * side, side), qi - kj, acc, False)

        dq[:, pl.ds(q_start, side)] = lax.fori_loop(0, qi, earlier, acc)
        return carry

    lax.fori_loop(0, n_tiles, one_query_tile, 0)
    full[:head_dim, :] = (dq[...] * 0.125).astype(bf16)
    full[head_dim : 2 * head_dim, :] = dk[...].astype(bf16)
    full[2 * head_dim :, :] = dv[...].astype(bf16)
    for b in range(pay.shape[0]):
        pay[b] = full[:, b * 128 : (b + 1) * 128]
    flip = jnp.where(iota((side, side), 0) + iota((side, side), 1) == side - 1, 1.0, 0.0)
    flip = flip.astype(bf16)
    diag[...] = jnp.zeros_like(diag)
    for o in range(n_tiles):
        high, low = split2(sums[o])
        turned = dot(flip, high, NN) + dot(flip, low, NN)
        wide = jnp.concatenate([turned, jnp.zeros((side, side), f32)], axis=1)
        lined = pltpu.roll(wide, 0, axis=1, stride=1, stride_axis=0)
        where_d = slice(o * side, (o + 2) * side)
        diag[:, where_d] = diag[:, where_d] + jnp.sum(lined, axis=0, keepdims=True)
    hot = jnp.where(shifted[...] == iota((128, shifted.shape[1]), 0), 1.0, 0.0).astype(bf16)
    high, low = split2(jnp.broadcast_to(diag[...], (8, diag.shape[1])))
    rel_grad = dot(high, hot, NT) + dot(low, hot, NT)
    grad_w = dot(full[...], h1[...], NN).astype(bf16)
    n_pay, pay_rows, lanes = weight_pay.shape
    n_ctx = n_pay // n_dp
    rows = grad_w.shape[0] // n_ctx
    rel_rows = jnp.concatenate([rel_grad, jnp.zeros((8, lanes - 128), f32)], axis=1)
    rel_rows = jnp.concatenate([rel_rows, jnp.zeros((8, lanes), f32)], axis=0).astype(bf16)
    for d in range(n_dp):
        for c in range(n_ctx):
            weight_pay[d * n_ctx + c, :rows, :] = grad_w[
                c * rows : (c + 1) * rows, d * lanes : (d + 1) * lanes
            ]
            weight_pay[d * n_ctx + c, rows:, :] = rel_rows


def middle_kernel(n_heads, sc, recv, w_out, x, gain, pick, middle, send):
    rows, width = x.shape
    attn_t = jnp.concatenate([recv[h] for h in range(n_heads)], axis=0)
    branch = dot(attn_t, w_out[...], TN)
    valid = iota((rows, 1), 0) < sc[0]
    mid = x[...].astype(f32) + jnp.where(valid, branch, 0.0)
    middle[...] = mid
    h2 = (mid * norm_scale(mid) * gain[...]).astype(bf16)
    send[...] = dot(pick[...], h2, NN).astype(bf16)


def gate_of(h2, pay, width, w3, own):
    logits = dot(h2, w3, NN)
    sel = 2.0 * own - pay[:, width:].astype(f32)
    diff = jnp.sum(logits * sel, axis=1, keepdims=True)
    return 1.0 / (1.0 + jnp.exp(-diff)), sel


def own_lanes(expert, n_experts):
    lane = iota((1, 128), 1)
    return jnp.where((lane < 3 * n_experts) & (lane % n_experts == expert), 1.0, 0.0)


def expert_kernel(
    n_experts, sc, h2, pay, w3, w3_t, w_up, w_down, mix, back, router, z_acc, in_acc, dz, gates
):
    step = pl.program_id(0)
    width = h2.shape[1]
    own = own_lanes(sc[0], n_experts)

    @pl.when(step == 0)
    def _():
        gate, _ = gate_of(h2[...], pay, width, w3[...], own)
        gates[...] = jnp.broadcast_to(gate, gates.shape)
        dz[...] = (gate * pay[:, :width].astype(f32)).astype(bf16)
        z_acc[...] = jnp.zeros_like(z_acc)
        in_acc[...] = jnp.zeros_like(in_acc)

    up = dot(h2[...], w_up[...], NN)
    act, slope = gelu_parts(up)
    grad_hidden = dot(dz[...], w_down[...], NT)
    grad_up = (grad_hidden * slope).astype(bf16)
    z_acc[...] += dot(act.astype(bf16), w_down[...], NN)
    in_acc[...] += dot(grad_up, w_up[...], NT)

    @pl.when(step == pl.num_programs(0) - 1)
    def _():
        gate = gates[:, 0:1]
        sel = 2.0 * own - pay[:, width:].astype(f32)
        z = z_acc[...].astype(bf16).astype(f32)
        mix[...] = (gate * z).astype(bf16)
        grad_gate = jnp.sum(pay[:, :width].astype(f32) * z, axis=1, keepdims=True)
        high, low = split2((gate * (1.0 - gate) * grad_gate) * sel)
        back[...] = (in_acc[...] + dot(high, w3_t[...], NN) + dot(low, w3_t[...], NN)).astype(bf16)
        router[...] = (dot(high, h2[...], TN) + dot(low, h2[...], TN))[:8]


def middle_back_kernel(
    n_heads, sc, back, pick, middle, dy, gain, recv, w_out, router, dmid, grad_t, red
):
    rows, width = middle.shape
    grad_h2 = dot(pick[...], back[...], TN)
    grad_in, xhat = norm_back(middle[...], gain[...], grad_h2)
    grad_mid = dy[...].astype(f32) + grad_in
    dmid[...] = grad_mid
    valid = iota((rows, 1), 0) < sc[0]
    branch = jnp.where(valid, grad_mid, 0.0).astype(bf16)
    attn_t = jnp.concatenate([recv[h] for h in range(n_heads)], axis=0)
    heads = dot(w_out[...], branch, NT).astype(bf16)
    head_dim = width // n_heads
    for h in range(n_heads):
        grad_t[h] = heads[h * head_dim : (h + 1) * head_dim]
    for h in range(n_heads, grad_t.shape[0]):
        grad_t[h] = jnp.zeros((head_dim, rows), bf16)
    red[:width, :] = dot(attn_t, branch, NN).astype(bf16)
    gains = jnp.sum(grad_h2 * xhat, axis=0, keepdims=True)
    small = jnp.concatenate([jnp.broadcast_to(gains, (8, width)), router[...]], axis=0)
    red[width : width + 16, :] = small.astype(bf16)
    rest = red.shape[0] - width - 16
    red[width + 16 :, :] = jnp.zeros((rest, width), bf16)


def output_kernel(sc, mix, pick, middle, out):
    rows = middle.shape[0]
    valid = iota((rows, 1), 0) < sc[0]
    total = dot(pick[...], mix[...], TN)
    out[...] = (middle[...] + jnp.where(valid, total, 0.0)).astype(bf16)


def token_grad_kernel(n_heads, recv, w_qkv, x, gain, dmid, out):
    grad_t = jnp.concatenate([recv[h] for h in range(n_heads)], axis=0)
    grad_h1 = dot(w_qkv[...], grad_t, NN).T
    grad_in, _ = norm_back(x[...].astype(f32), gain[...], grad_h1)
    out[...] = dmid[...] + grad_in


def weight_grad_kernel(n_experts, n_pieces, sc, *refs):
    h_pieces, p_pieces = refs[:n_pieces], refs[n_pieces : 2 * n_pieces]
    w3, w_up, w_down = refs[2 * n_pieces : 2 * n_pieces + 3]
    up_out, down_out, up_low, down_low = refs[2 * n_pieces + 3 : 2 * n_pieces + 7]
    h2, pay, dz, hid_t, dup_t, sem = refs[2 * n_pieces + 7 :]
    step = pl.program_id(0)
    rows = h_pieces[0].shape[0]
    width = h2.shape[1]

    @pl.when(step == 0)
    def _():
        copies = []
        for i in range(n_pieces):
            for j, (src, dst) in enumerate(((h_pieces[i], h2), (p_pieces[i], pay))):
                copy = pltpu.make_async_copy(
                    src, dst.at[pl.ds(i * rows, rows), :], sem.at[j, i]
                )
                copy.start()
                copies.append(copy)
        for copy in copies:
            copy.wait()
        own = own_lanes(sc[1], n_experts)
        gate, _ = gate_of(h2[...], pay, width, w3[...], own)
        dz[...] = (gate * pay[:, :width].astype(f32)).astype(bf16)

    up_t = w_up[...].T
    down = w_down[...]
    chunk = 512
    for r in range(0, h2.shape[0], chunk):
        act, slope = gelu_parts(dot(up_t, h2[r : r + chunk, :], NT))
        hid_t[:, r : r + chunk] = act.astype(bf16)
        grad_hidden = dot(down, dz[r : r + chunk, :], NT)
        dup_t[:, r : r + chunk] = (grad_hidden * slope).astype(bf16)
    grad_down = dot(hid_t[...], dz[...], NN)
    down_out[...] = grad_down
    down_low[...] = grad_down.astype(bf16)
    grad_up = dot(dup_t[...], h2[...], NN).T
    up_out[...] = grad_up
    up_low[...] = grad_up.astype(bf16)


def fill_kernel(sc, up_low, down_low, up_full, down_full, up_out, down_out):
    up_out[...] = up_low[...].astype(f32)
    down_out[...] = down_low[...].astype(f32)


def assemble_kernel(n_exp, rows, n_groups, head_cols, sc, *refs):
    n_pieces = (len(refs) - 7) // 1
    pieces = refs[:n_pieces]
    w_qkv, gain, grad, gain_grad, rel_grad, turned, rel_t = refs[n_pieces:]
    lanes = pieces[0].shape[-1]
    rel_t[...] = jnp.zeros_like(rel_t)
    slot = 0
    for piece in pieces:
        for i in range(piece.shape[0]):
            d, c, e = sc[3 * slot], sc[3 * slot + 1], sc[3 * slot + 2]
            slot += 1
            lane_at = pl.multiple_of(d * lanes, 128)
            for g in range(n_groups):
                head = g * n_exp + e
                row_at = pl.multiple_of(head * head_cols + c * rows, 16)
                turned[pl.ds(row_at, rows), pl.ds(lane_at, lanes)] = piece[
                    i, g * rows : (g + 1) * rows, :
                ]
                rel_t[pl.ds(head, 1), :] = piece[
                    i, n_groups * rows + g : n_groups * rows + g + 1, :128
                ].astype(f32)
    rel = rel_t[...].T
    rel_grad[...] = rel[: rel_grad.shape[0], : rel_grad.shape[1]]
    width, columns = grad.shape
    for a in range(0, width, 128):
        total = jnp.zeros((128, 128), f32)
        for b in range(0, columns, 128):
            tile = turned[b : b + 128, a : a + 128].astype(f32).T
            grad[a : a + 128, b : b + 128] = tile
            total = total + tile * w_qkv[a : a + 128, b : b + 128].astype(f32)
        sums = jnp.sum(total.T, axis=0, keepdims=True)
        gain_grad[:, a : a + 128] = sums / gain[:, a : a + 128]


def on_device(
    n_dp,
    n_ctx,
    n_exp,
    tokens,
    lengths,
    routes,
    buckets,
    cotangent,
    attn_gain,
    w_qkv,
    w_attn_out,
    rel_bias,
    ffn_gain,
    w_router,
    w_up,
    w_down,
):
    x = tokens[0]
    dy = cotangent[0]
    length = lengths[0]
    dp, ctx, exp = (lax.axis_index(name) for name in ("dp", "ctx", "exp"))
    rows, width = x.shape
    seq = buckets.shape[0]
    n_buckets, n_heads = rel_bias.shape
    head_dim = width // n_heads
    n_experts = w_router.shape[1]
    ff = w_up.shape[2]
    n_slot = n_ctx * n_exp
    n_groups = n_heads // n_exp
    n_x = n_ctx // 2
    cx, core = ctx // 2, ctx % 2
    small = n_x == 2 and n_dp == 2
    side = 512 if seq <= 2048 else 256
    n_tiles = seq // side
    slot_rows = n_experts * CAP

    def ring(v, shift):
        return lax.ppermute(v, "exp", [(i, (i + shift) % n_exp) for i in range(n_exp)])

    def swap(v):
        return lax.ppermute(v, "ctx", [(i, i ^ 1) for i in range(n_ctx)])

    def chips(v, a, b):
        perm = []
        for d in range(n_dp):
            for c in range(n_ctx):
                to = ((d + a) % n_dp) * n_ctx + ((c // 2 + b) % n_x) * 2 + c % 2
                perm.append((d * n_ctx + c, to))
        return lax.ppermute(v, ("dp", "ctx"), perm)

    first_pos = (ctx * n_exp + exp) * rows
    n_valid = jnp.clip(length - first_pos, 0, rows).astype(jnp.int32)
    valid_arg = n_valid.reshape(1)
    own_arg = jnp.stack([exp, core]).astype(jnp.int32)

    with jax.named_scope("gather_tokens"):
        if small:
            column = [(x, 0, 0)] + [(ring(x, k), 0, k) for k in range(1, n_exp)]
            pieces = column + [(chips(v, 0, 1), 1, k) for v, _, k in column]
            pieces = [(v, b, 0, k) for v, b, k in pieces]
            pieces = pieces + [(swap(v), b, 1, k) for v, b, _, k in pieces]
            blocks = [v for v, _, _, _ in pieces]
            starts = [
                ((((cx - b) % n_x) * 2 + (core ^ o)) * n_exp + (exp - k) % n_exp) * rows
                for _, b, o, k in pieces
            ]
        else:
            blocks = [lax.all_gather(x, ("ctx", "exp"), axis=0, tiled=True)]
            starts = [jnp.int32(0)]

    with jax.named_scope("routing"):
        pick, pay = call(
            functools.partial(route_kernel, n_experts),
            (sds((slot_rows, rows), bf16), sds((slot_rows, width + 128), bf16)),
            [smem(), vmem(), vmem(), vmem()],
            name="routing",
        )(valid_arg, routes[0], routes[0].T, dy)

        def to_experts(v):
            return lax.all_to_all(
                v.reshape(n_exp, CAP, v.shape[-1]), "exp", split_axis=0, concat_axis=0, tiled=True
            ).reshape(n_exp * CAP, v.shape[-1])

        pay_in = to_experts(pay)
        high = w_router.astype(bf16)
        rest = w_router - high.astype(f32)
        mid = rest.astype(bf16)
        low = (rest - mid.astype(f32)).astype(bf16)
        w3 = jnp.pad(
            jnp.concatenate([high, mid, low], axis=1), ((0, 0), (0, 128 - 3 * n_experts))
        )
        w3_t = w3.T

    with jax.named_scope("attention"):
        head = (ctx * n_exp + exp) % n_heads
        w_head = lax.dynamic_slice_in_dim(w_qkv, head * 3 * head_dim, 3 * head_dim, 1)
        w_head = jnp.pad(
            w_head.reshape(width, 3, head_dim), ((0, 0), (0, 0), (0, 128 - head_dim))
        ).reshape(width, 384)
        rel = lax.dynamic_slice_in_dim(rel_bias, head, 1, 1)[:, 0]
        where_arg = jnp.stack([length] + [s for s in starts]).astype(jnp.int32)
        bucket_row = buckets.reshape(1, seq)
        attn_outs = (
            sds((seq, width), bf16),
            sds((seq, 128), bf16),
            sds((seq, 128), bf16),
            sds((seq, 128), bf16),
            sds((head_dim, seq), bf16),
            sds((head_dim, seq), bf16),
            sds((n_slot, head_dim, 128), bf16),
            sds((1, seq), f32),
        )
        h1, qa, ka, va, qt, kt, out_t, lse = call(
            functools.partial(attn_kernel, len(blocks), n_buckets, head_dim),
            attn_outs,
            [smem(), smem()] + [vmem()] * (len(blocks) + 3),
            [
                pltpu.VMEM((head_dim, seq), bf16),
                pltpu.VMEM((1, seq + side), f32),
                pltpu.VMEM((n_tiles, side, side), f32),
            ],
            cost=(4 << 30, 8 << 20),
            name="attention",
        )(where_arg, rel, *blocks, attn_gain.reshape(1, width), w_head, bucket_row)
        slot_axes = ("ctx", "exp")
        attn_in = lax.all_to_all(out_t, slot_axes, split_axis=0, concat_axis=0, tiled=True)

    with jax.named_scope("middle"):
        gain2 = ffn_gain.reshape(1, width)
        middle, send = call(
            functools.partial(middle_kernel, n_heads),
            (sds((rows, width), f32), sds((slot_rows, width), bf16)),
            [smem()] + [vmem()] * 5,
            name="middle",
        )(valid_arg, attn_in, w_attn_out, x, gain2, pick)
        h2_in = to_experts(send)

    with jax.named_scope("experts"):
        block = 512
        row_spec = pl.BlockSpec((slot_rows, width), lambda i, *_: (0, 0))
        pay_spec = pl.BlockSpec((slot_rows, width + 128), lambda i, *_: (0, 0))
        w3_spec = pl.BlockSpec((width, 128), lambda i, *_: (0, 0))
        mix_rows, back_rows, router = pl.pallas_call(
            functools.partial(expert_kernel, n_experts),
            out_shape=(
                sds((slot_rows, width), bf16),
                sds((slot_rows, width), bf16),
                sds((8, width), f32),
            ),
            grid_spec=pltpu.PrefetchScalarGridSpec(
                num_scalar_prefetch=1,
                grid=(ff // block,),
                in_specs=[
                    row_spec,
                    pay_spec,
                    w3_spec,
                    pl.BlockSpec((128, width), lambda i, *_: (0, 0)),
                    pl.BlockSpec((width, block), lambda i, *_: (0, i)),
                    pl.BlockSpec((block, width), lambda i, *_: (i, 0)),
                ],
                out_specs=(row_spec, row_spec, pl.BlockSpec((8, width), lambda i, *_: (0, 0))),
                scratch_shapes=[
                    pltpu.VMEM((slot_rows, width), f32),
                    pltpu.VMEM((slot_rows, width), f32),
                    pltpu.VMEM((slot_rows, width), bf16),
                    pltpu.VMEM((slot_rows, 128), f32),
                ],
            ),
            compiler_params=params(),
            cost_estimate=pl.CostEstimate(
                flops=8 * slot_rows * width * ff, bytes_accessed=10 << 20, transcendentals=0
            ),
            name="experts",
        )(own_arg, h2_in, pay_in, w3, w3_t, w_up[0], w_down[0])
        back_in = to_experts(back_rows)
        mix_in = to_experts(mix_rows)

    with jax.named_scope("middle_back"):
        shares = n_dp * n_ctx
        red_rows = -(-(width + 16) // (16 * shares)) * 16 * shares
        dmid, grad_t, red = call(
            functools.partial(middle_back_kernel, n_heads),
            (
                sds((rows, width), f32),
                sds((n_slot, head_dim, rows), bf16),
                sds((red_rows, width), bf16),
            ),
            [smem()] + [vmem()] * 8,
            name="middle_back",
        )(valid_arg, back_in, pick, middle, dy, gain2, attn_in, w_attn_out, router)
        grad_in = lax.all_to_all(grad_t, slot_axes, split_axis=0, concat_axis=0, tiled=True)
        output = call(
            output_kernel,
            sds((rows, width), bf16),
            [smem()] + [vmem()] * 3,
            name="output",
        )(valid_arg, mix_in, pick, middle)

    with jax.named_scope("attention_back"):
        shifted = jnp.pad(bucket_row, ((0, 0), (side - 1, 1)), constant_values=-1)
        part = 3 * head_dim // n_ctx
        lanes = width // n_dp
        dqkv, weight_pay = call(
            functools.partial(attn_back_kernel, n_buckets, head_dim, n_dp),
            (sds((n_slot, 3 * head_dim, rows), bf16), sds((shares, part + 16, lanes), bf16)),
            [smem(), smem()] + [vmem()] * 11,
            [
                pltpu.VMEM((1, seq), f32),
                pltpu.VMEM((head_dim, seq), f32),
                pltpu.VMEM((head_dim, seq), f32),
                pltpu.VMEM((head_dim, seq), f32),
                pltpu.VMEM((3 * head_dim, seq), bf16),
                pltpu.VMEM((1, seq + side), f32),
                pltpu.VMEM((n_tiles, side, side), f32),
                pltpu.VMEM((n_tiles, side, side), f32),
                pltpu.VMEM((1, seq + side), f32),
            ],
            cost=(8 << 30, 8 << 20),
            name="attention_back",
        )(where_arg, rel, qa, ka, va, qt, kt, out_t, grad_in, lse, h1, bucket_row, shifted)
        all_chips = ("dp", "ctx")
        summed = lax.all_to_all(weight_pay, all_chips, split_axis=0, concat_axis=0, tiled=True)
        dqkv_in = lax.all_to_all(dqkv, slot_axes, split_axis=0, concat_axis=0, tiled=True)

    with jax.named_scope("token_grads"):
        grad_tokens = call(
            functools.partial(token_grad_kernel, n_heads),
            sds((rows, width), f32),
            [vmem()] * 5,
            name="token_grads",
        )(dqkv_in, w_qkv, x, attn_gain.reshape(1, width), dmid)

    with jax.named_scope("projection_grad"):
        by_ctx = summed.reshape(n_dp, n_ctx, part + 16, lanes)[:, :n_groups].astype(f32).sum(0)
        shard = jnp.concatenate(
            [
                by_ctx[:, :part].reshape(n_groups * part, lanes),
                by_ctx[:, part],
                jnp.zeros((16 - n_groups, lanes), f32),
            ]
        ).astype(bf16)[None]
        if small:
            near = [(shard, [(0, 0, 0)]), ]
            far = jnp.concatenate([ring(shard, k) for k in range(1, n_exp)])
            near.append((far, [(0, 0, k) for k in range(1, n_exp)]))
            spread = list(near)
            for a, b in ((0, 1), (1, 0), (1, 1)):
                spread += [(chips(v, a, b), [(a, b, k) for _, _, k in ids]) for v, ids in near]
            final, ids = [], []
            for v, keys in spread:
                final.append(v)
                ids += [(a, b, 0, k) for a, b, k in keys]
            for v, keys in spread:
                final.append(swap(v))
                ids += [(a, b, 1, k) for a, b, k in keys]
            at = []
            for a, b, o, k in ids:
                at += [(dp - a) % n_dp, ((cx - b) % n_x) * 2 + (core ^ o), (exp - k) % n_exp]
            at = jnp.stack(at).astype(jnp.int32)
            grad_qkv, grad_attn_gain, grad_rel = call(
                functools.partial(assemble_kernel, n_exp, part, n_groups, 3 * head_dim),
                (sds((width, 3 * width), f32), sds((1, width), f32), sds(rel_bias.shape, f32)),
                [smem()] + [vmem()] * (len(final) + 2),
                [pltpu.VMEM((3 * width, width), bf16), pltpu.VMEM((128, 128), f32)],
                name="assemble",
            )(at, *final, w_qkv, attn_gain.reshape(1, width))
            grad_attn_gain = grad_attn_gain[0]
        else:
            every = lax.all_gather(shard[0], ("dp", "ctx", "exp"), axis=0, tiled=False)
            every = every.reshape(n_dp, n_ctx, n_exp, n_groups * part + 16, lanes).astype(f32)
            main = every[:, :, :, : n_groups * part]
            main = main.reshape(n_dp, n_ctx, n_exp, n_groups, part, lanes)
            grad_qkv = main.transpose(0, 5, 3, 2, 1, 4).reshape(width, 3 * width)
            rel_rows = every[0, 0, :, n_groups * part : n_groups * (part + 1), :n_buckets]
            grad_rel = rel_rows.transpose(2, 1, 0).reshape(n_buckets, n_heads)
            grad_attn_gain = jnp.sum(grad_qkv * w_qkv.astype(f32), axis=1) / attn_gain

    with jax.named_scope("output_projection_grad"):
        reduced = lax.psum(red, ("dp", "ctx", "exp")).astype(f32)
        grad_attn_out = reduced[:width]
        grad_ffn_gain = reduced[width]
        grad_router = reduced[width + 8 : width + 8 + n_experts].T

    with jax.named_scope("expert_weight_grads"):
        if small:
            def all_rows(v):
                mine = [v, chips(v, 0, 1), chips(v, 1, 0), chips(v, 1, 1)]
                return mine + [swap(u) for u in mine]

            h_pieces, p_pieces = all_rows(h2_in), all_rows(pay_in)
            n_pieces = len(h_pieces)
            total_rows = n_pieces * slot_rows
            half = ff // 2
            steps = half // block
            any_spec = pl.BlockSpec(memory_space=pl.ANY)
            low_up = pl.BlockSpec((width, block), lambda i, s: (0, i))
            low_down = pl.BlockSpec((block, width), lambda i, s: (i, 0))
            at_up = pl.BlockSpec((width, block), lambda i, s: (0, s[0] * steps + i))
            at_down = pl.BlockSpec((block, width), lambda i, s: (s[0] * steps + i, 0))
            core_arg = jnp.stack([core, exp]).astype(jnp.int32)
            up_part, down_part, up_low, down_low = pl.pallas_call(
                functools.partial(weight_grad_kernel, n_experts, n_pieces),
                out_shape=(
                    sds((width, ff), f32),
                    sds((ff, width), f32),
                    sds((width, half), bf16),
                    sds((half, width), bf16),
                ),
                grid_spec=pltpu.PrefetchScalarGridSpec(
                    num_scalar_prefetch=1,
                    grid=(steps,),
                    in_specs=[any_spec] * (2 * n_pieces) + [w3_spec, at_up, at_down],
                    out_specs=(at_up, at_down, low_up, low_down),
                    scratch_shapes=[
                        pltpu.VMEM((total_rows, width), bf16),
                        pltpu.VMEM((total_rows, width + 128), bf16),
                        pltpu.VMEM((total_rows, width), bf16),
                        pltpu.VMEM((block, total_rows), bf16),
                        pltpu.VMEM((block, total_rows), bf16),
                        pltpu.SemaphoreType.DMA((2, n_pieces)),
                    ],
                ),
                compiler_params=params(),
                cost_estimate=pl.CostEstimate(
                    flops=8 * total_rows * width * half,
                    bytes_accessed=40 << 20,
                    transcendentals=0,
                ),
                name="weight_grads",
            )(core_arg, *h_pieces, *p_pieces, w3, w_up[0], w_down[0])
            up_got, down_got = swap(up_low), swap(down_low)
            other_up = pl.BlockSpec((width, block), lambda i, s: (0, (1 - s[0]) * steps + i))
            other_down = pl.BlockSpec((block, width), lambda i, s: ((1 - s[0]) * steps + i, 0))
            grad_up, grad_down = pl.pallas_call(
                fill_kernel,
                out_shape=(sds((width, ff), f32), sds((ff, width), f32)),
                grid_spec=pltpu.PrefetchScalarGridSpec(
                    num_scalar_prefetch=1,
                    grid=(steps,),
                    in_specs=[low_up, low_down, any_spec, any_spec],
                    out_specs=(other_up, other_down),
                ),
                input_output_aliases={3: 0, 4: 1},
                compiler_params=params(),
                name="fill",
            )(core_arg, up_got, down_got, up_part, down_part)
        else:
            own = own_lanes(exp, n_experts)
            gate, _ = gate_of(h2_in, pay_in, width, w3, own)
            dz = (gate * pay_in[:, :width].astype(f32)).astype(bf16)
            act, slope = gelu_parts(dot(h2_in, w_up[0], NN))
            dup = (dot(dz, w_down[0], NT) * slope).astype(bf16)
            grad_up = lax.psum(dot(h2_in, dup, TN).astype(bf16), all_chips).astype(f32)
            grad_down = lax.psum(dot(act.astype(bf16), dz, TN).astype(bf16), all_chips)
            grad_down = grad_down.astype(f32)

    return (
        output[None],
        grad_tokens[None],
        grad_attn_gain,
        grad_qkv,
        grad_attn_out,
        grad_rel,
        grad_ffn_gain,
        grad_router,
        grad_up[None],
        grad_down[None],
    )


def solution(mesh):
    sizes = dict(mesh.shape)
    by_token = P("dp", ("ctx", "exp"), None)
    by_expert = P("exp", None, None)
    return jax.shard_map(
        functools.partial(on_device, sizes["dp"], sizes["ctx"], sizes["exp"]),
        mesh=mesh,
        in_specs=(
            by_token,
            P("dp"),
            by_token,
            P(),
            by_token,
            P(),
            P(),
            P(),
            P(),
            P(),
            P(),
            by_expert,
            by_expert,
        ),
        out_specs=(
            by_token,
            by_token,
            P(),
            P(),
            P(),
            P(),
            P(),
            P(),
            by_expert,
            by_expert,
        ),
        check_vma=False,
    )
```

```python
import functools

import jax
import jax.numpy as jnp
from jax import lax
from jax.experimental import pallas as pl
from jax.experimental.pallas import tpu as pltpu
from jax.sharding import PartitionSpec as P

CAP = 80
EPS = 1e-06
NEG = -1e30
VMEM_LIMIT = 58 << 20
bf16 = jnp.bfloat16
f32 = jnp.float32
NN = ((1,), (0,))
NT = ((1,), (1,))
TN = ((0,), (0,))
GELU_C = 0.7978845608028654
GELU_A = 0.044715


def dot(left, right, dims):
    return lax.dot_general(left, right, (dims, ((), ())), preferred_element_type=f32)


def iota(shape, axis):
    return lax.broadcasted_iota(jnp.int32, shape, axis)


def norm_scale(values):
    return lax.rsqrt(jnp.mean(values * values, axis=-1, keepdims=True) + EPS)


def row_of(ref):
    return ref[...].reshape(1, ref.shape[0])


def norm_back(values, gain, grad):
    scale = norm_scale(values)
    xhat = values * scale
    gxhat = grad * gain
    grad_in = scale * (gxhat - xhat * jnp.mean(gxhat * xhat, axis=-1, keepdims=True))
    return grad_in, xhat


def gelu_parts(u):
    square = u * u
    t = jnp.tanh(u * (GELU_C + (GELU_C * GELU_A) * square))
    half = 0.5 * (1.0 + t)
    slope = half + (0.5 * u) * (1.0 - t * t) * (GELU_C + (3.0 * GELU_C * GELU_A) * square)
    return u * half, slope


def split2(values):
    high = values.astype(bf16)
    return high, (values - high.astype(f32)).astype(bf16)


def params(limit=VMEM_LIMIT):
    return pltpu.CompilerParams(vmem_limit_bytes=limit)


def vmem():
    return pl.BlockSpec(memory_space=pltpu.VMEM)


def smem():
    return pl.BlockSpec(memory_space=pltpu.SMEM)


def call(kernel, outs, ins, scratch=(), cost=None, name=None):
    flops, size = cost if cost else (1 << 20, 1 << 20)
    return pl.pallas_call(
        kernel,
        out_shape=outs,
        in_specs=ins,
        out_specs=jax.tree.map(lambda _: vmem(), outs),
        scratch_shapes=list(scratch),
        compiler_params=params(),
        cost_estimate=pl.CostEstimate(flops=flops, bytes_accessed=size, transcendentals=0),
        name=name,
    )


def sds(shape, dtype):
    return jax.ShapeDtypeStruct(shape, dtype)


def valid_rows(lengths, rows):
    index = lax.axis_index("ctx") * lax.axis_size("exp") + lax.axis_index("exp")
    return lengths[0] - index * rows


def route_kernel(n_experts, sc, routes_t, dy, router_t, pick, pay, w3, w3_t):
    rows = dy.shape[0]
    width = dy.shape[1]
    table = jnp.concatenate(
        [router_t[...], jnp.zeros((128 - n_experts, width), f32)], axis=0
    )
    high = table.astype(bf16).astype(f32)
    mid = (table - high).astype(bf16).astype(f32)
    low = table - high - mid
    table = high + pltpu.roll(mid, n_experts, 0) + pltpu.roll(low, 2 * n_experts, 0)
    w3_t[...] = table.astype(bf16)
    w3[...] = table.T.astype(bf16)
    first, second = routes_t[0:1, :], routes_t[1:2, :]
    eight = iota((8, rows), 0)
    named = jnp.where((first == eight) | (second == eight), 1.0, 0.0)
    upper = jnp.where(iota((rows, rows), 0) < iota((rows, rows), 1), 1.0, 0.0)
    rank = dot(named.astype(bf16), upper.astype(bf16), NN)
    slot = iota((CAP, rows), 0).astype(f32)
    for e in range(n_experts):
        hit = (named[e : e + 1] > 0.5) & (rank[e : e + 1] == slot)
        pick[e * CAP : (e + 1) * CAP, :] = jnp.where(hit, 1.0, 0.0).astype(bf16)
    all_pick = pick[...].astype(f32)
    valid = iota((1, rows), 1) < valid_rows(sc, rows)
    live = jnp.where(valid, all_pick, 0.0).astype(bf16)
    pay[:, :width] = dot(live, dy[...], NN).astype(bf16)
    line = iota((128, rows), 0)
    kind = jnp.where(line < 3 * n_experts, lax.rem(line, n_experts), -1)
    pair = jnp.where((first == kind) | (second == kind), 1.0, 0.0).astype(bf16)
    pay[:, width:] = dot(pick[...], pair, NT).astype(bf16)


def head_index(n_heads):
    index = lax.axis_index("ctx") * lax.axis_size("exp") + lax.axis_index("exp")
    return lax.rem(index, n_heads)


def bias_tiles(rel, buckets, brow, tiles):
    n_tiles, side, _ = tiles.shape
    n_heads, n_buckets = rel.shape
    head = head_index(n_heads)
    ids = buckets[...]
    row = jnp.zeros(ids.shape, f32)
    for b in range(n_buckets):
        row = jnp.where(ids == b, rel[head, b], row)
    brow[:, :side] = jnp.zeros((1, side), f32)
    brow[:, side:] = row
    for o in range(n_tiles):
        wide = jnp.broadcast_to(brow[:, o * side : (o + 2) * side], (side, 2 * side))
        tiles[o] = pltpu.roll(wide, 0, axis=1, stride=1, stride_axis=0)[:, side:]


def attn_kernel(shifts, head_dim, sc, rel, *refs):
    n_pieces = len(shifts)
    pieces = refs[:n_pieces]
    gain, w_qkv, buckets = refs[n_pieces : n_pieces + 3]
    h1, qa, ka, va, qt, kt, out_t, lse = refs[n_pieces + 3 : n_pieces + 11]
    vt, brow, tiles, window, weight, sem = refs[n_pieces + 11 :]
    head = head_index(rel.shape[0])
    pair_at = pl.multiple_of((head // 2) * 6 * head_dim, 128)
    fetch = pltpu.make_async_copy(w_qkv.at[:, pl.ds(pair_at, 6 * head_dim)], window, sem)
    fetch.start()
    bias_tiles(rel, buckets, brow, tiles)
    fetch.wait()
    odd = lax.rem(head, 2) == 1
    for i in range(3):
        even_part = window[:, i * head_dim : (i + 1) * head_dim]
        odd_part = window[:, (3 + i) * head_dim : (4 + i) * head_dim]
        part = jnp.where(odd, odd_part.astype(f32), even_part.astype(f32)).astype(bf16)
        pad = jnp.zeros((window.shape[0], 128 - head_dim), bf16)
        weight[:, i * 128 : (i + 1) * 128] = jnp.concatenate([part, pad], axis=1)
    n_exp = lax.axis_size("exp")
    n_x = lax.axis_size("ctx") // 2
    ctx, exp = lax.axis_index("ctx"), lax.axis_index("exp")

    def piece_start(b, o, k):
        if b < 0:
            return 0
        x_at = lax.rem(ctx // 2 + (n_x - b), n_x)
        core = lax.rem(lax.rem(ctx, 2) + o, 2)
        return ((x_at * 2 + core) * n_exp + lax.rem(exp + (n_exp - k), n_exp)) * 128

    n_tiles, side, _ = tiles.shape
    length = sc[0]
    lane = iota((128, 128), 1)

    def rows_in(x, start):
        x = x.astype(f32)
        h = (x * norm_scale(x) * row_of(gain)).astype(bf16)
        h1[pl.ds(start, 128), :] = h
        qkv = dot(h, weight[...], NN).astype(bf16).astype(f32)
        q, k, v = qkv[:, :128] * 0.125, qkv[:, 128:256], qkv[:, 256:]
        live = jnp.where(start + iota((128, 128), 0) < length, 0.0, NEG)
        qa[pl.ds(start, 128), :] = jnp.where(lane == head_dim, 1.0, q).astype(bf16)
        ka[pl.ds(start, 128), :] = jnp.where(lane == head_dim, live, k).astype(bf16)
        va[pl.ds(start, 128), :] = v.astype(bf16)
        qt[:, pl.ds(start, 128)] = q.T[:head_dim].astype(bf16)
        kt[:, pl.ds(start, 128)] = k.T[:head_dim].astype(bf16)
        vt[:, pl.ds(start, 128)] = v.T[:head_dim].astype(bf16)

    for i, piece in enumerate(pieces):
        if piece.shape[0] == 128:
            rows_in(piece[...], pl.multiple_of(piece_start(*shifts[i]), 128))
        else:

            def step(j, carry, piece=piece):
                start = pl.multiple_of(j * 128, 128)
                rows_in(piece[pl.ds(start, 128), :], start)
                return carry

            lax.fori_loop(0, piece.shape[0] // 128, step, 0)
    blocks = side // 128

    def one_query_tile(qi, carry):
        q_start = pl.multiple_of(qi * side, side)
        q = qa[pl.ds(q_start, side), :]

        def fold(k_start, offset, state, diagonal):
            top, total, acc = state
            scores = dot(ka[pl.ds(k_start, side), :], q, NT) + tiles[offset]
            if diagonal:
                scores = jnp.where(iota((side, side), 0) <= iota((side, side), 1), scores, NEG)
            new_top = jnp.maximum(top, jnp.max(scores, axis=0, keepdims=True))
            probs = jnp.exp(scores - new_top)
            scale = jnp.exp(top - new_top)
            total = total * scale + jnp.sum(probs, axis=0, keepdims=True)
            acc = acc * scale + dot(vt[:, pl.ds(k_start, side)], probs.astype(bf16), NN)
            return new_top, total, acc

        state = (
            jnp.full((1, side), NEG, f32),
            jnp.zeros((1, side), f32),
            jnp.zeros((head_dim, side), f32),
        )
        state = fold(q_start, 0, state, True)

        def earlier(kj, state):
            return fold(pl.multiple_of(kj * side, side), qi - kj, state, False)

        top, total, acc = lax.fori_loop(0, qi, earlier, state)
        result = (acc / total).astype(bf16)
        lse[:, pl.ds(q_start, side)] = top + jnp.log(total)
        for b in range(blocks):
            out_t[qi * blocks + b] = result[:, b * 128 : (b + 1) * 128]
        return carry

    lax.fori_loop(0, n_tiles, one_query_tile, 0)


def attn_back_kernel(head_dim, n_dp, rel, *refs):
    qa, ka, va, qt, kt, out_t, grad_t, lse, h1, buckets = refs[:10]
    pay, weight_pay = refs[10:12]
    dq, dk, dv, full, brow, tiles, sums, diag = refs[12:]
    n_tiles, side, _ = tiles.shape
    blocks = side // 128
    bias_tiles(rel, buckets, brow, tiles)
    sums[...] = jnp.zeros_like(sums)
    dk[...] = jnp.zeros_like(dk)
    dv[...] = jnp.zeros_like(dv)

    def one_query_tile(qi, carry):
        q_start = pl.multiple_of(qi * side, side)
        q = qa[pl.ds(q_start, side), :]
        q_t = qt[:, pl.ds(q_start, side)]
        g_t = jnp.concatenate([grad_t[qi * blocks + b] for b in range(blocks)], axis=1)
        o_t = jnp.concatenate([out_t[qi * blocks + b] for b in range(blocks)], axis=1)
        row_dots = jnp.sum(g_t.astype(f32) * o_t.astype(f32), axis=0, keepdims=True)
        norm = lse[:, pl.ds(q_start, side)]

        def fold(k_start, offset, acc, diagonal):
            where_k = pl.ds(k_start, side)
            scores = dot(ka[where_k, :], q, NT) + tiles[offset]
            probs = jnp.exp(scores - norm)
            if diagonal:
                probs = jnp.where(iota((side, side), 0) <= iota((side, side), 1), probs, 0.0)
            grad_prob = dot(va[where_k, :][:, :head_dim], g_t, NN)
            grad_score = probs * (grad_prob - row_dots)
            low = grad_score.astype(bf16)
            sums[offset] = sums[offset] + grad_score
            dv[:, where_k] = dv[:, where_k] + dot(g_t, probs.astype(bf16), NT)
            dk[:, where_k] = dk[:, where_k] + dot(q_t, low, NT)
            return acc + dot(kt[:, where_k], low, NN)

        acc = fold(q_start, 0, jnp.zeros((head_dim, side), f32), True)

        def earlier(kj, acc):
            return fold(pl.multiple_of(kj * side, side), qi - kj, acc, False)

        dq[:, pl.ds(q_start, side)] = lax.fori_loop(0, qi, earlier, acc)
        return carry

    lax.fori_loop(0, n_tiles, one_query_tile, 0)
    full[:head_dim, :] = (dq[...] * 0.125).astype(bf16)
    full[head_dim : 2 * head_dim, :] = dk[...].astype(bf16)
    full[2 * head_dim :, :] = dv[...].astype(bf16)
    for b in range(pay.shape[0]):
        pay[b] = full[:, b * 128 : (b + 1) * 128]
    flip = jnp.where(iota((side, side), 0) + iota((side, side), 1) == side - 1, 1.0, 0.0)
    flip = flip.astype(bf16)
    diag[...] = jnp.zeros_like(diag)
    for o in range(n_tiles):
        high, low = split2(sums[o])
        turned = dot(flip, high, NN) + dot(flip, low, NN)
        wide = jnp.concatenate([turned, jnp.zeros((side, side), f32)], axis=1)
        lined = pltpu.roll(wide, 0, axis=1, stride=1, stride_axis=0)
        where_d = slice(o * side, (o + 2) * side)
        diag[:, where_d] = diag[:, where_d] + jnp.sum(lined, axis=0, keepdims=True)
    ids = jnp.concatenate([buckets[...], jnp.full((1, side), -1, jnp.int32)], axis=1)
    ids = pltpu.roll(ids, side - 1, 1)
    hot = jnp.where(ids == iota((128, ids.shape[1]), 0), 1.0, 0.0).astype(bf16)
    high, low = split2(jnp.broadcast_to(diag[...], (8, diag.shape[1])))
    rel_grad = dot(high, hot, NT) + dot(low, hot, NT)
    grad_w = dot(full[...], h1[...], NN).astype(bf16)
    n_pay, pay_rows, lanes = weight_pay.shape
    n_ctx = n_pay // n_dp
    rows = grad_w.shape[0] // n_ctx
    rel_rows = jnp.concatenate([rel_grad, jnp.zeros((8, lanes - 128), f32)], axis=1)
    rel_rows = jnp.concatenate([rel_rows, jnp.zeros((8, lanes), f32)], axis=0).astype(bf16)
    for d in range(n_dp):
        for c in range(n_ctx):
            weight_pay[d * n_ctx + c, :rows, :] = grad_w[
                c * rows : (c + 1) * rows, d * lanes : (d + 1) * lanes
            ]
            weight_pay[d * n_ctx + c, rows:, :] = rel_rows


def middle_kernel(n_heads, sc, recv, w_out, x, gain, pick, middle, *send):
    rows, width = x.shape
    attn_t = jnp.concatenate([recv[h] for h in range(n_heads)], axis=0)
    branch = dot(attn_t, w_out[...], TN)
    valid = iota((rows, 1), 0) < valid_rows(sc, rows)
    mid = x[...].astype(f32) + jnp.where(valid, branch, 0.0)
    middle[...] = mid
    h2 = (mid * norm_scale(mid) * row_of(gain)).astype(bf16)
    for k, piece in enumerate(send):
        expert = lax.rem(lax.axis_index("exp") + k, len(send))
        chosen = pick[pl.ds(pl.multiple_of(expert * CAP, 16), CAP), :]
        piece[...] = dot(chosen, h2, NN).astype(bf16)


def gate_of(h2, pay, width, w3, own):
    logits = dot(h2, w3, NN)
    sel = 2.0 * own - pay[:, width:].astype(f32)
    diff = jnp.sum(logits * sel, axis=1, keepdims=True)
    return 1.0 / (1.0 + jnp.exp(-diff)), sel


def own_lanes(expert, n_experts):
    lane = iota((1, 128), 1)
    return jnp.where((lane < 3 * n_experts) & (lane % n_experts == expert), 1.0, 0.0)


def expert_kernel(n_experts, *refs):
    arrived = refs[:n_experts]
    pay, w3, w3_t, w_up, w_down = refs[n_experts : n_experts + 5]
    mix, back = refs[n_experts + 5 : 2 * n_experts + 5], refs[2 * n_experts + 5 : 3 * n_experts + 5]
    h2, router, z_acc, in_acc, dz, gates, rows_out = refs[3 * n_experts + 5 :]
    step = pl.program_id(0)
    width = h2.shape[1]
    expert = lax.axis_index("exp")
    own = own_lanes(expert, n_experts)

    @pl.when(step == 0)
    def _():
        for k in range(n_experts):
            source = lax.rem(expert + (n_experts - k), n_experts)
            h2[pl.ds(pl.multiple_of(source * CAP, 16), CAP), :] = arrived[k][...]
        gate, _ = gate_of(h2[...], pay, width, w3[...], own)
        gates[...] = jnp.broadcast_to(gate, gates.shape)
        dz[...] = (gate * pay[:, :width].astype(f32)).astype(bf16)
        z_acc[...] = jnp.zeros_like(z_acc)
        in_acc[...] = jnp.zeros_like(in_acc)

    up = dot(h2[...], w_up[...], NN)
    act, slope = gelu_parts(up)
    grad_hidden = dot(dz[...], w_down[...], NT)
    grad_up = (grad_hidden * slope).astype(bf16)
    z_acc[...] += dot(act.astype(bf16), w_down[...], NN)
    in_acc[...] += dot(grad_up, w_up[...], NT)

    @pl.when(step == pl.num_programs(0) - 1)
    def _():
        gate = gates[:, 0:1]
        sel = 2.0 * own - pay[:, width:].astype(f32)
        z = z_acc[...].astype(bf16).astype(f32)
        rows_out[...] = (gate * z).astype(bf16)
        for k in range(n_experts):
            source = lax.rem(expert + (n_experts - k), n_experts)
            mix[k][...] = rows_out[pl.ds(pl.multiple_of(source * CAP, 16), CAP), :]
        grad_gate = jnp.sum(pay[:, :width].astype(f32) * z, axis=1, keepdims=True)
        high, low = split2((gate * (1.0 - gate) * grad_gate) * sel)
        total = in_acc[...] + dot(high, w3_t[...], NN) + dot(low, w3_t[...], NN)
        rows_out[...] = total.astype(bf16)
        for k in range(n_experts):
            source = lax.rem(expert + (n_experts - k), n_experts)
            back[k][...] = rows_out[pl.ds(pl.multiple_of(source * CAP, 16), CAP), :]
        router[...] = (dot(high, h2[...], TN) + dot(low, h2[...], TN))[:8]


def collect(pieces, pick):
    n_experts = len(pieces)
    total = None
    for k, piece in enumerate(pieces):
        expert = lax.rem(lax.axis_index("exp") + k, n_experts)
        chosen = pick[pl.ds(pl.multiple_of(expert * CAP, 16), CAP), :]
        part = dot(chosen, piece[...], TN)
        total = part if total is None else total + part
    return total


def middle_back_kernel(n_heads, n_experts, sc, *refs):
    back = refs[:n_experts]
    pick, middle, dy, gain, recv, w_out, router, dmid, grad_t, red = refs[n_experts:]
    rows, width = middle.shape
    grad_h2 = collect(back, pick)
    grad_in, xhat = norm_back(middle[...], row_of(gain), grad_h2)
    grad_mid = dy[...].astype(f32) + grad_in
    dmid[...] = grad_mid
    valid = iota((rows, 1), 0) < valid_rows(sc, rows)
    branch = jnp.where(valid, grad_mid, 0.0).astype(bf16)
    attn_t = jnp.concatenate([recv[h] for h in range(n_heads)], axis=0)
    heads = dot(w_out[...], branch, NT).astype(bf16)
    head_dim = width // n_heads
    for h in range(n_heads):
        grad_t[h] = heads[h * head_dim : (h + 1) * head_dim]
    for h in range(n_heads, grad_t.shape[0]):
        grad_t[h] = jnp.zeros((head_dim, rows), bf16)
    red[:width, :] = dot(attn_t, branch, NN).astype(bf16)
    gains = jnp.sum(grad_h2 * xhat, axis=0, keepdims=True)
    small = jnp.concatenate([jnp.broadcast_to(gains, (8, width)), router[...]], axis=0)
    red[width : width + 16, :] = small.astype(bf16)
    rest = red.shape[0] - width - 16
    red[width + 16 :, :] = jnp.zeros((rest, width), bf16)


def output_kernel(n_experts, sc, *refs):
    mix = refs[:n_experts]
    pick, middle, out = refs[n_experts:]
    rows = middle.shape[0]
    valid = iota((rows, 1), 0) < valid_rows(sc, rows)
    total = collect(mix, pick)
    out[...] = (middle[...] + jnp.where(valid, total, 0.0)).astype(bf16)


def token_grad_kernel(n_heads, recv, w_qkv, x, gain, dmid, out):
    grad_t = jnp.concatenate([recv[h] for h in range(n_heads)], axis=0)
    grad_h1 = dot(w_qkv[...], grad_t, NN).T
    grad_in, _ = norm_back(x[...].astype(f32), row_of(gain), grad_h1)
    out[...] = dmid[...] + grad_in


def load_rows(h_pieces, where, pay_all, h2, pay, sem):
    rows = h_pieces[0].shape[0]
    copies = []
    for i, piece in enumerate(h_pieces):
        here = pl.ds(i * rows, rows)
        there = pl.ds(pl.multiple_of(where[i] * rows, 16), rows)
        copies.append(pltpu.make_async_copy(piece, h2.at[here, :], sem.at[0, i]))
        copies.append(pltpu.make_async_copy(pay_all.at[there, :], pay.at[here, :], sem.at[1, i]))
    return copies


def chip_index(a, b, o):
    n_dp = lax.axis_size("dp")
    n_x = lax.axis_size("ctx") // 2
    dp, ctx = lax.axis_index("dp"), lax.axis_index("ctx")
    core = lax.rem(lax.rem(ctx, 2) + o, 2)
    x_at = lax.rem(ctx // 2 + (n_x - b), n_x)
    return (lax.rem(dp + (n_dp - a), n_dp) * n_x + x_at) * 2 + core


def weight_grad_kernel(n_experts, keys, together, has_base, sc, *refs):
    n_pieces = len(keys)
    h_pieces = refs[:n_pieces]
    pay_all, w3, w_up, w_down = refs[n_pieces : n_pieces + 4]
    if has_base:
        up_base, down_base = refs[n_pieces + 4 : n_pieces + 6]
        up_out, down_out, low = refs[-9:-6]
    else:
        up_out, down_out = refs[-8:-6]
    h2, pay, dz, hid_t, dup_t, sem = refs[-6:]
    step = pl.program_id(0)
    rows = h_pieces[0].shape[0]
    width = h2.shape[1]
    block = w_down.shape[0]
    copies = load_rows(h_pieces, [chip_index(*key) for key in keys], pay_all, h2, pay, sem)

    @pl.when(step == 0)
    def _():
        for copy in copies:
            copy.start()

    up_t = w_up[...].T
    down = w_down[...]
    chunk = together * rows
    for i in range(n_pieces // together):
        here = slice(i * chunk, (i + 1) * chunk)

        @pl.when(step == 0)
        def _(i=i, here=here):
            for copy in copies[2 * together * i : 2 * together * (i + 1)]:
                copy.wait()
            own = own_lanes(lax.axis_index("exp"), n_experts)
            part = pay[here, :]
            gate, _ = gate_of(h2[here, :], part, width, w3[...], own)
            dz[here, :] = (gate * part[:, :width].astype(f32)).astype(bf16)

        act, slope = gelu_parts(dot(up_t, h2[here, :], NT))
        hid_t[:, here] = act.astype(bf16)
        dup_t[:, here] = (dot(down, dz[here, :], NT) * slope).astype(bf16)
    grad_down = dot(hid_t[...], dz[...], NN)
    grad_up = dot(dup_t[...], h2[...], NN)
    if has_base:
        grad_down = grad_down + down_base[...]
        grad_up = grad_up + up_base[...]
        low[:block, :] = grad_up.astype(bf16)
        low[block:, :] = grad_down.astype(bf16)
        up_out[...] = grad_up.T
        down_out[...] = grad_down
    else:
        up_out[...] = grad_up
        down_out[...] = grad_down


def fill_kernel(sc, low, *refs):
    up_out, down_out = refs[-2:]
    block = down_out.shape[0]
    up_out[...] = low[:block, :].astype(f32).T
    down_out[...] = low[block:, :].astype(f32)


def assemble_kernel(keys, rows, n_groups, head_cols, *refs):
    n_pieces = len(keys)
    pieces = refs[:n_pieces]
    w_qkv, gain, grad, gain_grad, rel_grad, turned, rel_t = refs[n_pieces:]
    lanes = pieces[0].shape[-1]
    n_dp, n_exp = lax.axis_size("dp"), lax.axis_size("exp")
    n_x = lax.axis_size("ctx") // 2
    dp, ctx, exp = (lax.axis_index(name) for name in ("dp", "ctx", "exp"))
    rel_t[...] = jnp.zeros_like(rel_t)
    for piece, ids in zip(pieces, keys):
        for i, (a, b, o, k) in enumerate(ids):
            d = lax.rem(dp + (n_dp - a), n_dp)
            c = lax.rem(ctx // 2 + (n_x - b), n_x) * 2 + lax.rem(lax.rem(ctx, 2) + o, 2)
            e = lax.rem(exp + (n_exp - k), n_exp)
            lane_at = pl.multiple_of(d * lanes, 128)
            for g in range(n_groups):
                head = g * n_exp + e
                row_at = pl.multiple_of(head * head_cols + c * rows, 16)
                turned[pl.ds(row_at, rows), pl.ds(lane_at, lanes)] = piece[
                    i, g * rows : (g + 1) * rows, :
                ]
                rel_t[pl.ds(head, 1), :] = piece[
                    i, n_groups * rows + g : n_groups * rows + g + 1, :128
                ].astype(f32)
    rel_grad[...] = rel_t[: rel_grad.shape[0], : rel_grad.shape[1]]
    width, columns = grad.shape
    for a in range(0, width, 128):
        total = jnp.zeros((128, 128), f32)
        for b in range(0, columns, 128):
            tile = turned[b : b + 128, a : a + 128].astype(f32).T
            grad[a : a + 128, b : b + 128] = tile
            total = total + tile * w_qkv[a : a + 128, b : b + 128].astype(f32)
        sums = jnp.sum(total.T, axis=0, keepdims=True)
        sums = sums / gain[a : a + 128].reshape(1, 128)
        gain_grad[a : a + 128] = sums.reshape(128)


def reduced_kernel(n_experts, red, attn_out, gain_grad, router_grad):
    width = attn_out.shape[0]
    attn_out[...] = red[:width, :].astype(f32)
    rows = red[width : width + 16, :].astype(f32)
    gain_grad[...] = rows[0:1].reshape(width)
    router_grad[...] = rows[8 : 8 + n_experts]


def after(value, *others):
    return lax.optimization_barrier((value, others))[0]


def on_device(
    n_dp,
    n_ctx,
    n_exp,
    tokens,
    lengths,
    routes,
    buckets,
    cotangent,
    attn_gain,
    w_qkv,
    w_attn_out,
    rel_bias,
    ffn_gain,
    w_router,
    w_up,
    w_down,
):
    x = tokens[0]
    dy = cotangent[0]
    rows, width = x.shape
    seq = buckets.shape[0]
    n_buckets, n_heads = rel_bias.shape
    head_dim = width // n_heads
    n_experts = w_router.shape[1]
    ff = w_up.shape[2]
    n_slot = n_ctx * n_exp
    n_groups = n_heads // n_exp
    n_x = n_ctx // 2
    small = n_x == 2 and n_dp == 2
    side = 512 if seq <= 2048 else 256
    n_tiles = seq // side
    slot_rows = n_experts * CAP
    slot_axes, all_chips = ("ctx", "exp"), ("dp", "ctx")

    def ring(v, shift):
        return lax.ppermute(v, "exp", [(i, (i + shift) % n_exp) for i in range(n_exp)])

    def swap(v):
        return lax.ppermute(v, "ctx", [(i, i ^ 1) for i in range(n_ctx)])

    def chips(v, a, b):
        perm = []
        for d in range(n_dp):
            for c in range(n_ctx):
                to = ((d + a) % n_dp) * n_ctx + ((c // 2 + b) % n_x) * 2 + c % 2
                perm.append((d * n_ctx + c, to))
        return lax.ppermute(v, all_chips, perm)

    def exchange(v, axes):
        return lax.all_to_all(v, axes, split_axis=0, concat_axis=0, tiled=True)

    def to_experts(v):
        return exchange(v.reshape(n_exp, CAP, v.shape[-1]), "exp").reshape(v.shape)

    def from_experts(parts):
        return [parts[0]] + [ring(parts[k], n_exp - k) for k in range(1, n_exp)]

    with jax.named_scope("gather_tokens"):
        if small:
            column = [(x, 0, k) if k == 0 else (ring(x, k), 0, k) for k in range(n_exp)]
            pieces = column + [(chips(v, 0, 1), 1, k) for v, _, k in column]
            pieces = [(v, b, 0, k) for v, b, k in pieces]
            pieces = pieces + [(swap(v), b, 1, k) for v, b, _, k in pieces]
            blocks = [v for v, _, _, _ in pieces]
            shifts = [ids for _, *ids in pieces]
        else:
            blocks = [lax.all_gather(x, slot_axes, axis=0, tiled=True)]
            shifts = [(-1, 0, 0)]

    with jax.named_scope("routing"):
        pick, pay, w3, w3_t = call(
            functools.partial(route_kernel, n_experts),
            (
                sds((slot_rows, rows), bf16),
                sds((slot_rows, width + 128), bf16),
                sds((width, 128), bf16),
                sds((128, width), bf16),
            ),
            [smem()] + [vmem()] * 3,
            name="routing",
        )(lengths, routes[0].T, dy, w_router.T)
        if small:
            pay = after(pay, column[-1][0])
        pay_in = to_experts(pay)

    with jax.named_scope("attention"):
        bucket_row = buckets.reshape(1, seq)
        blocks[-1] = after(blocks[-1], pay, bucket_row)
        attn_outs = (
            sds((seq, width), bf16),
            sds((seq, 128), bf16),
            sds((seq, 128), bf16),
            sds((seq, 128), bf16),
            sds((head_dim, seq), bf16),
            sds((head_dim, seq), bf16),
            sds((n_slot, head_dim, 128), bf16),
            sds((1, seq), f32),
        )
        any_spec = pl.BlockSpec(memory_space=pl.ANY)
        h1, qa, ka, va, qt, kt, out_t, lse = call(
            functools.partial(attn_kernel, shifts, head_dim),
            attn_outs,
            [smem(), smem()] + [vmem()] * (len(blocks) + 1) + [any_spec, vmem()],
            [
                pltpu.VMEM((head_dim, seq), bf16),
                pltpu.VMEM((1, seq + side), f32),
                pltpu.VMEM((n_tiles, side, side), f32),
                pltpu.VMEM((width, 6 * head_dim), bf16),
                pltpu.VMEM((width, 384), bf16),
                pltpu.SemaphoreType.DMA,
            ],
            cost=(4 << 30, 8 << 20),
            name="attention",
        )(lengths, rel_bias.T, *blocks, attn_gain, w_qkv, bucket_row)
        attn_in = exchange(after(out_t, pay_in), slot_axes)

    with jax.named_scope("middle"):
        piece_shape = sds((CAP, width), bf16)
        middle, *send = call(
            functools.partial(middle_kernel, n_heads),
            [sds((rows, width), f32)] + [piece_shape] * n_experts,
            [smem()] + [vmem()] * 5,
            name="middle",
        )(lengths, attn_in, w_attn_out, x, ffn_gain, pick)
        arrived = [send[0]] + [ring(send[k], k) for k in range(1, n_exp)]

    with jax.named_scope("experts"):
        block = 512
        row_spec = pl.BlockSpec((slot_rows, width), lambda i: (0, 0))
        piece_spec = pl.BlockSpec((CAP, width), lambda i: (0, 0))
        *parts, h2_in, router = pl.pallas_call(
            functools.partial(expert_kernel, n_experts),
            out_shape=[piece_shape] * (2 * n_experts)
            + [sds((slot_rows, width), bf16), sds((8, width), f32)],
            grid_spec=pltpu.PrefetchScalarGridSpec(
                num_scalar_prefetch=0,
                grid=(ff // block,),
                in_specs=[piece_spec] * n_experts
                + [
                    pl.BlockSpec((slot_rows, width + 128), lambda i: (0, 0)),
                    pl.BlockSpec((width, 128), lambda i: (0, 0)),
                    pl.BlockSpec((128, width), lambda i: (0, 0)),
                    pl.BlockSpec((width, block), lambda i: (0, i)),
                    pl.BlockSpec((block, width), lambda i: (i, 0)),
                ],
                out_specs=[piece_spec] * (2 * n_experts)
                + [row_spec, pl.BlockSpec((8, width), lambda i: (0, 0))],
                scratch_shapes=[
                    pltpu.VMEM((slot_rows, width), f32),
                    pltpu.VMEM((slot_rows, width), f32),
                    pltpu.VMEM((slot_rows, width), bf16),
                    pltpu.VMEM((slot_rows, 128), f32),
                    pltpu.VMEM((slot_rows, width), bf16),
                ],
            ),
            compiler_params=params(),
            cost_estimate=pl.CostEstimate(
                flops=8 * slot_rows * width * ff, bytes_accessed=10 << 20, transcendentals=0
            ),
            name="experts",
        )(*arrived, pay_in, w3, w3_t, w_up[0], w_down[0])
        mix_parts, back_parts = parts[:n_experts], parts[n_experts:]
        back_in = from_experts(back_parts)

    shares = n_dp * n_ctx
    with jax.named_scope("expert_weight_grads"):
        if small:
            half = ff // 2
            core_arg = (lax.axis_index("ctx") % 2).astype(jnp.int32).reshape(1)
            pay_all = lax.all_gather(pay_in, all_chips, axis=0, tiled=True)
            near = [h2_in, swap(h2_in)]
            far = [chips(h2_in, a, b) for a, b in ((0, 1), (1, 0), (1, 1))]

            def weight_part(pieces, keys, together, block, first, steps, base, before):
                up_spec = pl.BlockSpec(
                    (width, block), lambda i, s: (0, s[0] * (half // block) + first + i)
                )
                down_spec = pl.BlockSpec(
                    (block, width), lambda i, s: (s[0] * (half // block) + first + i, 0)
                )
                base_spec = pl.BlockSpec((block, width), lambda i, s: (first + i, 0))
                low_spec = pl.BlockSpec((2 * block, width), lambda i, s: (i, 0))
                if base:
                    shapes = [sds((width, ff), f32), sds((ff, width), f32)]
                    shapes.append(sds((2 * block * steps, width), bf16))
                    outs = [up_spec, down_spec, low_spec]
                else:
                    shapes = [sds((half, width), f32), sds((half, width), f32)]
                    outs = [base_spec, base_spec]
                count = len(pieces) * slot_rows
                n_in = len(pieces) + 5 + len(base)
                return pl.pallas_call(
                    functools.partial(weight_grad_kernel, n_experts, keys, together, bool(base)),
                    out_shape=shapes,
                    grid_spec=pltpu.PrefetchScalarGridSpec(
                        num_scalar_prefetch=1,
                        grid=(steps,),
                        in_specs=[any_spec] * (len(pieces) + 1)
                        + [pl.BlockSpec((width, 128), lambda i, s: (0, 0)), up_spec, down_spec]
                        + [base_spec] * len(base)
                        + [any_spec] * len(before),
                        out_specs=outs,
                        scratch_shapes=[
                            pltpu.VMEM((count, width), bf16),
                            pltpu.VMEM((count, width + 128), bf16),
                            pltpu.VMEM((count, width), bf16),
                            pltpu.VMEM((block, count), bf16),
                            pltpu.VMEM((block, count), bf16),
                            pltpu.SemaphoreType.DMA((2, len(pieces))),
                        ],
                    ),
                    input_output_aliases={n_in + i: i for i in range(len(before))},
                    compiler_params=params(),
                    cost_estimate=pl.CostEstimate(
                        flops=8 * count * width * block * steps,
                        bytes_accessed=16 << 20,
                        transcendentals=0,
                    ),
                    name="weight_grads",
                )(core_arg, *pieces, pay_all, w3, w_up[0], w_down[0], *base, *before)

            base = weight_part(near, [(0, 0, 0), (0, 0, 1)], 2, 512, 0, half // 512, (), ())
            back_in[0] = after(back_in[0], base)

    with jax.named_scope("middle_back"):
        red_rows = -(-(width + 16) // (16 * shares)) * 16 * shares
        dmid, grad_t, red = call(
            functools.partial(middle_back_kernel, n_heads, n_experts),
            (
                sds((rows, width), f32),
                sds((n_slot, head_dim, rows), bf16),
                sds((red_rows, width), bf16),
            ),
            [smem()] + [vmem()] * (7 + n_experts),
            name="middle_back",
        )(lengths, *back_in, pick, middle, dy, ffn_gain, attn_in, w_attn_out, router)
        grad_in = exchange(grad_t, slot_axes)

    if small:
        with jax.named_scope("expert_weight_grads"):
            part_block = 384
            part_steps = half // (2 * part_block)
            offsets = [(0, 1), (1, 0), (1, 1)]
            far = far + [swap(after(v, grad_t)) for v in far]
            far_keys = [(a, b, o) for o in (0, 1) for a, b in offsets]
            far = [after(far[0], grad_t)] + far[1:]
            up_1, down_1, low_1 = weight_part(
                far, far_keys, 2, part_block, 0, part_steps, base, ()
            )
            grad_in = after(grad_in, low_1)

    with jax.named_scope("attention_back"):
        part = 3 * head_dim // n_ctx
        lanes = width // n_dp
        dqkv, weight_pay = call(
            functools.partial(attn_back_kernel, head_dim, n_dp),
            (sds((n_slot, 3 * head_dim, rows), bf16), sds((shares, part + 16, lanes), bf16)),
            [smem()] + [vmem()] * 10,
            [
                pltpu.VMEM((head_dim, seq), f32),
                pltpu.VMEM((head_dim, seq), f32),
                pltpu.VMEM((head_dim, seq), f32),
                pltpu.VMEM((3 * head_dim, seq), bf16),
                pltpu.VMEM((1, seq + side), f32),
                pltpu.VMEM((n_tiles, side, side), f32),
                pltpu.VMEM((n_tiles, side, side), f32),
                pltpu.VMEM((1, seq + side), f32),
            ],
            cost=(8 << 30, 8 << 20),
            name="attention_back",
        )(rel_bias.T, qa, ka, va, qt, kt, out_t, grad_in, lse, h1, bucket_row)
        mix_in = from_experts([after(v, grad_in) for v in mix_parts])
        weight_pay = after(weight_pay, mix_in)
        summed = exchange(weight_pay, all_chips)

    if small:
        with jax.named_scope("expert_weight_grads"):
            far_2 = [after(far[0], weight_pay)] + far[1:]
            up_2, down_2, low_2 = weight_part(
                far_2, far_keys, 2, part_block, part_steps, part_steps, base, (up_1, down_1)
            )
            summed = after(summed, low_2)

    with jax.named_scope("projection_grad"):
        by_ctx = summed.reshape(n_dp, n_ctx, part + 16, lanes)[:, :n_groups].astype(f32).sum(0)
        shard = jnp.concatenate(
            [
                by_ctx[:, :part].reshape(n_groups * part, lanes),
                by_ctx[:, part],
                jnp.zeros((16 - n_groups, lanes), f32),
            ]
        ).astype(bf16)[None]
        if small:
            spread = [(shard, 0)] + [(ring(shard, k), k) for k in range(1, n_exp)]

    with jax.named_scope("token_grads"):
        dqkv_in = exchange(after(dqkv, shard), slot_axes)

    if small:
        with jax.named_scope("expert_weight_grads"):
            grads = (up_2, down_2)
            for first, low in ((0, swap(low_1)), (part_steps, swap(low_2))):

                def at(i, s, first=first):
                    return (1 - s[0]) * 2 * part_steps + first + i

                grads = pl.pallas_call(
                    fill_kernel,
                    out_shape=(sds((width, ff), f32), sds((ff, width), f32)),
                    grid_spec=pltpu.PrefetchScalarGridSpec(
                        num_scalar_prefetch=1,
                        grid=(part_steps,),
                        in_specs=[
                            pl.BlockSpec((2 * part_block, width), lambda i, s: (i, 0)),
                            any_spec,
                            any_spec,
                        ],
                        out_specs=(
                            pl.BlockSpec((width, part_block), lambda i, s, at=at: (0, at(i, s))),
                            pl.BlockSpec((part_block, width), lambda i, s, at=at: (at(i, s), 0)),
                        ),
                    ),
                    input_output_aliases={2: 0, 3: 1},
                    compiler_params=params(),
                    name="fill",
                )(core_arg, low, *grads)
            grad_up, grad_down = grads
    else:
        with jax.named_scope("expert_weight_grads"):
            own = own_lanes(lax.axis_index("exp"), n_experts)
            gate, _ = gate_of(h2_in, pay_in, width, w3, own)
            dz = (gate * pay_in[:, :width].astype(f32)).astype(bf16)
            act, slope = gelu_parts(dot(h2_in, w_up[0], NN))
            dup = (dot(dz, w_down[0], NT) * slope).astype(bf16)
            grad_up = lax.psum(dot(h2_in, dup, TN).astype(bf16), all_chips).astype(f32)
            grad_down = lax.psum(dot(act.astype(bf16), dz, TN).astype(bf16), all_chips)
            grad_down = grad_down.astype(f32)

    with jax.named_scope("output"):
        output = call(
            functools.partial(output_kernel, n_experts),
            sds((rows, width), bf16),
            [smem()] + [vmem()] * (2 + n_experts),
            name="output",
        )(lengths, *mix_in, pick, middle)

    with jax.named_scope("token_grads"):
        grad_tokens = call(
            functools.partial(token_grad_kernel, n_heads),
            sds((rows, width), f32),
            [vmem()] * 5,
            name="token_grads",
        )(dqkv_in, w_qkv, x, attn_gain, dmid)

    with jax.named_scope("projection_grad"):
        if small:
            near = [(shard, [0]), (jnp.concatenate([v for v, _ in spread[1:]]), [1, 2, 3])]
            wide = [(v, 0, 0, ks) for v, ks in near]
            for a, b in ((0, 1), (1, 0), (1, 1)):
                wide = wide + [(chips(v, a, b), a, b, ks) for v, ks in near]
            final = [v for v, _, _, _ in wide] + [swap(v) for v, _, _, _ in wide]
            keys = [[(a, b, o, k) for k in ks] for o in (0, 1) for _, a, b, ks in wide]
            grad_qkv, grad_attn_gain, grad_rel = call(
                functools.partial(assemble_kernel, keys, part, n_groups, 3 * head_dim),
                (sds((width, 3 * width), f32), sds((width,), f32), sds((n_heads, n_buckets), f32)),
                [vmem()] * (len(final) + 2),
                [pltpu.VMEM((3 * width, width), bf16), pltpu.VMEM((128, 128), f32)],
                name="assemble",
            )(*final, w_qkv, attn_gain)
            grad_rel = grad_rel.T
        else:
            every = lax.all_gather(shard[0], ("dp", "ctx", "exp"), axis=0, tiled=False)
            every = every.reshape(n_dp, n_ctx, n_exp, n_groups * part + 16, lanes).astype(f32)
            main = every[:, :, :, : n_groups * part]
            main = main.reshape(n_dp, n_ctx, n_exp, n_groups, part, lanes)
            grad_qkv = main.transpose(0, 5, 3, 2, 1, 4).reshape(width, 3 * width)
            rel_rows = every[0, 0, :, n_groups * part : n_groups * (part + 1), :n_buckets]
            grad_rel = rel_rows.transpose(2, 1, 0).reshape(n_buckets, n_heads)
            grad_attn_gain = jnp.sum(grad_qkv * w_qkv.astype(f32), axis=1) / attn_gain

    with jax.named_scope("output_projection_grad"):
        if small:
            share = lax.psum_scatter(red, all_chips, scatter_dimension=0, tiled=True)
            others = [ring(share, k).astype(f32) for k in range(1, n_exp)]
            share = (share.astype(f32) + others[0] + others[1] + others[2]).astype(bf16)
            reduced = lax.all_gather(share, all_chips, axis=0, tiled=True)
        else:
            reduced = lax.psum(red, ("dp", "ctx", "exp"))
        grad_attn_out, grad_ffn_gain, grad_router = call(
            functools.partial(reduced_kernel, n_experts),
            (sds((width, width), f32), sds((width,), f32), sds((n_experts, width), f32)),
            [vmem()],
            name="reduced",
        )(reduced)
        grad_router = grad_router.T

    return (
        output[None],
        grad_tokens[None],
        grad_attn_gain,
        grad_qkv,
        grad_attn_out,
        grad_rel,
        grad_ffn_gain,
        grad_router,
        grad_up[None],
        grad_down[None],
    )


def solution(mesh):
    sizes = dict(mesh.shape)
    by_token = P("dp", ("ctx", "exp"), None)
    by_expert = P("exp", None, None)
    return jax.shard_map(
        functools.partial(on_device, sizes["dp"], sizes["ctx"], sizes["exp"]),
        mesh=mesh,
        in_specs=(
            by_token,
            P("dp"),
            by_token,
            P(),
            by_token,
            P(),
            P(),
            P(),
            P(),
            P(),
            P(),
            by_expert,
            by_expert,
        ),
        out_specs=(
            by_token,
            by_token,
            P(),
            P(),
            P(),
            P(),
            P(),
            P(),
            by_expert,
            by_expert,
        ),
        check_vma=False,
    )
```

```python
import functools

import jax
import jax.numpy as jnp
from jax import lax
from jax.experimental import pallas as pl
from jax.experimental.pallas import tpu as pltpu
from jax.sharding import PartitionSpec as P

CAP = 80
EPS = 1e-06
NEG = -1e30
VMEM_LIMIT = 58 << 20
bf16 = jnp.bfloat16
f32 = jnp.float32
NN = ((1,), (0,))
NT = ((1,), (1,))
TN = ((0,), (0,))
GELU_C = 0.7978845608028654
GELU_A = 0.044715


def dot(left, right, dims):
    return lax.dot_general(left, right, (dims, ((), ())), preferred_element_type=f32)


def iota(shape, axis):
    return lax.broadcasted_iota(jnp.int32, shape, axis)


def norm_scale(values):
    return lax.rsqrt(jnp.mean(values * values, axis=-1, keepdims=True) + EPS)


def row_of(ref):
    return ref[...].reshape(1, ref.shape[0])


def norm_back(values, gain, grad):
    scale = norm_scale(values)
    xhat = values * scale
    gxhat = grad * gain
    grad_in = scale * (gxhat - xhat * jnp.mean(gxhat * xhat, axis=-1, keepdims=True))
    return grad_in, xhat


def gelu_parts(u):
    square = u * u
    t = jnp.tanh(u * (GELU_C + (GELU_C * GELU_A) * square))
    half = 0.5 * (1.0 + t)
    slope = half + (0.5 * u) * (1.0 - t * t) * (GELU_C + (3.0 * GELU_C * GELU_A) * square)
    return u * half, slope


def split2(values):
    high = values.astype(bf16)
    return high, (values - high.astype(f32)).astype(bf16)


def params(limit=VMEM_LIMIT):
    return pltpu.CompilerParams(vmem_limit_bytes=limit)


def vmem():
    return pl.BlockSpec(memory_space=pltpu.VMEM)


def smem():
    return pl.BlockSpec(memory_space=pltpu.SMEM)


def cost_of(micros):
    return pl.CostEstimate(
        flops=int(micros * 1e9), bytes_accessed=int(micros * 1e5), transcendentals=0
    )


def call(kernel, outs, ins, scratch=(), micros=3, name=None):
    return pl.pallas_call(
        kernel,
        out_shape=outs,
        in_specs=ins,
        out_specs=jax.tree.map(lambda o: smem() if o.dtype == jnp.int32 else vmem(), outs),
        scratch_shapes=list(scratch),
        compiler_params=params(),
        cost_estimate=cost_of(micros),
        name=name,
    )


def sds(shape, dtype):
    return jax.ShapeDtypeStruct(shape, dtype)


def valid_rows(lengths, rows):
    index = lax.axis_index("ctx") * lax.axis_size("exp") + lax.axis_index("exp")
    return lengths[0] - index * rows


def route_kernel(n_experts, sc, routes_t, dy, router_t, places, pick, w3, w3_t, full, *pay):
    places[0] = lax.rem(lax.axis_index("ctx"), 2)
    rows = dy.shape[0]
    width = dy.shape[1]
    table = jnp.concatenate(
        [router_t[...], jnp.zeros((128 - n_experts, width), f32)], axis=0
    )
    high = table.astype(bf16).astype(f32)
    mid = (table - high).astype(bf16).astype(f32)
    low = table - high - mid
    table = high + pltpu.roll(mid, n_experts, 0) + pltpu.roll(low, 2 * n_experts, 0)
    w3_t[...] = table.astype(bf16)
    w3[...] = table.T.astype(bf16)
    first, second = routes_t[0:1, :], routes_t[1:2, :]
    eight = iota((8, rows), 0)
    named = jnp.where((first == eight) | (second == eight), 1.0, 0.0)
    upper = jnp.where(iota((rows, rows), 0) < iota((rows, rows), 1), 1.0, 0.0)
    rank = dot(named.astype(bf16), upper.astype(bf16), NN)
    slot = iota((CAP, rows), 0).astype(f32)
    for e in range(n_experts):
        hit = (named[e : e + 1] > 0.5) & (rank[e : e + 1] == slot)
        pick[e * CAP : (e + 1) * CAP, :] = jnp.where(hit, 1.0, 0.0).astype(bf16)
    all_pick = pick[...].astype(f32)
    valid = iota((1, rows), 1) < valid_rows(sc, rows)
    live = jnp.where(valid, all_pick, 0.0).astype(bf16)
    full[:, :width] = dot(live, dy[...], NN).astype(bf16)
    line = iota((128, rows), 0)
    kind = jnp.where(line < 3 * n_experts, lax.rem(line, n_experts), -1)
    pair = jnp.where((first == kind) | (second == kind), 1.0, 0.0).astype(bf16)
    full[:, width:] = dot(pick[...], pair, NT).astype(bf16)
    for k, piece in enumerate(pay):
        expert = lax.rem(lax.axis_index("exp") + k, n_experts)
        piece[...] = full[pl.ds(pl.multiple_of(expert * CAP, 16), CAP), :]


def head_index(n_heads):
    index = lax.axis_index("ctx") * lax.axis_size("exp") + lax.axis_index("exp")
    return lax.rem(index, n_heads)


def bias_tiles(rel, buckets, brow, tiles):
    n_tiles, side, _ = tiles.shape
    n_heads, n_buckets = rel.shape
    head = head_index(n_heads)
    ids = buckets[...]
    row = jnp.zeros(ids.shape, f32)
    for b in range(n_buckets):
        row = jnp.where(ids == b, rel[head, b], row)
    brow[:, :side] = jnp.zeros((1, side), f32)
    brow[:, side:] = row
    for o in range(n_tiles):
        wide = jnp.broadcast_to(brow[:, o * side : (o + 2) * side], (side, 2 * side))
        tiles[o] = pltpu.roll(wide, 0, axis=1, stride=1, stride_axis=0)[:, side:]


def attn_kernel(shifts, head_dim, sc, rel, *refs):
    n_pieces = len(shifts)
    pieces = refs[:n_pieces]
    gain, w_qkv, buckets = refs[n_pieces : n_pieces + 3]
    h1, qa, ka, va, qt, kt, out_t, lse = refs[n_pieces + 3 : n_pieces + 11]
    vt, brow, tiles, window, weight, sem = refs[n_pieces + 11 :]
    head = head_index(rel.shape[0])
    pair_at = pl.multiple_of((head // 2) * 6 * head_dim, 128)
    fetch = pltpu.make_async_copy(w_qkv.at[:, pl.ds(pair_at, 6 * head_dim)], window, sem)
    fetch.start()
    bias_tiles(rel, buckets, brow, tiles)
    fetch.wait()
    odd = lax.rem(head, 2) == 1
    for i in range(3):
        even_part = window[:, i * head_dim : (i + 1) * head_dim]
        odd_part = window[:, (3 + i) * head_dim : (4 + i) * head_dim]
        part = jnp.where(odd, odd_part.astype(f32), even_part.astype(f32)).astype(bf16)
        pad = jnp.zeros((window.shape[0], 128 - head_dim), bf16)
        weight[:, i * 128 : (i + 1) * 128] = jnp.concatenate([part, pad], axis=1)
    n_exp = lax.axis_size("exp")
    n_x = lax.axis_size("ctx") // 2
    ctx, exp = lax.axis_index("ctx"), lax.axis_index("exp")

    def piece_start(b, o, k):
        if b < 0:
            return 0
        x_at = lax.rem(ctx // 2 + (n_x - b), n_x)
        core = lax.rem(lax.rem(ctx, 2) + o, 2)
        return ((x_at * 2 + core) * n_exp + lax.rem(exp + (n_exp - k), n_exp)) * 128

    n_tiles, side, _ = tiles.shape
    length = sc[0]
    lane = iota((128, 128), 1)

    def rows_in(x, start):
        x = x.astype(f32)
        h = (x * norm_scale(x) * row_of(gain)).astype(bf16)
        h1[pl.ds(start, 128), :] = h
        qkv = dot(h, weight[...], NN).astype(bf16).astype(f32)
        q, k, v = qkv[:, :128] * 0.125, qkv[:, 128:256], qkv[:, 256:]
        live = jnp.where(start + iota((128, 128), 0) < length, 0.0, NEG)
        qa[pl.ds(start, 128), :] = jnp.where(lane == head_dim, 1.0, q).astype(bf16)
        ka[pl.ds(start, 128), :] = jnp.where(lane == head_dim, live, k).astype(bf16)
        va[pl.ds(start, 128), :] = v.astype(bf16)
        qt[:, pl.ds(start, 128)] = q.T[:head_dim].astype(bf16)
        kt[:, pl.ds(start, 128)] = k.T[:head_dim].astype(bf16)
        vt[:, pl.ds(start, 128)] = v.T[:head_dim].astype(bf16)

    for i, piece in enumerate(pieces):
        if piece.shape[0] == 128:
            rows_in(piece[...], pl.multiple_of(piece_start(*shifts[i]), 128))
        else:

            def step(j, carry, piece=piece):
                start = pl.multiple_of(j * 128, 128)
                rows_in(piece[pl.ds(start, 128), :], start)
                return carry

            lax.fori_loop(0, piece.shape[0] // 128, step, 0)
    blocks = side // 128

    def one_query_tile(qi, carry):
        q_start = pl.multiple_of(qi * side, side)
        q = qa[pl.ds(q_start, side), :]

        def fold(k_start, offset, state, diagonal):
            top, total, acc = state
            scores = dot(ka[pl.ds(k_start, side), :], q, NT) + tiles[offset]
            if diagonal:
                scores = jnp.where(iota((side, side), 0) <= iota((side, side), 1), scores, NEG)
            new_top = jnp.maximum(top, jnp.max(scores, axis=0, keepdims=True))
            probs = jnp.exp(scores - new_top)
            scale = jnp.exp(top - new_top)
            total = total * scale + jnp.sum(probs, axis=0, keepdims=True)
            acc = acc * scale + dot(vt[:, pl.ds(k_start, side)], probs.astype(bf16), NN)
            return new_top, total, acc

        state = (
            jnp.full((1, side), NEG, f32),
            jnp.zeros((1, side), f32),
            jnp.zeros((head_dim, side), f32),
        )
        state = fold(q_start, 0, state, True)

        def earlier(kj, state):
            return fold(pl.multiple_of(kj * side, side), qi - kj, state, False)

        top, total, acc = lax.fori_loop(0, qi, earlier, state)
        result = (acc / total).astype(bf16)
        lse[:, pl.ds(q_start, side)] = top + jnp.log(total)
        for b in range(blocks):
            out_t[qi * blocks + b] = result[:, b * 128 : (b + 1) * 128]
        return carry

    lax.fori_loop(0, n_tiles, one_query_tile, 0)


def attn_back_kernel(head_dim, n_dp, rel, *refs):
    qa, ka, va, qt, kt, out_t, grad_t, lse, h1, buckets = refs[:10]
    pay, weight_pay = refs[10:12]
    dq, dk, dv, full, brow, tiles, sums, diag = refs[12:]
    n_tiles, side, _ = tiles.shape
    blocks = side // 128
    bias_tiles(rel, buckets, brow, tiles)
    sums[...] = jnp.zeros_like(sums)
    dk[...] = jnp.zeros_like(dk)
    dv[...] = jnp.zeros_like(dv)

    def one_query_tile(qi, carry):
        q_start = pl.multiple_of(qi * side, side)
        q = qa[pl.ds(q_start, side), :]
        q_t = qt[:, pl.ds(q_start, side)]
        g_t = jnp.concatenate([grad_t[qi * blocks + b] for b in range(blocks)], axis=1)
        o_t = jnp.concatenate([out_t[qi * blocks + b] for b in range(blocks)], axis=1)
        row_dots = jnp.sum(g_t.astype(f32) * o_t.astype(f32), axis=0, keepdims=True)
        norm = lse[:, pl.ds(q_start, side)]

        def fold(k_start, offset, acc, diagonal):
            where_k = pl.ds(k_start, side)
            scores = dot(ka[where_k, :], q, NT) + tiles[offset]
            probs = jnp.exp(scores - norm)
            if diagonal:
                probs = jnp.where(iota((side, side), 0) <= iota((side, side), 1), probs, 0.0)
            grad_prob = dot(va[where_k, :][:, :head_dim], g_t, NN)
            grad_score = probs * (grad_prob - row_dots)
            low = grad_score.astype(bf16)
            sums[offset] = sums[offset] + grad_score
            dv[:, where_k] = dv[:, where_k] + dot(g_t, probs.astype(bf16), NT)
            dk[:, where_k] = dk[:, where_k] + dot(q_t, low, NT)
            return acc + dot(kt[:, where_k], low, NN)

        acc = fold(q_start, 0, jnp.zeros((head_dim, side), f32), True)

        def earlier(kj, acc):
            return fold(pl.multiple_of(kj * side, side), qi - kj, acc, False)

        dq[:, pl.ds(q_start, side)] = lax.fori_loop(0, qi, earlier, acc)
        return carry

    lax.fori_loop(0, n_tiles, one_query_tile, 0)
    full[:head_dim, :] = (dq[...] * 0.125).astype(bf16)
    full[head_dim : 2 * head_dim, :] = dk[...].astype(bf16)
    full[2 * head_dim :, :] = dv[...].astype(bf16)
    for b in range(pay.shape[0]):
        pay[b] = full[:, b * 128 : (b + 1) * 128]
    flip = jnp.where(iota((side, side), 0) + iota((side, side), 1) == side - 1, 1.0, 0.0)
    flip = flip.astype(bf16)
    diag[...] = jnp.zeros_like(diag)
    for o in range(n_tiles):
        high, low = split2(sums[o])
        turned = dot(flip, high, NN) + dot(flip, low, NN)
        wide = jnp.concatenate([turned, jnp.zeros((side, side), f32)], axis=1)
        lined = pltpu.roll(wide, 0, axis=1, stride=1, stride_axis=0)
        where_d = slice(o * side, (o + 2) * side)
        diag[:, where_d] = diag[:, where_d] + jnp.sum(lined, axis=0, keepdims=True)
    ids = jnp.concatenate([buckets[...], jnp.full((1, side), -1, jnp.int32)], axis=1)
    ids = pltpu.roll(ids, side - 1, 1)
    hot = jnp.where(ids == iota((128, ids.shape[1]), 0), 1.0, 0.0).astype(bf16)
    high, low = split2(jnp.broadcast_to(diag[...], (8, diag.shape[1])))
    rel_grad = dot(high, hot, NT) + dot(low, hot, NT)
    grad_w = dot(full[...], h1[...], NN).astype(bf16)
    n_pay, pay_rows, lanes = weight_pay.shape
    n_ctx = n_pay // n_dp
    rows = grad_w.shape[0] // n_ctx
    rel_rows = jnp.concatenate([rel_grad, jnp.zeros((8, lanes - 128), f32)], axis=1)
    rel_rows = jnp.concatenate([rel_rows, jnp.zeros((8, lanes), f32)], axis=0).astype(bf16)
    for d in range(n_dp):
        for c in range(n_ctx):
            weight_pay[d * n_ctx + c, :rows, :] = grad_w[
                c * rows : (c + 1) * rows, d * lanes : (d + 1) * lanes
            ]
            weight_pay[d * n_ctx + c, rows:, :] = rel_rows


def middle_kernel(n_heads, sc, recv, w_out, x, gain, pick, middle, *send):
    rows, width = x.shape
    attn_t = jnp.concatenate([recv[h] for h in range(n_heads)], axis=0)
    branch = dot(attn_t, w_out[...], TN)
    valid = iota((rows, 1), 0) < valid_rows(sc, rows)
    mid = x[...].astype(f32) + jnp.where(valid, branch, 0.0)
    middle[...] = mid
    h2 = (mid * norm_scale(mid) * row_of(gain)).astype(bf16)
    for k, piece in enumerate(send):
        expert = lax.rem(lax.axis_index("exp") + k, len(send))
        chosen = pick[pl.ds(pl.multiple_of(expert * CAP, 16), CAP), :]
        piece[...] = dot(chosen, h2, NN).astype(bf16)


def gate_of(h2, pay, width, w3, own):
    logits = dot(h2, w3, NN)
    sel = 2.0 * own - pay[:, width:].astype(f32)
    diff = jnp.sum(logits * sel, axis=1, keepdims=True)
    return 1.0 / (1.0 + jnp.exp(-diff)), sel


def own_lanes(expert, n_experts):
    lane = iota((1, 128), 1)
    return jnp.where((lane < 3 * n_experts) & (lane % n_experts == expert), 1.0, 0.0)


def expert_kernel(n_experts, h2, pay, w3, w3_t, w_up, w_down, *refs):
    mix, back = refs[:n_experts], refs[n_experts : 2 * n_experts]
    router, z_acc, in_acc, dz, gates, rows_out = refs[2 * n_experts :]
    step = pl.program_id(0)
    width = h2.shape[1]
    expert = lax.axis_index("exp")
    own = own_lanes(expert, n_experts)

    @pl.when(step == 0)
    def _():
        gate, _ = gate_of(h2[...], pay, width, w3[...], own)
        gates[...] = jnp.broadcast_to(gate, gates.shape)
        dz[...] = (gate * pay[:, :width].astype(f32)).astype(bf16)
        z_acc[...] = jnp.zeros_like(z_acc)
        in_acc[...] = jnp.zeros_like(in_acc)

    up = dot(h2[...], w_up[...], NN)
    act, slope = gelu_parts(up)
    grad_hidden = dot(dz[...], w_down[...], NT)
    grad_up = (grad_hidden * slope).astype(bf16)
    z_acc[...] += dot(act.astype(bf16), w_down[...], NN)
    in_acc[...] += dot(grad_up, w_up[...], NT)

    @pl.when(step == pl.num_programs(0) - 1)
    def _():
        gate = gates[:, 0:1]
        sel = 2.0 * own - pay[:, width:].astype(f32)
        z = z_acc[...].astype(bf16).astype(f32)
        rows_out[...] = (gate * z).astype(bf16)
        for k in range(n_experts):
            mix[k][...] = rows_out[k * CAP : (k + 1) * CAP, :]
        grad_gate = jnp.sum(pay[:, :width].astype(f32) * z, axis=1, keepdims=True)
        high, low = split2((gate * (1.0 - gate) * grad_gate) * sel)
        total = in_acc[...] + dot(high, w3_t[...], NN) + dot(low, w3_t[...], NN)
        rows_out[...] = total.astype(bf16)
        for k in range(n_experts):
            back[k][...] = rows_out[k * CAP : (k + 1) * CAP, :]
        router[...] = (dot(high, h2[...], TN) + dot(low, h2[...], TN))[:8]


def collect(pieces, pick):
    n_experts = len(pieces)
    total = None
    for k, piece in enumerate(pieces):
        expert = lax.rem(lax.axis_index("exp") + k, n_experts)
        chosen = pick[pl.ds(pl.multiple_of(expert * CAP, 16), CAP), :]
        part = dot(chosen, piece[...], TN)
        total = part if total is None else total + part
    return total


def middle_back_kernel(n_heads, n_experts, sc, *refs):
    back = refs[:n_experts]
    pick, middle, dy, gain, recv, w_out, router, dmid, grad_t, red = refs[n_experts:]
    rows, width = middle.shape
    grad_h2 = collect(back, pick)
    grad_in, xhat = norm_back(middle[...], row_of(gain), grad_h2)
    grad_mid = dy[...].astype(f32) + grad_in
    dmid[...] = grad_mid
    valid = iota((rows, 1), 0) < valid_rows(sc, rows)
    branch = jnp.where(valid, grad_mid, 0.0).astype(bf16)
    attn_t = jnp.concatenate([recv[h] for h in range(n_heads)], axis=0)
    heads = dot(w_out[...], branch, NT).astype(bf16)
    head_dim = width // n_heads
    for h in range(n_heads):
        grad_t[h] = heads[h * head_dim : (h + 1) * head_dim]
    for h in range(n_heads, grad_t.shape[0]):
        grad_t[h] = jnp.zeros((head_dim, rows), bf16)
    red[:width, :] = dot(attn_t, branch, NN).astype(bf16)
    gains = jnp.sum(grad_h2 * xhat, axis=0, keepdims=True)
    small = jnp.concatenate([jnp.broadcast_to(gains, (8, width)), router[...]], axis=0)
    red[width : width + 16, :] = small.astype(bf16)
    rest = red.shape[0] - width - 16
    red[width + 16 :, :] = jnp.zeros((rest, width), bf16)


def output_kernel(n_experts, sc, *refs):
    mix = refs[:n_experts]
    pick, middle, out = refs[n_experts:]
    rows = middle.shape[0]
    valid = iota((rows, 1), 0) < valid_rows(sc, rows)
    total = collect(mix, pick)
    out[...] = (middle[...] + jnp.where(valid, total, 0.0)).astype(bf16)


def token_grad_kernel(n_heads, recv, w_qkv, x, gain, dmid, out):
    grad_t = jnp.concatenate([recv[h] for h in range(n_heads)], axis=0)
    grad_h1 = dot(w_qkv[...], grad_t, NN).T
    grad_in, _ = norm_back(x[...].astype(f32), row_of(gain), grad_h1)
    out[...] = dmid[...] + grad_in


def load_rows(h_pieces, where, pay_all, h2, pay, sem):
    rows = h_pieces[0].shape[0]
    copies = []
    for i, piece in enumerate(h_pieces):
        here = pl.ds(i * rows, rows)
        there = pl.ds(pl.multiple_of(where[i] * rows, 16), rows)
        copies.append(pltpu.make_async_copy(piece, h2.at[here, :], sem.at[0, i]))
        copies.append(pltpu.make_async_copy(pay_all.at[there, :], pay.at[here, :], sem.at[1, i]))
    return copies


def chip_index(a, b, o):
    n_dp = lax.axis_size("dp")
    n_x = lax.axis_size("ctx") // 2
    dp, ctx = lax.axis_index("dp"), lax.axis_index("ctx")
    core = lax.rem(lax.rem(ctx, 2) + o, 2)
    x_at = lax.rem(ctx // 2 + (n_x - b), n_x)
    return (lax.rem(dp + (n_dp - a), n_dp) * n_x + x_at) * 2 + core


def weight_grad_kernel(n_experts, keys, together, sc, *refs):
    n_pieces = len(keys)
    h_pieces = refs[:n_pieces]
    pay_all, w3, w_up, w_down = refs[n_pieces : n_pieces + 4]
    up_out, down_out, low, h2, pay, dz, hid_t, dup_t, sem = refs[-9:]
    step = pl.program_id(0)
    rows = h_pieces[0].shape[0]
    width = h2.shape[1]
    block = w_down.shape[0]
    copies = load_rows(h_pieces, [chip_index(*key) for key in keys], pay_all, h2, pay, sem)

    @pl.when(step == 0)
    def _():
        for copy in copies:
            copy.start()

    own = own_lanes(lax.axis_index("exp"), n_experts)
    up_t = w_up[...].T
    down = w_down[...]
    chunk = together * rows
    for i in range(n_pieces // together):
        here = slice(i * chunk, (i + 1) * chunk)

        @pl.when(step == 0)
        def _(i=i, here=here):
            for copy in copies[2 * together * i : 2 * together * (i + 1)]:
                copy.wait()
            part = pay[here, :]
            gate, _ = gate_of(h2[here, :], part, width, w3[...], own)
            dz[here, :] = (gate * part[:, :width].astype(f32)).astype(bf16)

        act, slope = gelu_parts(dot(up_t, h2[here, :], NT))
        hid_t[:, here] = act.astype(bf16)
        dup_t[:, here] = (dot(down, dz[here, :], NT) * slope).astype(bf16)
    grad_up = dot(dup_t[...], h2[...], NN)
    low[:block, :] = grad_up.astype(bf16)
    up_out[...] = grad_up.T
    grad_down = dot(hid_t[...], dz[...], NN)
    low[block:, :] = grad_down.astype(bf16)
    down_out[...] = grad_down


def fill_kernel(sc, low, *refs):
    up_out, down_out = refs[-2:]
    block = down_out.shape[0]
    up_out[...] = low[:block, :].astype(f32).T
    down_out[...] = low[block:, :].astype(f32)


def assemble_kernel(keys, rows, n_groups, head_cols, *refs):
    n_pieces = len(keys)
    pieces = refs[:n_pieces]
    w_qkv, gain, grad, gain_grad, rel_grad, turned, rel_t = refs[n_pieces:]
    lanes = pieces[0].shape[-1]
    n_dp, n_exp = lax.axis_size("dp"), lax.axis_size("exp")
    n_x = lax.axis_size("ctx") // 2
    dp, ctx, exp = (lax.axis_index(name) for name in ("dp", "ctx", "exp"))
    rel_t[...] = jnp.zeros_like(rel_t)
    for piece, ids in zip(pieces, keys):
        for i, (a, b, o, k) in enumerate(ids):
            d = lax.rem(dp + (n_dp - a), n_dp)
            c = lax.rem(ctx // 2 + (n_x - b), n_x) * 2 + lax.rem(lax.rem(ctx, 2) + o, 2)
            e = lax.rem(exp + (n_exp - k), n_exp)
            lane_at = pl.multiple_of(d * lanes, 128)
            for g in range(n_groups):
                head = g * n_exp + e
                row_at = pl.multiple_of(head * head_cols + c * rows, 16)
                turned[pl.ds(row_at, rows), pl.ds(lane_at, lanes)] = piece[
                    i, g * rows : (g + 1) * rows, :
                ]
                rel_t[pl.ds(head, 1), :] = piece[
                    i, n_groups * rows + g : n_groups * rows + g + 1, :128
                ].astype(f32)
    rel_grad[...] = rel_t[: rel_grad.shape[0], : rel_grad.shape[1]]
    width, columns = grad.shape
    for a in range(0, width, 128):
        total = jnp.zeros((128, 128), f32)
        for b in range(0, columns, 128):
            tile = turned[b : b + 128, a : a + 128].astype(f32).T
            grad[a : a + 128, b : b + 128] = tile
            total = total + tile * w_qkv[a : a + 128, b : b + 128].astype(f32)
        sums = jnp.sum(total.T, axis=0, keepdims=True)
        sums = sums / gain[a : a + 128].reshape(1, 128)
        gain_grad[a : a + 128] = sums.reshape(128)


def shard_kernel(n_dp, n_groups, summed, shard):
    n_ctx = summed.shape[0] // n_dp
    part = summed.shape[1] - 16
    extra = iota((16, summed.shape[2]), 0)
    tail = jnp.zeros(extra.shape, f32)
    for g in range(n_groups):
        total = summed[g].astype(f32)
        for d in range(1, n_dp):
            total = total + summed[d * n_ctx + g].astype(f32)
        shard[0, g * part : (g + 1) * part, :] = total[:part].astype(bf16)
        tail = jnp.where(extra == g, total[part:], tail)
    shard[0, n_groups * part :, :] = tail.astype(bf16)


def reduced_kernel(n_experts, red, attn_out, gain_grad, router_grad):
    width = attn_out.shape[0]
    attn_out[...] = red[:width, :].astype(f32)
    rows = red[width : width + 16, :].astype(f32)
    gain_grad[...] = rows[0:1].reshape(width)
    router_grad[...] = rows[8 : 8 + n_experts]


def after(value, *others):
    return lax.optimization_barrier((value, others))[0]


def on_device(
    n_dp,
    n_ctx,
    n_exp,
    tokens,
    lengths,
    routes,
    buckets,
    cotangent,
    attn_gain,
    w_qkv,
    w_attn_out,
    rel_bias,
    ffn_gain,
    w_router,
    w_up,
    w_down,
):
    x = tokens[0]
    dy = cotangent[0]
    rows, width = x.shape
    seq = buckets.shape[0]
    n_buckets, n_heads = rel_bias.shape
    head_dim = width // n_heads
    n_experts = w_router.shape[1]
    ff = w_up.shape[2]
    n_slot = n_ctx * n_exp
    n_groups = n_heads // n_exp
    n_x = n_ctx // 2
    small = n_x == 2 and n_dp == 2
    side = 512 if seq <= 2048 else 256
    n_tiles = seq // side
    slot_rows = n_experts * CAP
    slot_axes, all_chips = ("ctx", "exp"), ("dp", "ctx")

    def ring(v, shift):
        return lax.ppermute(v, "exp", [(i, (i + shift) % n_exp) for i in range(n_exp)])

    def swap(v):
        return lax.ppermute(v, "ctx", [(i, i ^ 1) for i in range(n_ctx)])

    def chips(v, a, b):
        perm = []
        for d in range(n_dp):
            for c in range(n_ctx):
                to = ((d + a) % n_dp) * n_ctx + ((c // 2 + b) % n_x) * 2 + c % 2
                perm.append((d * n_ctx + c, to))
        return lax.ppermute(v, all_chips, perm)

    def exchange(v, axes):
        return lax.all_to_all(v, axes, split_axis=0, concat_axis=0, tiled=True)

    def to_experts(parts):
        return [parts[0]] + [ring(parts[k], k) for k in range(1, n_exp)]

    def from_experts(parts):
        return [parts[0]] + [ring(parts[k], n_exp - k) for k in range(1, n_exp)]

    keys = [(a, b, o) for o in (0, 1) for a, b in ((0, 0), (0, 1), (1, 0), (1, 1))]

    with jax.named_scope("routing"):
        places, pick, w3, w3_t, _, *pay = call(
            functools.partial(route_kernel, n_experts),
            [
                sds((1,), jnp.int32),
                sds((slot_rows, rows), bf16),
                sds((width, 128), bf16),
                sds((128, width), bf16),
                sds((slot_rows, width + 128), bf16),
            ]
            + [sds((CAP, width + 128), bf16)] * n_experts,
            [smem()] + [vmem()] * 3,
            name="routing",
        )(lengths, routes[0].T, dy, w_router.T)

    with jax.named_scope("gather_tokens"):
        if small:
            column = [(x, 0, k) if k == 0 else (ring(x, k), 0, k) for k in range(n_exp)]
            onward = [v for v, _, _ in column]
            onward[-1] = after(onward[-1], pay)
            pieces = column + [(chips(v, 0, 1), 1, k) for k, v in enumerate(onward)]
            pieces = [(v, b, 0, k) for v, b, k in pieces]
            arrived = to_experts(after(pay, pieces[-1][0]))
            pieces = pieces + [(swap(v), b, 1, k) for v, b, _, k in pieces]
            blocks = [v for v, _, _, _ in pieces]
            shifts = [ids for _, *ids in pieces]
        else:
            blocks = [lax.all_gather(x, slot_axes, axis=0, tiled=True)]
            shifts = [(-1, 0, 0)]
            arrived = to_experts(pay)

    with jax.named_scope("attention"):
        bucket_row = buckets.reshape(1, seq)
        blocks[-1] = after(blocks[-1], bucket_row)
        attn_outs = (
            sds((seq, width), bf16),
            sds((seq, 128), bf16),
            sds((seq, 128), bf16),
            sds((seq, 128), bf16),
            sds((head_dim, seq), bf16),
            sds((head_dim, seq), bf16),
            sds((n_slot, head_dim, 128), bf16),
            sds((1, seq), f32),
        )
        any_spec = pl.BlockSpec(memory_space=pl.ANY)
        h1, qa, ka, va, qt, kt, out_t, lse = call(
            functools.partial(attn_kernel, shifts, head_dim),
            attn_outs,
            [smem(), smem()] + [vmem()] * (len(blocks) + 1) + [any_spec, vmem()],
            [
                pltpu.VMEM((head_dim, seq), bf16),
                pltpu.VMEM((1, seq + side), f32),
                pltpu.VMEM((n_tiles, side, side), f32),
                pltpu.VMEM((width, 6 * head_dim), bf16),
                pltpu.VMEM((width, 384), bf16),
                pltpu.SemaphoreType.DMA,
            ],
            micros=15,
            name="attention",
        )(lengths, rel_bias.T, *blocks, attn_gain, w_qkv, bucket_row)
        attn_in = exchange(out_t, slot_axes)
        pay_in = jnp.concatenate([arrived[0]] + [after(v, out_t) for v in arrived[1:]])

    with jax.named_scope("middle"):
        piece_shape = sds((CAP, width), bf16)
        middle, *send = call(
            functools.partial(middle_kernel, n_heads),
            [sds((rows, width), f32)] + [piece_shape] * n_experts,
            [smem()] + [vmem()] * 5,
            name="middle",
        )(lengths, attn_in, w_attn_out, x, ffn_gain, pick)
        h2_in = jnp.concatenate(to_experts(send))

    with jax.named_scope("experts"):
        block = 512
        row_spec = pl.BlockSpec((slot_rows, width), lambda i: (0, 0))
        piece_spec = pl.BlockSpec((CAP, width), lambda i: (0, 0))
        *parts, router = pl.pallas_call(
            functools.partial(expert_kernel, n_experts),
            out_shape=[piece_shape] * (2 * n_experts)
            + [sds((8, width), f32)],
            grid_spec=pltpu.PrefetchScalarGridSpec(
                num_scalar_prefetch=0,
                grid=(ff // block,),
                in_specs=[
                    row_spec,
                    pl.BlockSpec((slot_rows, width + 128), lambda i: (0, 0)),
                    pl.BlockSpec((width, 128), lambda i: (0, 0)),
                    pl.BlockSpec((128, width), lambda i: (0, 0)),
                    pl.BlockSpec((width, block), lambda i: (0, i)),
                    pl.BlockSpec((block, width), lambda i: (i, 0)),
                ],
                out_specs=[piece_spec] * (2 * n_experts)
                + [pl.BlockSpec((8, width), lambda i: (0, 0))],
                scratch_shapes=[
                    pltpu.VMEM((slot_rows, width), f32),
                    pltpu.VMEM((slot_rows, width), f32),
                    pltpu.VMEM((slot_rows, width), bf16),
                    pltpu.VMEM((slot_rows, 128), f32),
                    pltpu.VMEM((slot_rows, width), bf16),
                ],
            ),
            compiler_params=params(),
            cost_estimate=cost_of(12),
            name="experts",
        )(h2_in, pay_in, w3, w3_t, w_up[0], w_down[0])
        mix_parts, back_parts = parts[:n_experts], parts[n_experts:]
        back_in = from_experts(back_parts)

    shares = n_dp * n_ctx
    with jax.named_scope("expert_weight_grads"):
        if small:
            pay_all = lax.all_gather(pay_in, all_chips, axis=0, tiled=True)
            beside = [chips(h2_in, a, b) for a, b in ((0, 1), (1, 0), (1, 1))]
            block = 512
            n_parts = ff // (2 * block)
            full_shapes = [sds((width, ff), f32), sds((ff, width), f32)]

            back_in[0] = after(back_in[0], beside, pay_all)

            def half_specs(other):
                def at(i, s):
                    return (1 - s[0] if other else s[0]) * n_parts + i

                return (
                    pl.BlockSpec((width, block), lambda i, s: (0, at(i, s))),
                    pl.BlockSpec((block, width), lambda i, s: (at(i, s), 0)),
                )

            low_spec = pl.BlockSpec((2 * block, width), lambda i, s: (i, 0))

            def weight_half(pieces):
                specs = half_specs(False)
                count = len(pieces) * slot_rows
                return pl.pallas_call(
                    functools.partial(weight_grad_kernel, n_experts, keys, 2),
                    out_shape=full_shapes + [sds((ff, width), bf16)],
                    grid_spec=pltpu.PrefetchScalarGridSpec(
                        num_scalar_prefetch=1,
                        grid=(n_parts,),
                        in_specs=[any_spec] * (len(pieces) + 1)
                        + [pl.BlockSpec((width, 128), lambda i, s: (0, 0)), *specs],
                        out_specs=[*specs, low_spec],
                        scratch_shapes=[
                            pltpu.VMEM((count, width), bf16),
                            pltpu.VMEM((count, width + 128), bf16),
                            pltpu.VMEM((count, width), bf16),
                            pltpu.VMEM((block, count), bf16),
                            pltpu.VMEM((block, count), bf16),
                            pltpu.SemaphoreType.DMA((2, len(pieces))),
                        ],
                    ),
                    compiler_params=params(),
                    cost_estimate=cost_of(36),
                    name="weight_grads",
                )(places, *pieces, pay_all, w3, w_up[0], w_down[0])

            def weight_fill(low, grads):
                return pl.pallas_call(
                    fill_kernel,
                    out_shape=full_shapes,
                    grid_spec=pltpu.PrefetchScalarGridSpec(
                        num_scalar_prefetch=1,
                        grid=(n_parts,),
                        in_specs=[low_spec, any_spec, any_spec],
                        out_specs=half_specs(True),
                    ),
                    input_output_aliases={2: 0, 3: 1},
                    compiler_params=params(),
                    cost_estimate=cost_of(8),
                    name="fill",
                )(places, low, *grads)


    with jax.named_scope("middle_back"):
        red_rows = -(-(width + 16) // (16 * shares)) * 16 * shares
        dmid, grad_t, red = call(
            functools.partial(middle_back_kernel, n_heads, n_experts),
            (
                sds((rows, width), f32),
                sds((n_slot, head_dim, rows), bf16),
                sds((red_rows, width), bf16),
            ),
            [smem()] + [vmem()] * (7 + n_experts),
            name="middle_back",
        )(lengths, *back_in, pick, middle, dy, ffn_gain, attn_in, w_attn_out, router)
        grad_in = exchange(grad_t, slot_axes)

    if small:
        with jax.named_scope("expert_weight_grads"):
            own_side = [h2_in] + beside
            own_side = [after(v, grad_t) for v in own_side]
            pieces = own_side + [swap(v) for v in own_side]
            *grads, low = weight_half(pieces)
            share = lax.psum_scatter(red, all_chips, scatter_dimension=0, tiled=True)
            mix_in = from_experts([after(v, grad_t) for v in mix_parts])
            grad_in = after(grad_in, low, share, mix_in)
            others = [ring(share, k).astype(f32) for k in range(1, n_exp)]

    with jax.named_scope("attention_back"):
        part = 3 * head_dim // n_ctx
        lanes = width // n_dp
        dqkv, weight_pay = call(
            functools.partial(attn_back_kernel, head_dim, n_dp),
            (sds((n_slot, 3 * head_dim, rows), bf16), sds((shares, part + 16, lanes), bf16)),
            [smem()] + [vmem()] * 10,
            [
                pltpu.VMEM((head_dim, seq), f32),
                pltpu.VMEM((head_dim, seq), f32),
                pltpu.VMEM((head_dim, seq), f32),
                pltpu.VMEM((3 * head_dim, seq), bf16),
                pltpu.VMEM((1, seq + side), f32),
                pltpu.VMEM((n_tiles, side, side), f32),
                pltpu.VMEM((n_tiles, side, side), f32),
                pltpu.VMEM((1, seq + side), f32),
            ],
            micros=17,
            name="attention_back",
        )(rel_bias.T, qa, ka, va, qt, kt, out_t, grad_in, lse, h1, bucket_row)
        if small:
            share = share.astype(f32) + others[0] + others[1] + others[2]
            share = after(share, weight_pay).astype(bf16)
        else:
            mix_in = from_experts(mix_parts)
        summed = exchange(weight_pay, all_chips)
        if small:
            summed = after(summed, share)

    with jax.named_scope("projection_grad"):
        shard = call(
            functools.partial(shard_kernel, n_dp, n_groups),
            sds((1, n_groups * part + 16, lanes), bf16),
            [vmem()],
            name="shard",
        )(summed)
        if small:
            column = [shard] + [ring(shard, k) for k in range(1, n_exp)]
            column = jnp.concatenate(column)

    with jax.named_scope("token_grads"):
        if small:
            dqkv = after(dqkv, column)
        dqkv_in = exchange(dqkv, slot_axes)

    if small:
        with jax.named_scope("expert_weight_grads"):
            grad_up, grad_down = weight_fill(swap(after(low, shard)), grads)
    else:
        with jax.named_scope("expert_weight_grads"):
            own = own_lanes(lax.axis_index("exp"), n_experts)
            gate, _ = gate_of(h2_in, pay_in, width, w3, own)
            dz = (gate * pay_in[:, :width].astype(f32)).astype(bf16)
            act, slope = gelu_parts(dot(h2_in, w_up[0], NN))
            dup = (dot(dz, w_down[0], NT) * slope).astype(bf16)
            grad_up = lax.psum(dot(h2_in, dup, TN).astype(bf16), all_chips).astype(f32)
            grad_down = lax.psum(dot(act.astype(bf16), dz, TN).astype(bf16), all_chips)
            grad_down = grad_down.astype(f32)

    with jax.named_scope("output"):
        output = call(
            functools.partial(output_kernel, n_experts),
            sds((rows, width), bf16),
            [smem()] + [vmem()] * (2 + n_experts),
            name="output",
        )(lengths, *mix_in, pick, middle)

    with jax.named_scope("token_grads"):
        grad_tokens = call(
            functools.partial(token_grad_kernel, n_heads),
            sds((rows, width), f32),
            [vmem()] * 5,
            name="token_grads",
        )(dqkv_in, w_qkv, x, attn_gain, dmid)

    with jax.named_scope("projection_grad"):
        if small:
            wide = [(column, 0, 0, range(n_exp))]
            for a, b in ((0, 1), (1, 0), (1, 1)):
                wide.append((chips(column, a, b), a, b, range(n_exp)))
            wide = [(after(v, dqkv_in), a, b, ks) for v, a, b, ks in wide]
            final = [v for v, _, _, _ in wide] + [swap(v) for v, _, _, _ in wide]
            final[-1] = after(final[-1], grad_tokens, output, grad_up, grad_down)
            keys = [[(a, b, o, k) for k in ks] for o in (0, 1) for _, a, b, ks in wide]
            grad_qkv, grad_attn_gain, grad_rel = call(
                functools.partial(assemble_kernel, keys, part, n_groups, 3 * head_dim),
                (sds((width, 3 * width), f32), sds((width,), f32), sds((n_heads, n_buckets), f32)),
                [vmem()] * (len(final) + 2),
                [pltpu.VMEM((3 * width, width), bf16), pltpu.VMEM((128, 128), f32)],
                micros=8,
                name="assemble",
            )(*final, w_qkv, attn_gain)
            grad_rel = grad_rel.T
        else:
            every = lax.all_gather(shard[0], ("dp", "ctx", "exp"), axis=0, tiled=False)
            every = every.reshape(n_dp, n_ctx, n_exp, n_groups * part + 16, lanes).astype(f32)
            main = every[:, :, :, : n_groups * part]
            main = main.reshape(n_dp, n_ctx, n_exp, n_groups, part, lanes)
            grad_qkv = main.transpose(0, 5, 3, 2, 1, 4).reshape(width, 3 * width)
            rel_rows = every[0, 0, :, n_groups * part : n_groups * (part + 1), :n_buckets]
            grad_rel = rel_rows.transpose(2, 1, 0).reshape(n_buckets, n_heads)
            grad_attn_gain = jnp.sum(grad_qkv * w_qkv.astype(f32), axis=1) / attn_gain

    with jax.named_scope("output_projection_grad"):
        if small:
            reduced = lax.all_gather(share, all_chips, axis=0, tiled=True)
        else:
            reduced = lax.psum(red, ("dp", "ctx", "exp"))
        grad_attn_out, grad_ffn_gain, grad_router = call(
            functools.partial(reduced_kernel, n_experts),
            (sds((width, width), f32), sds((width,), f32), sds((n_experts, width), f32)),
            [vmem()],
            name="reduced",
        )(reduced)
        grad_router = grad_router.T

    return (
        output[None],
        grad_tokens[None],
        grad_attn_gain,
        grad_qkv,
        grad_attn_out,
        grad_rel,
        grad_ffn_gain,
        grad_router,
        grad_up[None],
        grad_down[None],
    )


def solution(mesh):
    sizes = dict(mesh.shape)
    by_token = P("dp", ("ctx", "exp"), None)
    by_expert = P("exp", None, None)
    return jax.shard_map(
        functools.partial(on_device, sizes["dp"], sizes["ctx"], sizes["exp"]),
        mesh=mesh,
        in_specs=(
            by_token,
            P("dp"),
            by_token,
            P(),
            by_token,
            P(),
            P(),
            P(),
            P(),
            P(),
            P(),
            by_expert,
            by_expert,
        ),
        out_specs=(
            by_token,
            by_token,
            P(),
            P(),
            P(),
            P(),
            P(),
            P(),
            by_expert,
            by_expert,
        ),
        check_vma=False,
    )
```

```python
import functools

import jax
import jax.numpy as jnp
from jax import lax
from jax.experimental import pallas as pl
from jax.experimental.pallas import tpu as pltpu
from jax.sharding import PartitionSpec as P

CAP = 80
EPS = 1e-06
NEG = -1e30
VMEM_LIMIT = 58 << 20
bf16 = jnp.bfloat16
f32 = jnp.float32
NN = ((1,), (0,))
NT = ((1,), (1,))
TN = ((0,), (0,))
GELU_C = 0.7978845608028654
GELU_A = 0.044715


def dot(left, right, dims):
    return lax.dot_general(left, right, (dims, ((), ())), preferred_element_type=f32)


def iota(shape, axis):
    return lax.broadcasted_iota(jnp.int32, shape, axis)


def norm_scale(values):
    return lax.rsqrt(jnp.mean(values * values, axis=-1, keepdims=True) + EPS)


def row_of(ref):
    return ref[...].reshape(1, ref.shape[0])


def norm_back(values, gain, grad):
    scale = norm_scale(values)
    xhat = values * scale
    gxhat = grad * gain
    grad_in = scale * (gxhat - xhat * jnp.mean(gxhat * xhat, axis=-1, keepdims=True))
    return grad_in, xhat


def gelu_parts(u):
    square = u * u
    t = jnp.tanh(u * (GELU_C + (GELU_C * GELU_A) * square))
    half = 0.5 * (1.0 + t)
    slope = half + (0.5 * u) * (1.0 - t * t) * (GELU_C + (3.0 * GELU_C * GELU_A) * square)
    return u * half, slope


def split2(values):
    high = values.astype(bf16)
    return high, (values - high.astype(f32)).astype(bf16)


def params(limit=VMEM_LIMIT):
    return pltpu.CompilerParams(vmem_limit_bytes=limit)


def vmem():
    return pl.BlockSpec(memory_space=pltpu.VMEM)


def smem():
    return pl.BlockSpec(memory_space=pltpu.SMEM)


def cost_of(micros):
    return pl.CostEstimate(
        flops=int(micros * 1e9), bytes_accessed=int(micros * 1e5), transcendentals=0
    )


def call(kernel, outs, ins, scratch=(), micros=3, name=None, limit=24, out_specs=None):
    return pl.pallas_call(
        kernel,
        out_shape=outs,
        in_specs=ins,
        out_specs=out_specs
        or jax.tree.map(lambda o: smem() if o.dtype == jnp.int32 else vmem(), outs),
        scratch_shapes=list(scratch),
        compiler_params=params(limit << 20),
        cost_estimate=cost_of(micros),
        name=name,
    )


def sds(shape, dtype):
    return jax.ShapeDtypeStruct(shape, dtype)


def valid_rows(lengths, rows):
    index = lax.axis_index("ctx") * lax.axis_size("exp") + lax.axis_index("exp")
    return lengths[0] - index * rows


def route_kernel(n_experts, sc, routes_t, dy, router_t, places, pick, w3, w3_t, full, *pay):
    places[0] = lax.rem(lax.axis_index("ctx"), 2)
    rows = dy.shape[0]
    width = dy.shape[1]
    table = jnp.concatenate(
        [router_t[...], jnp.zeros((128 - n_experts, width), f32)], axis=0
    )
    high = table.astype(bf16).astype(f32)
    mid = (table - high).astype(bf16).astype(f32)
    low = table - high - mid
    table = high + pltpu.roll(mid, n_experts, 0) + pltpu.roll(low, 2 * n_experts, 0)
    w3_t[...] = table.astype(bf16)
    w3[...] = table.T.astype(bf16)
    first, second = routes_t[0:1, :], routes_t[1:2, :]
    eight = iota((8, rows), 0)
    named = jnp.where((first == eight) | (second == eight), 1.0, 0.0)
    upper = jnp.where(iota((rows, rows), 0) < iota((rows, rows), 1), 1.0, 0.0)
    rank = dot(named.astype(bf16), upper.astype(bf16), NN)
    slot = iota((CAP, rows), 0).astype(f32)
    for e in range(n_experts):
        hit = (named[e : e + 1] > 0.5) & (rank[e : e + 1] == slot)
        pick[e * CAP : (e + 1) * CAP, :] = jnp.where(hit, 1.0, 0.0).astype(bf16)
    all_pick = pick[...].astype(f32)
    valid = iota((1, rows), 1) < valid_rows(sc, rows)
    live = jnp.where(valid, all_pick, 0.0).astype(bf16)
    full[:, :width] = dot(live, dy[...], NN).astype(bf16)
    line = iota((128, rows), 0)
    kind = jnp.where(line < 3 * n_experts, lax.rem(line, n_experts), -1)
    pair = jnp.where((first == kind) | (second == kind), 1.0, 0.0).astype(bf16)
    full[:, width:] = dot(pick[...], pair, NT).astype(bf16)
    for k, piece in enumerate(pay):
        expert = lax.rem(lax.axis_index("exp") + k, n_experts)
        piece[...] = full[pl.ds(pl.multiple_of(expert * CAP, 16), CAP), :]


def head_index(n_heads):
    index = lax.axis_index("ctx") * lax.axis_size("exp") + lax.axis_index("exp")
    return lax.rem(index, n_heads)


def bias_tiles(rel, buckets, brow, tiles):
    n_tiles, side, _ = tiles.shape
    n_heads, n_buckets = rel.shape
    head = head_index(n_heads)
    ids = buckets[...]
    row = jnp.zeros(ids.shape, f32)
    for b in range(n_buckets):
        row = jnp.where(ids == b, rel[head, b], row)
    brow[:, :side] = jnp.zeros((1, side), f32)
    brow[:, side:] = row
    for o in range(n_tiles):
        wide = jnp.broadcast_to(brow[:, o * side : (o + 2) * side], (side, 2 * side))
        tiles[o] = pltpu.roll(wide, 0, axis=1, stride=1, stride_axis=0)[:, side:]


def at_tile(index, side):
    return index * side if isinstance(index, int) else pl.multiple_of(index * side, side)


def loop(count, body, state):
    if isinstance(count, int) and count <= 4:
        for i in range(count):
            state = body(i, state)
        return state
    return lax.fori_loop(0, count, body, state)


def attn_kernel(shifts, head_dim, sc, rel, *refs):
    n_pieces = len(shifts)
    pieces = refs[:n_pieces]
    gain, w_qkv, buckets = refs[n_pieces : n_pieces + 3]
    kept, (out_t, lse) = refs[n_pieces + 3 : n_pieces + 9], refs[n_pieces + 9 : n_pieces + 11]
    h1, qa, ka, va, qt, kt, vt, brow, tiles, window, weight, sem, sems = refs[n_pieces + 11 :]
    head = head_index(rel.shape[0])
    pair_at = pl.multiple_of((head // 2) * 6 * head_dim, 128)
    fetch = pltpu.make_async_copy(w_qkv.at[:, pl.ds(pair_at, 6 * head_dim)], window, sem)
    fetch.start()
    bias_tiles(rel, buckets, brow, tiles)
    fetch.wait()
    odd = lax.rem(head, 2) == 1
    for i in range(3):
        even_part = window[:, i * head_dim : (i + 1) * head_dim]
        odd_part = window[:, (3 + i) * head_dim : (4 + i) * head_dim]
        part = jnp.where(odd, odd_part.astype(f32), even_part.astype(f32)).astype(bf16)
        pad = jnp.zeros((window.shape[0], 128 - head_dim), bf16)
        weight[:, i * 128 : (i + 1) * 128] = jnp.concatenate([part, pad], axis=1)
    n_exp = lax.axis_size("exp")
    n_x = lax.axis_size("ctx") // 2
    ctx, exp = lax.axis_index("ctx"), lax.axis_index("exp")

    def piece_start(b, o, k):
        if b < 0:
            return 0
        x_at = lax.rem(ctx // 2 + (n_x - b), n_x)
        core = lax.rem(lax.rem(ctx, 2) + o, 2)
        return ((x_at * 2 + core) * n_exp + lax.rem(exp + (n_exp - k), n_exp)) * 128

    n_tiles, side, _ = tiles.shape
    length = sc[0]
    lane = iota((128, 128), 1)

    def rows_in(x, start):
        x = x.astype(f32)
        h = (x * norm_scale(x) * row_of(gain)).astype(bf16)
        h1[pl.ds(start, 128), :] = h
        qkv = dot(h, weight[...], NN).astype(bf16).astype(f32)
        q, k, v = qkv[:, :128] * 0.125, qkv[:, 128:256], qkv[:, 256:]
        live = jnp.where(start + iota((128, 128), 0) < length, 0.0, NEG)
        qa[pl.ds(start, 128), :] = jnp.where(lane == head_dim, 1.0, q).astype(bf16)
        ka[pl.ds(start, 128), :] = jnp.where(lane == head_dim, live, k).astype(bf16)
        va[pl.ds(start, 128), :] = v.astype(bf16)
        qt[:, pl.ds(start, 128)] = q.T[:head_dim].astype(bf16)
        kt[:, pl.ds(start, 128)] = k.T[:head_dim].astype(bf16)
        vt[:, pl.ds(start, 128)] = v.T[:head_dim].astype(bf16)

    for i, piece in enumerate(pieces):
        if piece.shape[0] == 128:
            rows_in(piece[...], pl.multiple_of(piece_start(*shifts[i]), 128))
        else:

            def step(j, carry, piece=piece):
                start = pl.multiple_of(j * 128, 128)
                rows_in(piece[pl.ds(start, 128), :], start)
                return carry

            lax.fori_loop(0, piece.shape[0] // 128, step, 0)
    leave = [
        pltpu.make_async_copy(src, dst, sems.at[i])
        for i, (src, dst) in enumerate(zip((h1, qa, ka, va, qt, kt), kept))
    ]
    for copy in leave:
        copy.start()
    blocks = side // 128

    def one_query_tile(qi, carry):
        q_start = at_tile(qi, side)
        q = qa[pl.ds(q_start, side), :]

        def fold(k_start, offset, state, diagonal):
            top, total, acc = state
            scores = dot(ka[pl.ds(k_start, side), :], q, NT) + tiles[offset]
            if diagonal:
                scores = jnp.where(iota((side, side), 0) <= iota((side, side), 1), scores, NEG)
            new_top = jnp.maximum(top, jnp.max(scores, axis=0, keepdims=True))
            probs = jnp.exp(scores - new_top)
            scale = jnp.exp(top - new_top)
            total = total * scale + jnp.sum(probs, axis=0, keepdims=True)
            acc = acc * scale + dot(vt[:, pl.ds(k_start, side)], probs.astype(bf16), NN)
            return new_top, total, acc

        state = (
            jnp.full((1, side), NEG, f32),
            jnp.zeros((1, side), f32),
            jnp.zeros((head_dim, side), f32),
        )
        state = fold(q_start, 0, state, True)

        def earlier(kj, state):
            return fold(at_tile(kj, side), qi - kj, state, False)

        top, total, acc = loop(qi, earlier, state)
        result = (acc / total).astype(bf16)
        lse[:, pl.ds(q_start, side)] = top + jnp.log(total)
        for b in range(blocks):
            out_t[qi * blocks + b] = result[:, b * 128 : (b + 1) * 128]
        return carry

    loop(n_tiles, one_query_tile, 0)
    for copy in leave:
        copy.wait()


def attn_back_kernel(head_dim, n_dp, rel, *refs):
    qa, ka, va, qt, kt, out_t, grad_t, lse, h1_far, buckets = refs[:10]
    pay, weight_pay = refs[10:12]
    dq, dk, dv, full, brow, tiles, sums, diag, h1, sem = refs[12:]
    fetch = pltpu.make_async_copy(h1_far, h1, sem)
    fetch.start()
    n_tiles, side, _ = tiles.shape
    blocks = side // 128
    bias_tiles(rel, buckets, brow, tiles)
    sums[...] = jnp.zeros_like(sums)
    dk[...] = jnp.zeros_like(dk)
    dv[...] = jnp.zeros_like(dv)

    def one_query_tile(qi, carry):
        q_start = at_tile(qi, side)
        q = qa[pl.ds(q_start, side), :]
        q_t = qt[:, pl.ds(q_start, side)]
        g_t = jnp.concatenate([grad_t[qi * blocks + b] for b in range(blocks)], axis=1)
        o_t = jnp.concatenate([out_t[qi * blocks + b] for b in range(blocks)], axis=1)
        row_dots = jnp.sum(g_t.astype(f32) * o_t.astype(f32), axis=0, keepdims=True)
        norm = lse[:, pl.ds(q_start, side)]

        def fold(k_start, offset, acc, diagonal):
            where_k = pl.ds(k_start, side)
            scores = dot(ka[where_k, :], q, NT) + tiles[offset]
            probs = jnp.exp(scores - norm)
            if diagonal:
                probs = jnp.where(iota((side, side), 0) <= iota((side, side), 1), probs, 0.0)
            grad_prob = dot(va[where_k, :][:, :head_dim], g_t, NN)
            grad_score = probs * (grad_prob - row_dots)
            low = grad_score.astype(bf16)
            sums[offset] = sums[offset] + grad_score
            dv[:, where_k] = dv[:, where_k] + dot(g_t, probs.astype(bf16), NT)
            dk[:, where_k] = dk[:, where_k] + dot(q_t, low, NT)
            return acc + dot(kt[:, where_k], low, NN)

        acc = fold(q_start, 0, jnp.zeros((head_dim, side), f32), True)

        def earlier(kj, acc):
            return fold(at_tile(kj, side), qi - kj, acc, False)

        dq[:, pl.ds(q_start, side)] = loop(qi, earlier, acc)
        return carry

    loop(n_tiles, one_query_tile, 0)
    full[:head_dim, :] = (dq[...] * 0.125).astype(bf16)
    full[head_dim : 2 * head_dim, :] = dk[...].astype(bf16)
    full[2 * head_dim :, :] = dv[...].astype(bf16)
    for b in range(pay.shape[0]):
        pay[b] = full[:, b * 128 : (b + 1) * 128]
    flip = jnp.where(iota((128, 128), 0) + iota((128, 128), 1) == 127, 1.0, 0.0).astype(bf16)
    diag[...] = jnp.zeros_like(diag)
    for o in range(n_tiles):
        for a in range(blocks):
            turned = dot(flip, sums[o, a * 128 : (a + 1) * 128, :].astype(bf16), NN)
            wide = jnp.concatenate([turned, jnp.zeros((128, 128), f32)], axis=1)
            lined = pltpu.roll(wide, 0, axis=1, stride=1, stride_axis=0)
            first = (o + 1) * side - (a + 1) * 128
            where_d = slice(first, first + side + 128)
            diag[:, where_d] = diag[:, where_d] + jnp.sum(lined, axis=0, keepdims=True)
    ids = jnp.concatenate([buckets[...], jnp.full((1, side), -1, jnp.int32)], axis=1)
    ids = pltpu.roll(ids, side - 1, 1)
    hot = jnp.where(ids == iota((128, ids.shape[1]), 0), 1.0, 0.0).astype(bf16)
    high, low = split2(jnp.broadcast_to(diag[...], (8, diag.shape[1])))
    rel_grad = dot(high, hot, NT) + dot(low, hot, NT)
    fetch.wait()
    grad_w = dot(full[...], h1[...], NN).astype(bf16)
    n_pay, pay_rows, lanes = weight_pay.shape
    n_ctx = n_pay // n_dp
    rows = grad_w.shape[0] // n_ctx
    rel_rows = jnp.concatenate([rel_grad, jnp.zeros((8, lanes - 128), f32)], axis=1)
    rel_rows = jnp.concatenate([rel_rows, jnp.zeros((8, lanes), f32)], axis=0).astype(bf16)
    for d in range(n_dp):
        for c in range(n_ctx):
            weight_pay[d * n_ctx + c, :rows, :] = grad_w[
                c * rows : (c + 1) * rows, d * lanes : (d + 1) * lanes
            ]
            weight_pay[d * n_ctx + c, rows:, :] = rel_rows


def middle_kernel(n_heads, sc, recv, w_out, x, gain, pick, middle, *send):
    rows, width = x.shape
    attn_t = jnp.concatenate([recv[h] for h in range(n_heads)], axis=0)
    branch = dot(attn_t, w_out[...], TN)
    valid = iota((rows, 1), 0) < valid_rows(sc, rows)
    mid = x[...].astype(f32) + jnp.where(valid, branch, 0.0)
    middle[...] = mid
    h2 = (mid * norm_scale(mid) * row_of(gain)).astype(bf16)
    for k, piece in enumerate(send):
        expert = lax.rem(lax.axis_index("exp") + k, len(send))
        chosen = pick[pl.ds(pl.multiple_of(expert * CAP, 16), CAP), :]
        piece[...] = dot(chosen, h2, NN).astype(bf16)


def gate_of(h2, pay, width, w3, own):
    logits = dot(h2, w3, NN)
    sel = 2.0 * own - pay[:, width:].astype(f32)
    diff = jnp.sum(logits * sel, axis=1, keepdims=True)
    return 1.0 / (1.0 + jnp.exp(-diff)), sel


def own_lanes(expert, n_experts):
    lane = iota((1, 128), 1)
    return jnp.where((lane < 3 * n_experts) & (lane % n_experts == expert), 1.0, 0.0)


def expert_kernel(n_experts, h2, pay, w3, w3_t, w_up, w_down, *refs):
    mix, back = refs[:n_experts], refs[n_experts : 2 * n_experts]
    router, z_acc, in_acc, dz, gates, rows_out = refs[2 * n_experts :]
    step = pl.program_id(0)
    width = h2.shape[1]
    expert = lax.axis_index("exp")
    own = own_lanes(expert, n_experts)

    @pl.when(step == 0)
    def _():
        gate, _ = gate_of(h2[...], pay, width, w3[...], own)
        gates[...] = jnp.broadcast_to(gate, gates.shape)
        dz[...] = (gate * pay[:, :width].astype(f32)).astype(bf16)
        z_acc[...] = jnp.zeros_like(z_acc)
        in_acc[...] = jnp.zeros_like(in_acc)

    up = dot(h2[...], w_up[...], NN)
    act, slope = gelu_parts(up)
    grad_hidden = dot(dz[...], w_down[...], NT)
    grad_up = (grad_hidden * slope).astype(bf16)
    z_acc[...] += dot(act.astype(bf16), w_down[...], NN)
    in_acc[...] += dot(grad_up, w_up[...], NT)

    @pl.when(step == pl.num_programs(0) - 1)
    def _():
        gate = gates[:, 0:1]
        sel = 2.0 * own - pay[:, width:].astype(f32)
        z = z_acc[...].astype(bf16).astype(f32)
        rows_out[...] = (gate * z).astype(bf16)
        for k in range(n_experts):
            mix[k][...] = rows_out[k * CAP : (k + 1) * CAP, :]
        grad_gate = jnp.sum(pay[:, :width].astype(f32) * z, axis=1, keepdims=True)
        high, low = split2((gate * (1.0 - gate) * grad_gate) * sel)
        total = in_acc[...] + dot(high, w3_t[...], NN) + dot(low, w3_t[...], NN)
        rows_out[...] = total.astype(bf16)
        for k in range(n_experts):
            back[k][...] = rows_out[k * CAP : (k + 1) * CAP, :]
        router[...] = (dot(high, h2[...], TN) + dot(low, h2[...], TN))[:8]


def collect(pieces, pick):
    n_experts = len(pieces)
    total = None
    for k, piece in enumerate(pieces):
        expert = lax.rem(lax.axis_index("exp") + k, n_experts)
        chosen = pick[pl.ds(pl.multiple_of(expert * CAP, 16), CAP), :]
        part = dot(chosen, piece[...], TN)
        total = part if total is None else total + part
    return total


def middle_back_kernel(n_heads, n_experts, sc, *refs):
    back = refs[:n_experts]
    pick, middle, dy, gain, recv, w_out, router, dmid, grad_t, red = refs[n_experts:]
    rows, width = middle.shape
    grad_h2 = collect(back, pick)
    grad_in, xhat = norm_back(middle[...], row_of(gain), grad_h2)
    grad_mid = dy[...].astype(f32) + grad_in
    dmid[...] = grad_mid
    valid = iota((rows, 1), 0) < valid_rows(sc, rows)
    branch = jnp.where(valid, grad_mid, 0.0).astype(bf16)
    attn_t = jnp.concatenate([recv[h] for h in range(n_heads)], axis=0)
    heads = dot(w_out[...], branch, NT).astype(bf16)
    head_dim = width // n_heads
    for h in range(n_heads):
        grad_t[h] = heads[h * head_dim : (h + 1) * head_dim]
    for h in range(n_heads, grad_t.shape[0]):
        grad_t[h] = jnp.zeros((head_dim, rows), bf16)
    red[:width, :] = dot(attn_t, branch, NN).astype(bf16)
    gains = jnp.sum(grad_h2 * xhat, axis=0, keepdims=True)
    small = jnp.concatenate([jnp.broadcast_to(gains, (8, width)), router[...]], axis=0)
    red[width : width + 16, :] = small.astype(bf16)
    rest = red.shape[0] - width - 16
    red[width + 16 :, :] = jnp.zeros((rest, width), bf16)


def output_kernel(n_experts, sc, *refs):
    mix = refs[:n_experts]
    pick, middle, out = refs[n_experts:]
    rows = middle.shape[0]
    valid = iota((rows, 1), 0) < valid_rows(sc, rows)
    total = collect(mix, pick)
    out[...] = (middle[...] + jnp.where(valid, total, 0.0)).astype(bf16)


def token_grad_kernel(n_heads, recv, w_qkv, x, gain, dmid, out):
    grad_t = jnp.concatenate([recv[h] for h in range(n_heads)], axis=0)
    grad_h1 = dot(w_qkv[...], grad_t, NN).T
    grad_in, _ = norm_back(x[...].astype(f32), row_of(gain), grad_h1)
    out[...] = dmid[...] + grad_in


def load_rows(h_pieces, where, pay_all, h2, pay, sem):
    rows = h_pieces[0].shape[0]
    copies = []
    for i, piece in enumerate(h_pieces):
        here = pl.ds(i * rows, rows)
        there = pl.ds(pl.multiple_of(where[i] * rows, 16), rows)
        copies.append(pltpu.make_async_copy(piece, h2.at[here, :], sem.at[0, i]))
        copies.append(pltpu.make_async_copy(pay_all.at[there, :], pay.at[here, :], sem.at[1, i]))
    return copies


def chip_index(a, b, o):
    n_dp = lax.axis_size("dp")
    n_x = lax.axis_size("ctx") // 2
    dp, ctx = lax.axis_index("dp"), lax.axis_index("ctx")
    core = lax.rem(lax.rem(ctx, 2) + o, 2)
    x_at = lax.rem(ctx // 2 + (n_x - b), n_x)
    return (lax.rem(dp + (n_dp - a), n_dp) * n_x + x_at) * 2 + core


def weight_grad_kernel(n_experts, keys, together, sc, *refs):
    n_pieces = len(keys)
    h_pieces = refs[:n_pieces]
    pay_all, w3, w_up, w_down = refs[n_pieces : n_pieces + 4]
    up_out, down_out, low, h2, pay, dz, hid_t, dup_t, sem = refs[-9:]
    step = pl.program_id(0)
    rows = h_pieces[0].shape[0]
    width = h2.shape[1]
    block = w_down.shape[0]
    copies = load_rows(h_pieces, [chip_index(*key) for key in keys], pay_all, h2, pay, sem)

    @pl.when(step == 0)
    def _():
        for copy in copies:
            copy.start()

    own = own_lanes(lax.axis_index("exp"), n_experts)
    up_t = w_up[...].T
    down = w_down[...]
    chunk = together * rows
    for i in range(n_pieces // together):
        here = slice(i * chunk, (i + 1) * chunk)

        @pl.when(step == 0)
        def _(i=i, here=here):
            for copy in copies[2 * together * i : 2 * together * (i + 1)]:
                copy.wait()
            part = pay[here, :]
            gate, _ = gate_of(h2[here, :], part, width, w3[...], own)
            dz[here, :] = (gate * part[:, :width].astype(f32)).astype(bf16)

        act, slope = gelu_parts(dot(up_t, h2[here, :], NT))
        hid_t[:, here] = act.astype(bf16)
        dup_t[:, here] = (dot(down, dz[here, :], NT) * slope).astype(bf16)
    grad_up = dot(dup_t[...], h2[...], NN)
    low[:block, :] = grad_up.astype(bf16)
    up_out[...] = grad_up.T
    grad_down = dot(hid_t[...], dz[...], NN)
    low[block:, :] = grad_down.astype(bf16)
    down_out[...] = grad_down


def fill_kernel(sc, low, *refs):
    up_out, down_out = refs[-2:]
    block = down_out.shape[0]
    up_out[...] = low[:block, :].astype(f32).T
    down_out[...] = low[block:, :].astype(f32)


def assemble_kernel(keys, rows, n_groups, head_cols, *refs):
    n_pieces = len(keys)
    pieces = refs[:n_pieces]
    w_qkv, gain, grad, gain_grad, rel_grad, turned, rel_t, stage, sem = refs[n_pieces:]
    lanes = pieces[0].shape[-1]
    n_dp, n_exp = lax.axis_size("dp"), lax.axis_size("exp")
    n_x = lax.axis_size("ctx") // 2
    dp, ctx, exp = (lax.axis_index(name) for name in ("dp", "ctx", "exp"))
    rel_t[...] = jnp.zeros_like(rel_t)
    for piece, ids in zip(pieces, keys):
        for i, (a, b, o, k) in enumerate(ids):
            d = lax.rem(dp + (n_dp - a), n_dp)
            c = lax.rem(ctx // 2 + (n_x - b), n_x) * 2 + lax.rem(lax.rem(ctx, 2) + o, 2)
            e = lax.rem(exp + (n_exp - k), n_exp)
            lane_at = pl.multiple_of(d * lanes, 128)
            for g in range(n_groups):
                head = g * n_exp + e
                row_at = pl.multiple_of(head * head_cols + c * rows, 16)
                turned[pl.ds(row_at, rows), pl.ds(lane_at, lanes)] = piece[
                    i, g * rows : (g + 1) * rows, :
                ]
                rel_t[pl.ds(head, 1), :] = piece[
                    i, n_groups * rows + g : n_groups * rows + g + 1, :128
                ].astype(f32)
    rel_grad[...] = rel_t[: rel_grad.shape[0], : rel_grad.shape[1]]
    width, columns = grad.shape
    copies = []
    for i, a in enumerate(range(0, width, 128)):
        total = jnp.zeros((128, 128), f32)
        for b in range(0, columns, 128):
            tile = turned[b : b + 128, a : a + 128].astype(f32).T
            stage[a : a + 128, b : b + 128] = tile
            total = total + tile * w_qkv[a : a + 128, b : b + 128].astype(f32)
        where_a = pl.ds(a, 128)
        copy = pltpu.make_async_copy(stage.at[where_a, :], grad.at[where_a, :], sem.at[i])
        copy.start()
        copies.append(copy)
        sums = jnp.sum(total.T, axis=0, keepdims=True)
        sums = sums / gain[a : a + 128].reshape(1, 128)
        gain_grad[a : a + 128] = sums.reshape(128)
    for copy in copies:
        copy.wait()


def shard_kernel(n_dp, n_groups, summed, shard):
    n_ctx = summed.shape[0] // n_dp
    part = summed.shape[1] - 16
    extra = iota((16, summed.shape[2]), 0)
    tail = jnp.zeros(extra.shape, f32)
    for g in range(n_groups):
        total = summed[g].astype(f32)
        for d in range(1, n_dp):
            total = total + summed[d * n_ctx + g].astype(f32)
        shard[0, g * part : (g + 1) * part, :] = total[:part].astype(bf16)
        tail = jnp.where(extra == g, total[part:], tail)
    shard[0, n_groups * part :, :] = tail.astype(bf16)


def reduced_kernel(n_experts, red, attn_out, gain_grad, router_grad):
    width = attn_out.shape[0]
    attn_out[...] = red[:width, :].astype(f32)
    rows = red[width : width + 16, :].astype(f32)
    gain_grad[...] = rows[0:1].reshape(width)
    router_grad[...] = rows[8 : 8 + n_experts]


def after(value, *others):
    return lax.optimization_barrier((value, others))[0]


def on_device(
    n_dp,
    n_ctx,
    n_exp,
    tokens,
    lengths,
    routes,
    buckets,
    cotangent,
    attn_gain,
    w_qkv,
    w_attn_out,
    rel_bias,
    ffn_gain,
    w_router,
    w_up,
    w_down,
):
    x = tokens[0]
    dy = cotangent[0]
    rows, width = x.shape
    seq = buckets.shape[0]
    n_buckets, n_heads = rel_bias.shape
    head_dim = width // n_heads
    n_experts = w_router.shape[1]
    ff = w_up.shape[2]
    n_slot = n_ctx * n_exp
    n_groups = n_heads // n_exp
    n_x = n_ctx // 2
    small = n_x == 2 and n_dp == 2
    side = 512 if seq <= 2048 else 256
    n_tiles = seq // side
    slot_rows = n_experts * CAP
    slot_axes, all_chips = ("ctx", "exp"), ("dp", "ctx")

    def ring(v, shift):
        return lax.ppermute(v, "exp", [(i, (i + shift) % n_exp) for i in range(n_exp)])

    def swap(v):
        return lax.ppermute(v, "ctx", [(i, i ^ 1) for i in range(n_ctx)])

    def chips(v, a, b):
        perm = []
        for d in range(n_dp):
            for c in range(n_ctx):
                to = ((d + a) % n_dp) * n_ctx + ((c // 2 + b) % n_x) * 2 + c % 2
                perm.append((d * n_ctx + c, to))
        return lax.ppermute(v, all_chips, perm)

    def exchange(v, axes):
        return lax.all_to_all(v, axes, split_axis=0, concat_axis=0, tiled=True)

    def to_experts(parts):
        return [parts[0]] + [ring(parts[k], k) for k in range(1, n_exp)]

    def from_experts(parts):
        return [parts[0]] + [ring(parts[k], n_exp - k) for k in range(1, n_exp)]

    keys = [(a, b, o) for o in (0, 1) for a, b in ((0, 0), (0, 1), (1, 0), (1, 1))]

    with jax.named_scope("routing"):
        places, pick, w3, w3_t, _, *pay = call(
            functools.partial(route_kernel, n_experts),
            [
                sds((1,), jnp.int32),
                sds((slot_rows, rows), bf16),
                sds((width, 128), bf16),
                sds((128, width), bf16),
                sds((slot_rows, width + 128), bf16),
            ]
            + [sds((CAP, width + 128), bf16)] * n_experts,
            [smem()] + [vmem()] * 3,
            name="routing",
        )(lengths, routes[0].T, dy, w_router.T)

    with jax.named_scope("gather_tokens"):
        if small:
            column = [(x, 0, 0), (ring(after(x, pick), 1), 0, 1)]
            column += [(ring(x, k), 0, k) for k in range(2, n_exp)]
            onward = [v for v, _, _ in column]
            onward[-1] = after(onward[-1], pay)
            pieces = column + [(chips(v, 0, 1), 1, k) for k, v in enumerate(onward)]
            pieces = [(v, b, 0, k) for v, b, k in pieces]
            arrived = to_experts(after(pay, pieces[-1][0]))
            pieces = pieces + [(swap(v), b, 1, k) for v, b, _, k in pieces]
            blocks = [v for v, _, _, _ in pieces]
            shifts = [ids for _, *ids in pieces]
        else:
            blocks = [lax.all_gather(x, slot_axes, axis=0, tiled=True)]
            shifts = [(-1, 0, 0)]
            arrived = to_experts(pay)

    with jax.named_scope("attention"):
        bucket_row = buckets.reshape(1, seq)
        blocks[-1] = after(blocks[-1], bucket_row)
        attn_outs = (
            sds((seq, width), bf16),
            sds((seq, 128), bf16),
            sds((seq, 128), bf16),
            sds((seq, 128), bf16),
            sds((head_dim, seq), bf16),
            sds((head_dim, seq), bf16),
            sds((n_slot, head_dim, 128), bf16),
            sds((1, seq), f32),
        )
        any_spec = pl.BlockSpec(memory_space=pl.ANY)
        h1, qa, ka, va, qt, kt, out_t, lse = call(
            functools.partial(attn_kernel, shifts, head_dim),
            attn_outs,
            [smem(), smem()] + [vmem()] * (len(blocks) + 1) + [any_spec, vmem()],
            [pltpu.VMEM(o.shape, o.dtype) for o in attn_outs[:6]]
            + [
                pltpu.VMEM((head_dim, seq), bf16),
                pltpu.VMEM((1, seq + side), f32),
                pltpu.VMEM((n_tiles, side, side), f32),
                pltpu.VMEM((width, 6 * head_dim), bf16),
                pltpu.VMEM((width, 384), bf16),
                pltpu.SemaphoreType.DMA,
                pltpu.SemaphoreType.DMA((6,)),
            ],
            micros=10,
            name="attention",
            limit=58,
            out_specs=(any_spec,) * 6 + (vmem(),) * 2,
        )(lengths, rel_bias.T, *blocks, attn_gain, w_qkv, bucket_row)
        attn_in = exchange(out_t, slot_axes)
        pay_in = jnp.concatenate([arrived[0]] + [after(v, out_t) for v in arrived[1:]])

    with jax.named_scope("middle"):
        piece_shape = sds((CAP, width), bf16)
        middle, *send = call(
            functools.partial(middle_kernel, n_heads),
            [sds((rows, width), f32)] + [piece_shape] * n_experts,
            [smem()] + [vmem()] * 5,
            name="middle",
        )(lengths, attn_in, w_attn_out, x, ffn_gain, pick)
        h2_in = jnp.concatenate(to_experts(send))

    with jax.named_scope("experts"):
        block = 512
        row_spec = pl.BlockSpec((slot_rows, width), lambda i: (0, 0))
        piece_spec = pl.BlockSpec((CAP, width), lambda i: (0, 0))
        *parts, router = pl.pallas_call(
            functools.partial(expert_kernel, n_experts),
            out_shape=[piece_shape] * (2 * n_experts)
            + [sds((8, width), f32)],
            grid_spec=pltpu.PrefetchScalarGridSpec(
                num_scalar_prefetch=0,
                grid=(ff // block,),
                in_specs=[
                    row_spec,
                    pl.BlockSpec((slot_rows, width + 128), lambda i: (0, 0)),
                    pl.BlockSpec((width, 128), lambda i: (0, 0)),
                    pl.BlockSpec((128, width), lambda i: (0, 0)),
                    pl.BlockSpec((width, block), lambda i: (0, i)),
                    pl.BlockSpec((block, width), lambda i: (i, 0)),
                ],
                out_specs=[piece_spec] * (2 * n_experts)
                + [pl.BlockSpec((8, width), lambda i: (0, 0))],
                scratch_shapes=[
                    pltpu.VMEM((slot_rows, width), f32),
                    pltpu.VMEM((slot_rows, width), f32),
                    pltpu.VMEM((slot_rows, width), bf16),
                    pltpu.VMEM((slot_rows, 128), f32),
                    pltpu.VMEM((slot_rows, width), bf16),
                ],
            ),
            compiler_params=params(),
            cost_estimate=cost_of(12),
            name="experts",
        )(h2_in, pay_in, w3, w3_t, w_up[0], w_down[0])
        mix_parts, back_parts = parts[:n_experts], parts[n_experts:]
        back_in = from_experts(back_parts)

    shares = n_dp * n_ctx
    with jax.named_scope("expert_weight_grads"):
        if small:
            pay_all = lax.all_gather(pay_in, all_chips, axis=0, tiled=True)
            beside = [chips(h2_in, a, b) for a, b in ((0, 1), (1, 0), (1, 1))]
            block = 512
            n_parts = ff // (2 * block)
            full_shapes = [sds((width, ff), f32), sds((ff, width), f32)]

            back_in[0] = after(back_in[0], beside, pay_all)

            def half_specs(other):
                def at(i, s):
                    return (1 - s[0] if other else s[0]) * n_parts + i

                return (
                    pl.BlockSpec((width, block), lambda i, s: (0, at(i, s))),
                    pl.BlockSpec((block, width), lambda i, s: (at(i, s), 0)),
                )

            low_spec = pl.BlockSpec((2 * block, width), lambda i, s: (i, 0))

            def weight_half(pieces):
                specs = half_specs(False)
                count = len(pieces) * slot_rows
                return pl.pallas_call(
                    functools.partial(weight_grad_kernel, n_experts, keys, 2),
                    out_shape=full_shapes + [sds((ff, width), bf16)],
                    grid_spec=pltpu.PrefetchScalarGridSpec(
                        num_scalar_prefetch=1,
                        grid=(n_parts,),
                        in_specs=[any_spec] * (len(pieces) + 1)
                        + [pl.BlockSpec((width, 128), lambda i, s: (0, 0)), *specs],
                        out_specs=[*specs, low_spec],
                        scratch_shapes=[
                            pltpu.VMEM((count, width), bf16),
                            pltpu.VMEM((count, width + 128), bf16),
                            pltpu.VMEM((count, width), bf16),
                            pltpu.VMEM((block, count), bf16),
                            pltpu.VMEM((block, count), bf16),
                            pltpu.SemaphoreType.DMA((2, len(pieces))),
                        ],
                    ),
                    compiler_params=params(),
                    cost_estimate=cost_of(36),
                    name="weight_grads",
                )(places, *pieces, pay_all, w3, w_up[0], w_down[0])

            def weight_fill(low, grads):
                return pl.pallas_call(
                    fill_kernel,
                    out_shape=full_shapes,
                    grid_spec=pltpu.PrefetchScalarGridSpec(
                        num_scalar_prefetch=1,
                        grid=(n_parts,),
                        in_specs=[low_spec, any_spec, any_spec],
                        out_specs=half_specs(True),
                    ),
                    input_output_aliases={2: 0, 3: 1},
                    compiler_params=params(),
                    cost_estimate=cost_of(8),
                    name="fill",
                )(places, low, *grads)


    with jax.named_scope("middle_back"):
        red_rows = -(-(width + 16) // (16 * shares)) * 16 * shares
        dmid, grad_t, red = call(
            functools.partial(middle_back_kernel, n_heads, n_experts),
            (
                sds((rows, width), f32),
                sds((n_slot, head_dim, rows), bf16),
                sds((red_rows, width), bf16),
            ),
            [smem()] + [vmem()] * (7 + n_experts),
            name="middle_back",
        )(lengths, *back_in, pick, middle, dy, ffn_gain, attn_in, w_attn_out, router)
        grad_in = exchange(grad_t, slot_axes)

    if small:
        with jax.named_scope("expert_weight_grads"):
            own_side = [h2_in] + beside
            own_side = [after(v, grad_t) for v in own_side]
            pieces = own_side + [swap(v) for v in own_side]
            *grads, low = weight_half(pieces)
            share = lax.psum_scatter(red, all_chips, scatter_dimension=0, tiled=True)
            grad_in = after(grad_in, low, share)
            others = [ring(share, k) for k in range(1, n_exp)]

    with jax.named_scope("attention_back"):
        part = 3 * head_dim // n_ctx
        lanes = width // n_dp
        dqkv, weight_pay = call(
            functools.partial(attn_back_kernel, head_dim, n_dp),
            (sds((n_slot, 3 * head_dim, rows), bf16), sds((shares, part + 16, lanes), bf16)),
            [smem()] + [vmem()] * 8 + [any_spec, vmem()],
            [
                pltpu.VMEM((head_dim, seq), f32),
                pltpu.VMEM((head_dim, seq), f32),
                pltpu.VMEM((head_dim, seq), f32),
                pltpu.VMEM((3 * head_dim, seq), bf16),
                pltpu.VMEM((1, seq + side), f32),
                pltpu.VMEM((n_tiles, side, side), f32),
                pltpu.VMEM((n_tiles, side, side), f32),
                pltpu.VMEM((1, seq + side), f32),
                pltpu.VMEM((seq, width), bf16),
                pltpu.SemaphoreType.DMA,
            ],
            micros=11,
            name="attention_back",
            limit=58,
        )(rel_bias.T, qa, ka, va, qt, kt, out_t, grad_in, lse, h1, bucket_row)
        if small:
            weight_pay = after(weight_pay, others)
            share = share.astype(f32) + others[0] + others[1] + others[2]
            share = after(share, weight_pay).astype(bf16)
        else:
            mix_in = from_experts(mix_parts)
        summed = exchange(weight_pay, all_chips)
        if small:
            summed = after(summed, share)

    with jax.named_scope("projection_grad"):
        shard = call(
            functools.partial(shard_kernel, n_dp, n_groups),
            sds((1, n_groups * part + 16, lanes), bf16),
            [vmem()],
            name="shard",
        )(summed)
        if small:
            column = [ring(shard, k) for k in range(1, n_exp)]
            column = jnp.concatenate([shard] + column)
            low_in = swap(after(low, weight_pay))
            column = after(column, low_in)
            dqkv = after(dqkv, column)
            mix_in = from_experts([after(v, column) for v in mix_parts])


    if small:
        with jax.named_scope("expert_weight_grads"):
            grad_up, grad_down = weight_fill(low_in, grads)
    else:
        with jax.named_scope("expert_weight_grads"):
            own = own_lanes(lax.axis_index("exp"), n_experts)
            gate, _ = gate_of(h2_in, pay_in, width, w3, own)
            dz = (gate * pay_in[:, :width].astype(f32)).astype(bf16)
            act, slope = gelu_parts(dot(h2_in, w_up[0], NN))
            dup = (dot(dz, w_down[0], NT) * slope).astype(bf16)
            grad_up = lax.psum(dot(h2_in, dup, TN).astype(bf16), all_chips).astype(f32)
            grad_down = lax.psum(dot(act.astype(bf16), dz, TN).astype(bf16), all_chips)
            grad_down = grad_down.astype(f32)

    with jax.named_scope("output"):
        output = call(
            functools.partial(output_kernel, n_experts),
            sds((rows, width), bf16),
            [smem()] + [vmem()] * (2 + n_experts),
            name="output",
        )(lengths, *mix_in, pick, middle)

    with jax.named_scope("token_grads"):
        dqkv_in = exchange(dqkv, slot_axes)
        grad_tokens = call(
            functools.partial(token_grad_kernel, n_heads),
            sds((rows, width), f32),
            [vmem()] * 5,
            name="token_grads",
        )(dqkv_in, w_qkv, x, attn_gain, dmid)

    with jax.named_scope("output_projection_grad"):
        if small:
            reduced = lax.all_gather(share, all_chips, axis=0, tiled=True)
        else:
            reduced = lax.psum(red, ("dp", "ctx", "exp"))
        grad_attn_out, grad_ffn_gain, grad_router = call(
            functools.partial(reduced_kernel, n_experts),
            (sds((width, width), f32), sds((width,), f32), sds((n_experts, width), f32)),
            [vmem()],
            name="reduced",
        )(reduced)
        grad_router = grad_router.T

    with jax.named_scope("projection_grad"):
        if small:
            wide = [(column, 0, 0, range(n_exp))]
            for v, a, b in ((column, 0, 1), (column, 1, 0)):
                wide.append((chips(v, a, b), a, b, range(n_exp)))
            wide.append((chips(wide[1][0], 1, 0), 1, 1, range(n_exp)))
            early = (grad_tokens, grad_up, grad_down, grad_attn_out, mix_in)
            wide = [(after(v, early), a, b, ks) for v, a, b, ks in wide]
            final = [v for v, _, _, _ in wide] + [swap(v) for v, _, _, _ in wide]
            keys = [[(a, b, o, k) for k in ks] for o in (0, 1) for _, a, b, ks in wide]
            grad_qkv, grad_attn_gain, grad_rel = call(
                functools.partial(assemble_kernel, keys, part, n_groups, 3 * head_dim),
                (sds((width, 3 * width), f32), sds((width,), f32), sds((n_heads, n_buckets), f32)),
                [vmem()] * (len(final) + 2),
                [
                    pltpu.VMEM((3 * width, width), bf16),
                    pltpu.VMEM((128, 128), f32),
                    pltpu.VMEM((width, 3 * width), f32),
                    pltpu.SemaphoreType.DMA((width // 128,)),
                ],
                micros=6,
                name="assemble",
                limit=32,
                out_specs=(any_spec, vmem(), vmem()),
            )(*final, w_qkv, attn_gain)
            grad_rel = grad_rel.T
        else:
            every = lax.all_gather(shard[0], ("dp", "ctx", "exp"), axis=0, tiled=False)
            every = every.reshape(n_dp, n_ctx, n_exp, n_groups * part + 16, lanes).astype(f32)
            main = every[:, :, :, : n_groups * part]
            main = main.reshape(n_dp, n_ctx, n_exp, n_groups, part, lanes)
            grad_qkv = main.transpose(0, 5, 3, 2, 1, 4).reshape(width, 3 * width)
            rel_rows = every[0, 0, :, n_groups * part : n_groups * (part + 1), :n_buckets]
            grad_rel = rel_rows.transpose(2, 1, 0).reshape(n_buckets, n_heads)
            grad_attn_gain = jnp.sum(grad_qkv * w_qkv.astype(f32), axis=1) / attn_gain

    return (
        output[None],
        grad_tokens[None],
        grad_attn_gain,
        grad_qkv,
        grad_attn_out,
        grad_rel,
        grad_ffn_gain,
        grad_router,
        grad_up[None],
        grad_down[None],
    )


def solution(mesh):
    sizes = dict(mesh.shape)
    by_token = P("dp", ("ctx", "exp"), None)
    by_expert = P("exp", None, None)
    return jax.shard_map(
        functools.partial(on_device, sizes["dp"], sizes["ctx"], sizes["exp"]),
        mesh=mesh,
        in_specs=(
            by_token,
            P("dp"),
            by_token,
            P(),
            by_token,
            P(),
            P(),
            P(),
            P(),
            P(),
            P(),
            by_expert,
            by_expert,
        ),
        out_specs=(
            by_token,
            by_token,
            P(),
            P(),
            P(),
            P(),
            P(),
            P(),
            by_expert,
            by_expert,
        ),
        check_vma=False,
    )
```

```python
import functools

import jax
import jax.numpy as jnp
from jax import lax
from jax.experimental import pallas as pl
from jax.experimental.pallas import tpu as pltpu
from jax.sharding import PartitionSpec as P

CAP = 80
EPS = 1e-06
NEG = -1e30
VMEM_LIMIT = 58 << 20
bf16 = jnp.bfloat16
f32 = jnp.float32
NN = ((1,), (0,))
NT = ((1,), (1,))
TN = ((0,), (0,))
GELU_C = 0.7978845608028654
GELU_A = 0.044715


def dot(left, right, dims):
    return lax.dot_general(left, right, (dims, ((), ())), preferred_element_type=f32)


def iota(shape, axis):
    return lax.broadcasted_iota(jnp.int32, shape, axis)


def norm_scale(values):
    return lax.rsqrt(jnp.mean(values * values, axis=-1, keepdims=True) + EPS)


def row_of(ref):
    return ref[...].reshape(1, ref.shape[0])


def norm_back(values, gain, grad):
    scale = norm_scale(values)
    xhat = values * scale
    gxhat = grad * gain
    grad_in = scale * (gxhat - xhat * jnp.mean(gxhat * xhat, axis=-1, keepdims=True))
    return grad_in, xhat


def gelu_parts(u):
    square = u * u
    t = jnp.tanh(u * (GELU_C + (GELU_C * GELU_A) * square))
    half = 0.5 * (1.0 + t)
    slope = half + (0.5 * u) * (1.0 - t * t) * (GELU_C + (3.0 * GELU_C * GELU_A) * square)
    return u * half, slope


def split2(values):
    high = values.astype(bf16)
    return high, (values - high.astype(f32)).astype(bf16)


def params(limit=VMEM_LIMIT):
    return pltpu.CompilerParams(vmem_limit_bytes=limit)


def vmem():
    return pl.BlockSpec(memory_space=pltpu.VMEM)


def smem():
    return pl.BlockSpec(memory_space=pltpu.SMEM)


def cost_of(micros):
    return pl.CostEstimate(
        flops=int(micros * 1e9), bytes_accessed=int(micros * 1e5), transcendentals=0
    )


def call(kernel, outs, ins, scratch=(), micros=3, name=None, limit=24, out_specs=None):
    return pl.pallas_call(
        kernel,
        out_shape=outs,
        in_specs=ins,
        out_specs=out_specs
        or jax.tree.map(lambda o: smem() if o.dtype == jnp.int32 else vmem(), outs),
        scratch_shapes=list(scratch),
        compiler_params=params(limit << 20),
        cost_estimate=cost_of(micros),
        name=name,
    )


def sds(shape, dtype):
    return jax.ShapeDtypeStruct(shape, dtype)


def valid_rows(lengths, rows):
    index = lax.axis_index("ctx") * lax.axis_size("exp") + lax.axis_index("exp")
    return lengths[0] - index * rows


def route_kernel(n_experts, sc, routes_t, dy, router_t, places, pick, w3, w3_t, full, *pay):
    places[0] = lax.rem(lax.axis_index("ctx"), 2)
    rows = dy.shape[0]
    width = dy.shape[1]
    table = jnp.concatenate(
        [router_t[...], jnp.zeros((128 - n_experts, width), f32)], axis=0
    )
    high = table.astype(bf16).astype(f32)
    mid = (table - high).astype(bf16).astype(f32)
    low = table - high - mid
    table = high + pltpu.roll(mid, n_experts, 0) + pltpu.roll(low, 2 * n_experts, 0)
    w3_t[...] = table.astype(bf16)
    w3[...] = table.T.astype(bf16)
    first, second = routes_t[0:1, :], routes_t[1:2, :]
    eight = iota((8, rows), 0)
    named = jnp.where((first == eight) | (second == eight), 1.0, 0.0)
    upper = jnp.where(iota((rows, rows), 0) < iota((rows, rows), 1), 1.0, 0.0)
    rank = dot(named.astype(bf16), upper.astype(bf16), NN)
    slot = iota((CAP, rows), 0).astype(f32)
    for e in range(n_experts):
        hit = (named[e : e + 1] > 0.5) & (rank[e : e + 1] == slot)
        pick[e * CAP : (e + 1) * CAP, :] = jnp.where(hit, 1.0, 0.0).astype(bf16)
    all_pick = pick[...].astype(f32)
    valid = iota((1, rows), 1) < valid_rows(sc, rows)
    live = jnp.where(valid, all_pick, 0.0).astype(bf16)
    full[:, :width] = dot(live, dy[...], NN).astype(bf16)
    line = iota((128, rows), 0)
    kind = jnp.where(line < 3 * n_experts, lax.rem(line, n_experts), -1)
    pair = jnp.where((first == kind) | (second == kind), 1.0, 0.0).astype(bf16)
    full[:, width:] = dot(pick[...], pair, NT).astype(bf16)
    for k, piece in enumerate(pay):
        expert = lax.rem(lax.axis_index("exp") + k, n_experts)
        piece[...] = full[pl.ds(pl.multiple_of(expert * CAP, 16), CAP), :]


def head_index(n_heads):
    index = lax.axis_index("ctx") * lax.axis_size("exp") + lax.axis_index("exp")
    return lax.rem(index, n_heads)


def bias_tiles(rel, buckets, brow, tiles):
    n_tiles, side, _ = tiles.shape
    n_heads, n_buckets = rel.shape
    head = head_index(n_heads)
    ids = buckets[...]
    row = jnp.zeros(ids.shape, f32)
    for b in range(n_buckets):
        row = jnp.where(ids == b, rel[head, b], row)
    brow[:, :side] = jnp.zeros((1, side), f32)
    brow[:, side:] = row
    for o in range(n_tiles):
        wide = jnp.broadcast_to(brow[:, o * side : (o + 2) * side], (side, 2 * side))
        tiles[o] = pltpu.roll(wide, 0, axis=1, stride=1, stride_axis=0)[:, side:]


def at_tile(index, side):
    return index * side if isinstance(index, int) else pl.multiple_of(index * side, side)


def loop(count, body, state):
    if isinstance(count, int) and count <= 4:
        for i in range(count):
            state = body(i, state)
        return state
    return lax.fori_loop(0, count, body, state)


def attn_kernel(shifts, head_dim, sc, rel, *refs):
    n_pieces = len(shifts)
    pieces = refs[:n_pieces]
    gain, w_qkv, buckets = refs[n_pieces : n_pieces + 3]
    kept, (out_t, lse) = refs[n_pieces + 3 : n_pieces + 9], refs[n_pieces + 9 : n_pieces + 11]
    h1, qa, ka, va, qt, kt, vt, brow, tiles, window, weight, sem, sems = refs[n_pieces + 11 :]
    head = head_index(rel.shape[0])
    pair_at = pl.multiple_of((head // 2) * 6 * head_dim, 128)
    fetch = pltpu.make_async_copy(w_qkv.at[:, pl.ds(pair_at, 6 * head_dim)], window, sem)
    fetch.start()
    bias_tiles(rel, buckets, brow, tiles)
    fetch.wait()
    odd = lax.rem(head, 2) == 1
    for i in range(3):
        even_part = window[:, i * head_dim : (i + 1) * head_dim]
        odd_part = window[:, (3 + i) * head_dim : (4 + i) * head_dim]
        part = jnp.where(odd, odd_part.astype(f32), even_part.astype(f32)).astype(bf16)
        pad = jnp.zeros((window.shape[0], 128 - head_dim), bf16)
        weight[:, i * 128 : (i + 1) * 128] = jnp.concatenate([part, pad], axis=1)
    n_exp = lax.axis_size("exp")
    n_x = lax.axis_size("ctx") // 2
    ctx, exp = lax.axis_index("ctx"), lax.axis_index("exp")

    def piece_start(b, o, k):
        if b < 0:
            return 0
        x_at = lax.rem(ctx // 2 + (n_x - b), n_x)
        core = lax.rem(lax.rem(ctx, 2) + o, 2)
        return ((x_at * 2 + core) * n_exp + lax.rem(exp + (n_exp - k), n_exp)) * 128

    n_tiles, side, _ = tiles.shape
    length = sc[0]

    def rows_in(x, start):
        x = x.astype(f32)
        h1[pl.ds(start, 128), :] = (x * norm_scale(x) * row_of(gain)).astype(bf16)

    def project(j, carry):
        group = 512
        start = at_tile(j, group)
        lane = iota((group, 128), 1)
        here = pl.ds(start, group)
        qkv = dot(h1[here, :], weight[...], NN).astype(bf16).astype(f32)
        q, k, v = qkv[:, :128] * 0.125, qkv[:, 128:256], qkv[:, 256:]
        live = jnp.where(start + iota((group, 128), 0) < length, 0.0, NEG)
        qa[here, :] = jnp.where(lane == head_dim, 1.0, q).astype(bf16)
        ka[here, :] = jnp.where(lane == head_dim, live, k).astype(bf16)
        va[here, :] = v.astype(bf16)
        qt[:, here] = q.T[:head_dim].astype(bf16)
        kt[:, here] = k.T[:head_dim].astype(bf16)
        vt[:, here] = v.T[:head_dim].astype(bf16)
        return carry

    for i, piece in enumerate(pieces):
        if piece.shape[0] == 128:
            rows_in(piece[...], pl.multiple_of(piece_start(*shifts[i]), 128))
        else:

            def step(j, carry, piece=piece):
                start = pl.multiple_of(j * 128, 128)
                rows_in(piece[pl.ds(start, 128), :], start)
                return carry

            lax.fori_loop(0, piece.shape[0] // 128, step, 0)
    loop(h1.shape[0] // 512, project, 0)
    leave = [
        pltpu.make_async_copy(src, dst, sems.at[i])
        for i, (src, dst) in enumerate(zip((h1, qa, ka, va, qt, kt), kept))
    ]
    for copy in leave:
        copy.start()
    blocks = side // 128

    def one_query_tile(qi, carry):
        q_start = at_tile(qi, side)
        q = qa[pl.ds(q_start, side), :]

        def fold(k_start, offset, state, diagonal):
            top, total, acc = state
            scores = dot(ka[pl.ds(k_start, side), :], q, NT) + tiles[offset]
            if diagonal:
                scores = jnp.where(iota((side, side), 0) <= iota((side, side), 1), scores, NEG)
            new_top = jnp.maximum(top, jnp.max(scores, axis=0, keepdims=True))
            probs = jnp.exp(scores - new_top)
            scale = jnp.exp(top - new_top)
            total = total * scale + jnp.sum(probs, axis=0, keepdims=True)
            acc = acc * scale + dot(vt[:, pl.ds(k_start, side)], probs.astype(bf16), NN)
            return new_top, total, acc

        state = (
            jnp.full((1, side), NEG, f32),
            jnp.zeros((1, side), f32),
            jnp.zeros((head_dim, side), f32),
        )
        state = fold(q_start, 0, state, True)

        def earlier(kj, state):
            return fold(at_tile(kj, side), qi - kj, state, False)

        top, total, acc = loop(qi, earlier, state)
        result = (acc / total).astype(bf16)
        lse[:, pl.ds(q_start, side)] = top + jnp.log(total)
        for b in range(blocks):
            out_t[qi * blocks + b] = result[:, b * 128 : (b + 1) * 128]
        return carry

    loop(n_tiles, one_query_tile, 0)
    for copy in leave:
        copy.wait()


def attn_back_kernel(head_dim, n_dp, rel, *refs):
    qa, ka, va, qt, kt, out_t, grad_t, lse, h1_far, buckets, small = refs[:11]
    pay, weight_pay = refs[11:13]
    dq, dk, dv, full, brow, tiles, sums, diag, h1, sem = refs[13:]
    fetch = pltpu.make_async_copy(h1_far, h1, sem)
    fetch.start()
    n_tiles, side, _ = tiles.shape
    blocks = side // 128
    bias_tiles(rel, buckets, brow, tiles)
    sums[...] = jnp.zeros_like(sums)
    dk[...] = jnp.zeros_like(dk)
    dv[...] = jnp.zeros_like(dv)

    def one_query_tile(qi, carry):
        q_start = at_tile(qi, side)
        q = qa[pl.ds(q_start, side), :]
        q_t = qt[:, pl.ds(q_start, side)]
        g_t = jnp.concatenate([grad_t[qi * blocks + b] for b in range(blocks)], axis=1)
        o_t = jnp.concatenate([out_t[qi * blocks + b] for b in range(blocks)], axis=1)
        row_dots = jnp.sum(g_t.astype(f32) * o_t.astype(f32), axis=0, keepdims=True)
        norm = lse[:, pl.ds(q_start, side)]

        def fold(k_start, offset, acc, diagonal):
            where_k = pl.ds(k_start, side)
            scores = dot(ka[where_k, :], q, NT) + tiles[offset]
            probs = jnp.exp(scores - norm)
            if diagonal:
                probs = jnp.where(iota((side, side), 0) <= iota((side, side), 1), probs, 0.0)
            grad_prob = dot(va[where_k, :][:, :head_dim], g_t, NN)
            grad_score = probs * (grad_prob - row_dots)
            low = grad_score.astype(bf16)
            sums[offset] = sums[offset] + grad_score
            dv[:, where_k] = dv[:, where_k] + dot(g_t, probs.astype(bf16), NT)
            dk[:, where_k] = dk[:, where_k] + dot(q_t, low, NT)
            return acc + dot(kt[:, where_k], low, NN)

        acc = fold(q_start, 0, jnp.zeros((head_dim, side), f32), True)

        def earlier(kj, acc):
            return fold(at_tile(kj, side), qi - kj, acc, False)

        dq[:, pl.ds(q_start, side)] = loop(qi, earlier, acc)
        return carry

    loop(n_tiles, one_query_tile, 0)
    full[:head_dim, :] = (dq[...] * 0.125).astype(bf16)
    full[head_dim : 2 * head_dim, :] = dk[...].astype(bf16)
    full[2 * head_dim :, :] = dv[...].astype(bf16)
    for b in range(pay.shape[0]):
        pay[b] = full[:, b * 128 : (b + 1) * 128]
    flip = jnp.where(iota((128, 128), 0) + iota((128, 128), 1) == 127, 1.0, 0.0).astype(bf16)
    diag[...] = jnp.zeros_like(diag)
    for o in range(n_tiles):
        for a in range(blocks):
            turned = dot(flip, sums[o, a * 128 : (a + 1) * 128, :].astype(bf16), NN)
            wide = jnp.concatenate([turned, jnp.zeros((128, 128), f32)], axis=1)
            lined = pltpu.roll(wide, 0, axis=1, stride=1, stride_axis=0)
            first = (o + 1) * side - (a + 1) * 128
            where_d = slice(first, first + side + 128)
            diag[:, where_d] = diag[:, where_d] + jnp.sum(lined, axis=0, keepdims=True)
    ids = jnp.concatenate([buckets[...], jnp.full((1, side), -1, jnp.int32)], axis=1)
    ids = pltpu.roll(ids, side - 1, 1)
    hot = jnp.where(ids == iota((128, ids.shape[1]), 0), 1.0, 0.0).astype(bf16)
    high, low = split2(jnp.broadcast_to(diag[...], (8, diag.shape[1])))
    rel_grad = dot(high, hot, NT) + dot(low, hot, NT)
    fetch.wait()
    grad_w = dot(full[...], h1[...], NN).astype(bf16)
    n_pay, pay_rows, lanes = weight_pay.shape
    n_ctx = n_pay // n_dp
    rows = grad_w.shape[0] // n_ctx
    rel_row = jnp.concatenate([rel_grad, jnp.zeros((8, lanes - 128), f32)], axis=1)
    line = iota((16, lanes), 0)
    for d in range(n_dp):
        for c in range(n_ctx):
            here = slice(d * lanes, (d + 1) * lanes)
            weight_pay[d * n_ctx + c, :rows, :] = grad_w[c * rows : (c + 1) * rows, here]
            extra = jnp.where(line == 0, rel_row[0:1], 0.0)
            if c < 4:
                for r in range(2):
                    row = small[2 * c + r : 2 * c + r + 1, here]
                    extra = jnp.where(line == 8 + r, row, extra)
            weight_pay[d * n_ctx + c, rows:, :] = extra.astype(bf16)


def middle_kernel(n_heads, sc, recv, w_out, x, gain, pick, middle, *send):
    rows, width = x.shape
    attn_t = jnp.concatenate([recv[h] for h in range(n_heads)], axis=0)
    branch = dot(attn_t, w_out[...], TN)
    valid = iota((rows, 1), 0) < valid_rows(sc, rows)
    mid = x[...].astype(f32) + jnp.where(valid, branch, 0.0)
    middle[...] = mid
    h2 = (mid * norm_scale(mid) * row_of(gain)).astype(bf16)
    for k, piece in enumerate(send):
        expert = lax.rem(lax.axis_index("exp") + k, len(send))
        chosen = pick[pl.ds(pl.multiple_of(expert * CAP, 16), CAP), :]
        piece[...] = dot(chosen, h2, NN).astype(bf16)


def gate_of(h2, pay, width, w3, own):
    logits = dot(h2, w3, NN)
    sel = 2.0 * own - pay[:, width:].astype(f32)
    diff = jnp.sum(logits * sel, axis=1, keepdims=True)
    return 1.0 / (1.0 + jnp.exp(-diff)), sel


def own_lanes(expert, n_experts):
    lane = iota((1, 128), 1)
    return jnp.where((lane < 3 * n_experts) & (lane % n_experts == expert), 1.0, 0.0)


def expert_kernel(n_experts, h2, pay, w3, w3_t, w_up, w_down, *refs):
    mix, back = refs[:n_experts], refs[n_experts : 2 * n_experts]
    router, z_acc, in_acc, dz, gates, rows_out = refs[2 * n_experts :]
    step = pl.program_id(0)
    width = h2.shape[1]
    expert = lax.axis_index("exp")
    own = own_lanes(expert, n_experts)

    @pl.when(step == 0)
    def _():
        gate, _ = gate_of(h2[...], pay, width, w3[...], own)
        gates[...] = jnp.broadcast_to(gate, gates.shape)
        dz[...] = (gate * pay[:, :width].astype(f32)).astype(bf16)
        z_acc[...] = jnp.zeros_like(z_acc)
        in_acc[...] = jnp.zeros_like(in_acc)

    up = dot(h2[...], w_up[...], NN)
    act, slope = gelu_parts(up)
    grad_hidden = dot(dz[...], w_down[...], NT)
    grad_up = (grad_hidden * slope).astype(bf16)
    z_acc[...] += dot(act.astype(bf16), w_down[...], NN)
    in_acc[...] += dot(grad_up, w_up[...], NT)

    @pl.when(step == pl.num_programs(0) - 1)
    def _():
        gate = gates[:, 0:1]
        sel = 2.0 * own - pay[:, width:].astype(f32)
        z = z_acc[...].astype(bf16).astype(f32)
        rows_out[...] = (gate * z).astype(bf16)
        for k in range(n_experts):
            mix[k][...] = rows_out[k * CAP : (k + 1) * CAP, :]
        grad_gate = jnp.sum(pay[:, :width].astype(f32) * z, axis=1, keepdims=True)
        high, low = split2((gate * (1.0 - gate) * grad_gate) * sel)
        total = in_acc[...] + dot(high, w3_t[...], NN) + dot(low, w3_t[...], NN)
        rows_out[...] = total.astype(bf16)
        for k in range(n_experts):
            back[k][...] = rows_out[k * CAP : (k + 1) * CAP, :]
        router[...] = (dot(high, h2[...], TN) + dot(low, h2[...], TN))[:8]


def collect(pieces, pick):
    n_experts = len(pieces)
    total = None
    for k, piece in enumerate(pieces):
        expert = lax.rem(lax.axis_index("exp") + k, n_experts)
        chosen = pick[pl.ds(pl.multiple_of(expert * CAP, 16), CAP), :]
        part = dot(chosen, piece[...], TN)
        total = part if total is None else total + part
    return total


def middle_back_kernel(n_heads, n_experts, sc, *refs):
    back = refs[:n_experts]
    pick, middle, dy, gain, recv, w_out, router, dmid, grad_t, red, small = refs[n_experts:]
    rows, width = middle.shape
    grad_h2 = collect(back, pick)
    grad_in, xhat = norm_back(middle[...], row_of(gain), grad_h2)
    grad_mid = dy[...].astype(f32) + grad_in
    dmid[...] = grad_mid
    valid = iota((rows, 1), 0) < valid_rows(sc, rows)
    branch = jnp.where(valid, grad_mid, 0.0).astype(bf16)
    attn_t = jnp.concatenate([recv[h] for h in range(n_heads)], axis=0)
    heads = dot(w_out[...], branch, NT).astype(bf16)
    head_dim = width // n_heads
    for h in range(n_heads):
        grad_t[h] = heads[h * head_dim : (h + 1) * head_dim]
    for h in range(n_heads, grad_t.shape[0]):
        grad_t[h] = jnp.zeros((head_dim, rows), bf16)
    red[...] = dot(attn_t, branch, NN).astype(bf16)
    gains = jnp.sum(grad_h2 * xhat, axis=0, keepdims=True)
    line = iota((8, width), 0)
    moved = pltpu.roll(router[...], 1, 0)
    small[...] = jnp.where(line == 0, gains, jnp.where(line < 5, moved, 0.0))


def output_kernel(n_experts, sc, *refs):
    mix = refs[:n_experts]
    pick, middle, out = refs[n_experts:]
    rows = middle.shape[0]
    valid = iota((rows, 1), 0) < valid_rows(sc, rows)
    total = collect(mix, pick)
    out[...] = (middle[...] + jnp.where(valid, total, 0.0)).astype(bf16)


def token_grad_kernel(n_heads, recv, w_qkv, x, gain, dmid, out):
    grad_t = jnp.concatenate([recv[h] for h in range(n_heads)], axis=0)
    grad_h1 = dot(w_qkv[...], grad_t, NN).T
    grad_in, _ = norm_back(x[...].astype(f32), row_of(gain), grad_h1)
    out[...] = dmid[...] + grad_in


def load_rows(h_pieces, where, pays, h2, pay, sem):
    rows = h_pieces[0].shape[0]
    copies = []
    for i, piece in enumerate(h_pieces):
        here = pl.ds(i * rows, rows)
        source = pays[i] if len(pays) > 1 else pays[0].at[
            pl.ds(pl.multiple_of(where[i] * rows, 16), rows), :
        ]
        copies.append(pltpu.make_async_copy(piece, h2.at[here, :], sem.at[0, i]))
        copies.append(pltpu.make_async_copy(source, pay.at[here, :], sem.at[1, i]))
    return copies


def chip_index(a, b, o):
    n_dp = lax.axis_size("dp")
    n_x = lax.axis_size("ctx") // 2
    dp, ctx = lax.axis_index("dp"), lax.axis_index("ctx")
    core = lax.rem(lax.rem(ctx, 2) + o, 2)
    x_at = lax.rem(ctx // 2 + (n_x - b), n_x)
    return (lax.rem(dp + (n_dp - a), n_dp) * n_x + x_at) * 2 + core


def weight_grad_kernel(n_experts, keys, together, last, sc, *refs):
    n_pieces = len(keys)
    h_pieces = refs[:n_pieces]
    n_in = n_pieces + (1 if last else n_pieces)
    pays = refs[n_pieces:n_in]
    w3, w_up, w_down = refs[n_in : n_in + 3]
    if last:
        up_base, down_base, up_out, down_out, low = refs[n_in + 3 : n_in + 8]
    else:
        up_out, down_out = refs[n_in + 3 : n_in + 5]
    h2, pay, dz, hid_t, dup_t, sem = refs[-6:]
    step = pl.program_id(0)
    rows = h_pieces[0].shape[0]
    width = h2.shape[1]
    block = w_down.shape[0]
    copies = load_rows(h_pieces, [chip_index(*key) for key in keys], pays, h2, pay, sem)

    @pl.when(step == 0)
    def _():
        for copy in copies:
            copy.start()

    own = own_lanes(lax.axis_index("exp"), n_experts)
    up_t = w_up[...].T
    down = w_down[...]
    chunk = together * rows
    for i in range(n_pieces // together):
        here = slice(i * chunk, (i + 1) * chunk)

        @pl.when(step == 0)
        def _(i=i, here=here):
            for copy in copies[2 * together * i : 2 * together * (i + 1)]:
                copy.wait()
            part = pay[here, :]
            gate, _ = gate_of(h2[here, :], part, width, w3[...], own)
            dz[here, :] = (gate * part[:, :width].astype(f32)).astype(bf16)

        act, slope = gelu_parts(dot(up_t, h2[here, :], NT))
        hid_t[:, here] = act.astype(bf16)
        dup_t[:, here] = (dot(down, dz[here, :], NT) * slope).astype(bf16)
    grad_up = dot(dup_t[...], h2[...], NN)
    grad_down = dot(hid_t[...], dz[...], NN)
    if last:
        grad_up = grad_up + up_base[...]
        grad_down = grad_down + down_base[...]
        low[:block, :] = grad_up.astype(bf16)
        low[block:, :] = grad_down.astype(bf16)
        up_out[...] = grad_up.T
    else:
        up_out[...] = grad_up
    down_out[...] = grad_down


def fill_kernel(sc, low, *refs):
    up_out, down_out = refs[-2:]
    block = down_out.shape[0]
    up_out[...] = low[:block, :].astype(f32).T
    down_out[...] = low[block:, :].astype(f32)


def assemble_kernel(keys, rows, n_groups, head_cols, *refs):
    n_pieces = len(keys)
    pieces = refs[:n_pieces]
    w_qkv, gain, grad, gain_grad, rel_grad, gain2_grad, router_grad = refs[
        n_pieces : n_pieces + 7
    ]
    turned, rel_t, stage, acc, sem = refs[n_pieces + 7 :]
    lanes = pieces[0].shape[-1]
    acc[...] = jnp.zeros_like(acc)
    n_dp, n_exp = lax.axis_size("dp"), lax.axis_size("exp")
    n_x = lax.axis_size("ctx") // 2
    dp, ctx, exp = (lax.axis_index(name) for name in ("dp", "ctx", "exp"))
    rel_t[...] = jnp.zeros_like(rel_t)
    for piece, ids in zip(pieces, keys):
        for i, (a, b, o, k) in enumerate(ids):
            d = lax.rem(dp + (n_dp - a), n_dp)
            c = lax.rem(ctx // 2 + (n_x - b), n_x) * 2 + lax.rem(lax.rem(ctx, 2) + o, 2)
            e = lax.rem(exp + (n_exp - k), n_exp)
            lane_at = pl.multiple_of(d * lanes, 128)
            for g in range(n_groups):
                head = g * n_exp + e
                row_at = pl.multiple_of(head * head_cols + c * rows, 16)
                turned[pl.ds(row_at, rows), pl.ds(lane_at, lanes)] = piece[
                    i, g * rows : (g + 1) * rows, :
                ]
                rel_t[pl.ds(head, 1), :] = piece[
                    i, n_groups * rows + g : n_groups * rows + g + 1, :128
                ].astype(f32)
            first = n_groups * rows + 8
            where_s = pl.ds(lane_at, lanes)
            small = piece[i, first : first + 8, :].astype(f32)
            acc[c, :, where_s] = acc[c, :, where_s] + small
    rel_grad[...] = rel_t[: rel_grad.shape[0], : rel_grad.shape[1]]
    width, columns = grad.shape
    gain2_grad[...] = acc[0, 0:1, :].reshape(width)
    for e in range(router_grad.shape[0]):
        router_grad[e : e + 1, :] = acc[(e + 1) // 2, (e + 1) % 2 : (e + 1) % 2 + 1, :]
    copies = []
    for i, a in enumerate(range(0, width, 128)):
        total = jnp.zeros((128, 128), f32)
        for b in range(0, columns, 128):
            tile = turned[b : b + 128, a : a + 128].astype(f32).T
            stage[a : a + 128, b : b + 128] = tile
            total = total + tile * w_qkv[a : a + 128, b : b + 128].astype(f32)
        where_a = pl.ds(a, 128)
        copy = pltpu.make_async_copy(stage.at[where_a, :], grad.at[where_a, :], sem.at[i])
        copy.start()
        copies.append(copy)
        sums = jnp.sum(total.T, axis=0, keepdims=True)
        sums = sums / gain[a : a + 128].reshape(1, 128)
        gain_grad[a : a + 128] = sums.reshape(128)
    for copy in copies:
        copy.wait()


def shard_kernel(n_dp, n_groups, summed, shard):
    n_ctx = summed.shape[0] // n_dp
    part = summed.shape[1] - 16
    line = iota((16, summed.shape[2]), 0)
    extra = jnp.zeros(line.shape, f32)
    for i in range(summed.shape[0]):
        extra = extra + summed[i, part:, :].astype(f32)
    extra = jnp.where(line >= 8, extra, 0.0)
    for g in range(n_groups):
        total = summed[g].astype(f32)
        for d in range(1, n_dp):
            total = total + summed[d * n_ctx + g].astype(f32)
        shard[0, g * part : (g + 1) * part, :] = total[:part].astype(bf16)
        extra = jnp.where(line == g, total[part : part + 1], extra)
    shard[0, n_groups * part :, :] = extra.astype(bf16)


def reduced_kernel(red, attn_out):
    attn_out[...] = red[...].astype(f32)


def after(value, *others):
    return lax.optimization_barrier((value, others))[0]


def on_device(
    n_dp,
    n_ctx,
    n_exp,
    tokens,
    lengths,
    routes,
    buckets,
    cotangent,
    attn_gain,
    w_qkv,
    w_attn_out,
    rel_bias,
    ffn_gain,
    w_router,
    w_up,
    w_down,
):
    x = tokens[0]
    dy = cotangent[0]
    rows, width = x.shape
    seq = buckets.shape[0]
    n_buckets, n_heads = rel_bias.shape
    head_dim = width // n_heads
    n_experts = w_router.shape[1]
    ff = w_up.shape[2]
    n_slot = n_ctx * n_exp
    n_groups = n_heads // n_exp
    n_x = n_ctx // 2
    small = n_x == 2 and n_dp == 2
    side = 512 if seq <= 2048 else 256
    n_tiles = seq // side
    slot_rows = n_experts * CAP
    slot_axes, all_chips = ("ctx", "exp"), ("dp", "ctx")

    def ring(v, shift):
        return lax.ppermute(v, "exp", [(i, (i + shift) % n_exp) for i in range(n_exp)])

    def swap(v):
        return lax.ppermute(v, "ctx", [(i, i ^ 1) for i in range(n_ctx)])

    def chips(v, a, b):
        perm = []
        for d in range(n_dp):
            for c in range(n_ctx):
                to = ((d + a) % n_dp) * n_ctx + ((c // 2 + b) % n_x) * 2 + c % 2
                perm.append((d * n_ctx + c, to))
        return lax.ppermute(v, all_chips, perm)

    def exchange(v, axes):
        return lax.all_to_all(v, axes, split_axis=0, concat_axis=0, tiled=True)

    def to_experts(parts):
        return [parts[0]] + [ring(parts[k], k) for k in range(1, n_exp)]

    def from_experts(parts):
        return [parts[0]] + [ring(parts[k], n_exp - k) for k in range(1, n_exp)]

    keys = [(a, b, o) for o in (0, 1) for a, b in ((0, 0), (0, 1), (1, 0), (1, 1))]

    with jax.named_scope("routing"):
        places, pick, w3, w3_t, _, *pay = call(
            functools.partial(route_kernel, n_experts),
            [
                sds((1,), jnp.int32),
                sds((slot_rows, rows), bf16),
                sds((width, 128), bf16),
                sds((128, width), bf16),
                sds((slot_rows, width + 128), bf16),
            ]
            + [sds((CAP, width + 128), bf16)] * n_experts,
            [smem()] + [vmem()] * 3,
            name="routing",
        )(lengths, routes[0].T, dy, w_router.T)

    with jax.named_scope("gather_tokens"):
        if small:
            column = [(x, 0, 0), (ring(after(x, pick), 1), 0, 1)]
            column += [(ring(x, k), 0, k) for k in range(2, n_exp)]
            onward = [v for v, _, _ in column]
            onward[-1] = after(onward[-1], pay)
            pieces = column + [(chips(v, 0, 1), 1, k) for k, v in enumerate(onward)]
            pieces = [(v, b, 0, k) for v, b, k in pieces]
            arrived = to_experts(after(pay, pieces[-1][0]))
            pieces = pieces + [(swap(v), b, 1, k) for v, b, _, k in pieces]
            blocks = [v for v, _, _, _ in pieces]
            shifts = [ids for _, *ids in pieces]
        else:
            blocks = [lax.all_gather(x, slot_axes, axis=0, tiled=True)]
            shifts = [(-1, 0, 0)]
            arrived = to_experts(pay)

    with jax.named_scope("attention"):
        bucket_row = buckets.reshape(1, seq)
        blocks[-1] = after(blocks[-1], bucket_row)
        attn_outs = (
            sds((seq, width), bf16),
            sds((seq, 128), bf16),
            sds((seq, 128), bf16),
            sds((seq, 128), bf16),
            sds((head_dim, seq), bf16),
            sds((head_dim, seq), bf16),
            sds((n_slot, head_dim, 128), bf16),
            sds((1, seq), f32),
        )
        any_spec = pl.BlockSpec(memory_space=pl.ANY)
        h1, qa, ka, va, qt, kt, out_t, lse = call(
            functools.partial(attn_kernel, shifts, head_dim),
            attn_outs,
            [smem(), smem()] + [vmem()] * (len(blocks) + 1) + [any_spec, vmem()],
            [pltpu.VMEM(o.shape, o.dtype) for o in attn_outs[:6]]
            + [
                pltpu.VMEM((head_dim, seq), bf16),
                pltpu.VMEM((1, seq + side), f32),
                pltpu.VMEM((n_tiles, side, side), f32),
                pltpu.VMEM((width, 6 * head_dim), bf16),
                pltpu.VMEM((width, 384), bf16),
                pltpu.SemaphoreType.DMA,
                pltpu.SemaphoreType.DMA((6,)),
            ],
            micros=10,
            name="attention",
            limit=58,
            out_specs=(any_spec,) * 6 + (vmem(),) * 2,
        )(lengths, rel_bias.T, *blocks, attn_gain, w_qkv, bucket_row)
        attn_in = exchange(out_t, slot_axes)
        pay_in = jnp.concatenate([arrived[0]] + [after(v, out_t) for v in arrived[1:]])

    with jax.named_scope("middle"):
        piece_shape = sds((CAP, width), bf16)
        middle, *send = call(
            functools.partial(middle_kernel, n_heads),
            [sds((rows, width), f32)] + [piece_shape] * n_experts,
            [smem()] + [vmem()] * 5,
            name="middle",
        )(lengths, attn_in, w_attn_out, x, ffn_gain, pick)
        h2_in = jnp.concatenate(to_experts(send))

    with jax.named_scope("experts"):
        block = 1024
        row_spec = pl.BlockSpec((slot_rows, width), lambda i: (0, 0))
        piece_spec = pl.BlockSpec((CAP, width), lambda i: (0, 0))
        *parts, router = pl.pallas_call(
            functools.partial(expert_kernel, n_experts),
            out_shape=[piece_shape] * (2 * n_experts)
            + [sds((8, width), f32)],
            grid_spec=pltpu.PrefetchScalarGridSpec(
                num_scalar_prefetch=0,
                grid=(ff // block,),
                in_specs=[
                    row_spec,
                    pl.BlockSpec((slot_rows, width + 128), lambda i: (0, 0)),
                    pl.BlockSpec((width, 128), lambda i: (0, 0)),
                    pl.BlockSpec((128, width), lambda i: (0, 0)),
                    pl.BlockSpec((width, block), lambda i: (0, i)),
                    pl.BlockSpec((block, width), lambda i: (i, 0)),
                ],
                out_specs=[piece_spec] * (2 * n_experts)
                + [pl.BlockSpec((8, width), lambda i: (0, 0))],
                scratch_shapes=[
                    pltpu.VMEM((slot_rows, width), f32),
                    pltpu.VMEM((slot_rows, width), f32),
                    pltpu.VMEM((slot_rows, width), bf16),
                    pltpu.VMEM((slot_rows, 128), f32),
                    pltpu.VMEM((slot_rows, width), bf16),
                ],
            ),
            compiler_params=params(),
            cost_estimate=cost_of(12),
            name="experts",
        )(h2_in, pay_in, w3, w3_t, w_up[0], w_down[0])
        mix_parts, back_parts = parts[:n_experts], parts[n_experts:]
        back_in = from_experts(back_parts)

    shares = n_dp * n_ctx
    with jax.named_scope("expert_weight_grads"):
        if small:
            pay_all = lax.all_gather(pay_in, all_chips, axis=0, tiled=True)
            beside = [chips(h2_in, a, b) for a, b in ((0, 1), (1, 0), (1, 1))]
            block = 512
            n_parts = ff // (2 * block)
            full_shapes = [sds((width, ff), f32), sds((ff, width), f32)]

            def half_specs(other):
                def at(i, s):
                    return (1 - s[0] if other else s[0]) * n_parts + i

                return (
                    pl.BlockSpec((width, block), lambda i, s: (0, at(i, s))),
                    pl.BlockSpec((block, width), lambda i, s: (at(i, s), 0)),
                )

            low_spec = pl.BlockSpec((2 * block, width), lambda i, s: (i, 0))

            base_spec = pl.BlockSpec((block, width), lambda i, s: (i, 0))
            base_shape = sds((ff // 2, width), f32)

            def weight_half(pieces, pays, keys, base, micros):
                specs = half_specs(False)
                count = len(pieces) * slot_rows
                shapes, outs = [base_shape] * 2, [base_spec] * 2
                if base:
                    shapes, outs = full_shapes + [sds((ff, width), bf16)], [*specs, low_spec]
                return pl.pallas_call(
                    functools.partial(weight_grad_kernel, n_experts, keys, 2, bool(base)),
                    out_shape=shapes,
                    grid_spec=pltpu.PrefetchScalarGridSpec(
                        num_scalar_prefetch=1,
                        grid=(n_parts,),
                        in_specs=[any_spec] * (len(pieces) + len(pays))
                        + [pl.BlockSpec((width, 128), lambda i, s: (0, 0)), *specs]
                        + [base_spec] * len(base),
                        out_specs=outs,
                        scratch_shapes=[
                            pltpu.VMEM((count, width), bf16),
                            pltpu.VMEM((count, width + 128), bf16),
                            pltpu.VMEM((count, width), bf16),
                            pltpu.VMEM((block, count), bf16),
                            pltpu.VMEM((block, count), bf16),
                            pltpu.SemaphoreType.DMA((2, len(pieces))),
                        ],
                    ),
                    compiler_params=params(),
                    cost_estimate=cost_of(micros),
                    name="weight_grads",
                )(places, *pieces, *pays, w3, w_up[0], w_down[0], *base)

            def weight_fill(low, grads):
                return pl.pallas_call(
                    fill_kernel,
                    out_shape=full_shapes,
                    grid_spec=pltpu.PrefetchScalarGridSpec(
                        num_scalar_prefetch=1,
                        grid=(n_parts,),
                        in_specs=[low_spec, any_spec, any_spec],
                        out_specs=half_specs(True),
                    ),
                    input_output_aliases={2: 0, 3: 1},
                    compiler_params=params(),
                    cost_estimate=cost_of(8),
                    name="fill",
                )(places, low, *grads)


            pays = [pay_in, swap(pay_in)]
            base = weight_half([h2_in, swap(h2_in)], pays, keys[::4], (), 11)
            back_in[0] = after(back_in[0], beside, base, pay_all)

    with jax.named_scope("middle_back"):
        dmid, grad_t, red, sums = call(
            functools.partial(middle_back_kernel, n_heads, n_experts),
            (
                sds((rows, width), f32),
                sds((n_slot, head_dim, rows), bf16),
                sds((width, width), bf16),
                sds((8, width), f32),
            ),
            [smem()] + [vmem()] * (7 + n_experts),
            name="middle_back",
        )(lengths, *back_in, pick, middle, dy, ffn_gain, attn_in, w_attn_out, router)
        grad_in = exchange(grad_t, slot_axes)

    if small:
        with jax.named_scope("expert_weight_grads"):
            beside = [after(v, grad_t) for v in beside]
            pieces = beside + [swap(v) for v in beside]
            *grads, low = weight_half(pieces, [pay_all], keys[1:4] + keys[5:], base, 8)
            share = lax.psum_scatter(red, all_chips, scatter_dimension=0, tiled=True)
            grad_in = after(grad_in, low, share)
            others = [ring(share, k) for k in range(1, n_exp)]

    with jax.named_scope("attention_back"):
        part = 3 * head_dim // n_ctx
        lanes = width // n_dp
        dqkv, weight_pay = call(
            functools.partial(attn_back_kernel, head_dim, n_dp),
            (sds((n_slot, 3 * head_dim, rows), bf16), sds((shares, part + 16, lanes), bf16)),
            [smem()] + [vmem()] * 8 + [any_spec, vmem(), vmem()],
            [
                pltpu.VMEM((head_dim, seq), f32),
                pltpu.VMEM((head_dim, seq), f32),
                pltpu.VMEM((head_dim, seq), f32),
                pltpu.VMEM((3 * head_dim, seq), bf16),
                pltpu.VMEM((1, seq + side), f32),
                pltpu.VMEM((n_tiles, side, side), f32),
                pltpu.VMEM((n_tiles, side, side), f32),
                pltpu.VMEM((1, seq + side), f32),
                pltpu.VMEM((seq, width), bf16),
                pltpu.SemaphoreType.DMA,
            ],
            micros=11,
            name="attention_back",
            limit=58,
        )(rel_bias.T, qa, ka, va, qt, kt, out_t, grad_in, lse, h1, bucket_row, sums)
        if small:
            weight_pay = after(weight_pay, others)
            share = share.astype(f32) + others[0] + others[1] + others[2]
            share = after(share, weight_pay).astype(bf16)
        else:
            mix_in = from_experts(mix_parts)
        summed = exchange(weight_pay, all_chips)
        if small:
            summed = after(summed, share)

    with jax.named_scope("projection_grad"):
        shard = call(
            functools.partial(shard_kernel, n_dp, n_groups),
            sds((1, n_groups * part + 16, lanes), bf16),
            [vmem()],
            name="shard",
        )(summed)
        if small:
            column = [ring(shard, k) for k in range(1, n_exp)]
            column = jnp.concatenate([shard] + column)
            low_in = swap(after(low, weight_pay))
            column = after(column, low_in)
            dqkv = after(dqkv, column)
            mix_in = from_experts([after(v, column) for v in mix_parts])


    if small:
        with jax.named_scope("expert_weight_grads"):
            grad_up, grad_down = weight_fill(low_in, grads)
    else:
        with jax.named_scope("expert_weight_grads"):
            own = own_lanes(lax.axis_index("exp"), n_experts)
            gate, _ = gate_of(h2_in, pay_in, width, w3, own)
            dz = (gate * pay_in[:, :width].astype(f32)).astype(bf16)
            act, slope = gelu_parts(dot(h2_in, w_up[0], NN))
            dup = (dot(dz, w_down[0], NT) * slope).astype(bf16)
            grad_up = lax.psum(dot(h2_in, dup, TN).astype(bf16), all_chips).astype(f32)
            grad_down = lax.psum(dot(act.astype(bf16), dz, TN).astype(bf16), all_chips)
            grad_down = grad_down.astype(f32)

    with jax.named_scope("output"):
        output = call(
            functools.partial(output_kernel, n_experts),
            sds((rows, width), bf16),
            [smem()] + [vmem()] * (2 + n_experts),
            micros=0.2,
            name="output",
        )(lengths, *mix_in, pick, middle)

    with jax.named_scope("token_grads"):
        dqkv_in = exchange(dqkv, slot_axes)
        grad_tokens = call(
            functools.partial(token_grad_kernel, n_heads),
            sds((rows, width), f32),
            [vmem()] * 5,
            name="token_grads",
        )(dqkv_in, w_qkv, x, attn_gain, dmid)

    with jax.named_scope("output_projection_grad"):
        if small:
            reduced = lax.all_gather(share, all_chips, axis=0, tiled=True)
        else:
            reduced = lax.psum(red, ("dp", "ctx", "exp"))
            sums = lax.psum(sums, ("dp", "ctx", "exp"))
            grad_ffn_gain, grad_router = sums[0], sums[1 : 1 + n_experts].T
        grad_attn_out = call(
            reduced_kernel,
            sds((width, width), f32),
            [vmem()],
            micros=0.2,
            name="reduced",
        )(reduced)

    with jax.named_scope("projection_grad"):
        if small:
            wide = [(column, 0, 0, range(n_exp))]
            for v, a, b in ((column, 0, 1), (column, 1, 0)):
                wide.append((chips(v, a, b), a, b, range(n_exp)))
            wide.append((chips(wide[1][0], 1, 0), 1, 1, range(n_exp)))
            early = (grad_tokens, grad_up, grad_down, grad_attn_out, mix_in)
            wide = [(after(v, early), a, b, ks) for v, a, b, ks in wide]
            final = [v for v, _, _, _ in wide] + [swap(v) for v, _, _, _ in wide]
            keys = [[(a, b, o, k) for k in ks] for o in (0, 1) for _, a, b, ks in wide]
            grad_qkv, grad_attn_gain, grad_rel, grad_ffn_gain, grad_router = call(
                functools.partial(assemble_kernel, keys, part, n_groups, 3 * head_dim),
                (
                    sds((width, 3 * width), f32),
                    sds((width,), f32),
                    sds((n_heads, n_buckets), f32),
                    sds((width,), f32),
                    sds((n_experts, width), f32),
                ),
                [vmem()] * (len(final) + 2),
                [
                    pltpu.VMEM((3 * width, width), bf16),
                    pltpu.VMEM((128, 128), f32),
                    pltpu.VMEM((width, 3 * width), f32),
                    pltpu.VMEM((n_ctx, 8, width), f32),
                    pltpu.SemaphoreType.DMA((width // 128,)),
                ],
                micros=6,
                name="assemble",
                limit=32,
                out_specs=(any_spec,) + (vmem(),) * 4,
            )(*final, w_qkv, attn_gain)
            grad_rel, grad_router = grad_rel.T, grad_router.T
        else:
            every = lax.all_gather(shard[0], ("dp", "ctx", "exp"), axis=0, tiled=False)
            every = every.reshape(n_dp, n_ctx, n_exp, n_groups * part + 16, lanes).astype(f32)
            main = every[:, :, :, : n_groups * part]
            main = main.reshape(n_dp, n_ctx, n_exp, n_groups, part, lanes)
            grad_qkv = main.transpose(0, 5, 3, 2, 1, 4).reshape(width, 3 * width)
            rel_rows = every[0, 0, :, n_groups * part : n_groups * (part + 1), :n_buckets]
            grad_rel = rel_rows.transpose(2, 1, 0).reshape(n_buckets, n_heads)
            grad_attn_gain = jnp.sum(grad_qkv * w_qkv.astype(f32), axis=1) / attn_gain

    return (
        output[None],
        grad_tokens[None],
        grad_attn_gain,
        grad_qkv,
        grad_attn_out,
        grad_rel,
        grad_ffn_gain,
        grad_router,
        grad_up[None],
        grad_down[None],
    )


def solution(mesh):
    sizes = dict(mesh.shape)
    by_token = P("dp", ("ctx", "exp"), None)
    by_expert = P("exp", None, None)
    return jax.shard_map(
        functools.partial(on_device, sizes["dp"], sizes["ctx"], sizes["exp"]),
        mesh=mesh,
        in_specs=(
            by_token,
            P("dp"),
            by_token,
            P(),
            by_token,
            P(),
            P(),
            P(),
            P(),
            P(),
            P(),
            by_expert,
            by_expert,
        ),
        out_specs=(
            by_token,
            by_token,
            P(),
            P(),
            P(),
            P(),
            P(),
            P(),
            by_expert,
            by_expert,
        ),
        check_vma=False,
    )
```

```python
import functools

import jax
import jax.numpy as jnp
from jax import lax
from jax.experimental import pallas as pl
from jax.experimental.pallas import tpu as pltpu
from jax.sharding import PartitionSpec as P

CAP = 80
EPS = 1e-06
NEG = -1e30
VMEM_LIMIT = 58 << 20
bf16 = jnp.bfloat16
f32 = jnp.float32
NN = ((1,), (0,))
NT = ((1,), (1,))
TN = ((0,), (0,))
GELU_C = 0.7978845608028654
GELU_A = 0.044715


def dot(left, right, dims):
    return lax.dot_general(left, right, (dims, ((), ())), preferred_element_type=f32)


def iota(shape, axis):
    return lax.broadcasted_iota(jnp.int32, shape, axis)


def norm_scale(values):
    return lax.rsqrt(jnp.mean(values * values, axis=-1, keepdims=True) + EPS)


def row_of(ref):
    return ref[...].reshape(1, ref.shape[0])


def norm_back(values, gain, grad):
    scale = norm_scale(values)
    xhat = values * scale
    gxhat = grad * gain
    grad_in = scale * (gxhat - xhat * jnp.mean(gxhat * xhat, axis=-1, keepdims=True))
    return grad_in, xhat


def gelu_parts(u):
    square = u * u
    t = jnp.tanh(u * (GELU_C + (GELU_C * GELU_A) * square))
    half = 0.5 * (1.0 + t)
    slope = half + (0.5 * u) * (1.0 - t * t) * (GELU_C + (3.0 * GELU_C * GELU_A) * square)
    return u * half, slope


def split2(values):
    high = values.astype(bf16)
    return high, (values - high.astype(f32)).astype(bf16)


def params(limit=VMEM_LIMIT):
    return pltpu.CompilerParams(vmem_limit_bytes=limit)


def vmem():
    return pl.BlockSpec(memory_space=pltpu.VMEM)


def smem():
    return pl.BlockSpec(memory_space=pltpu.SMEM)


def cost_of(micros):
    return pl.CostEstimate(
        flops=int(micros * 1e9), bytes_accessed=int(micros * 1e5), transcendentals=0
    )


def call(kernel, outs, ins, scratch=(), micros=3, name=None, limit=24, out_specs=None):
    return pl.pallas_call(
        kernel,
        out_shape=outs,
        in_specs=ins,
        out_specs=out_specs
        or jax.tree.map(lambda o: smem() if o.dtype == jnp.int32 else vmem(), outs),
        scratch_shapes=list(scratch),
        compiler_params=params(limit << 20),
        cost_estimate=cost_of(micros),
        name=name,
    )


def sds(shape, dtype):
    return jax.ShapeDtypeStruct(shape, dtype)


def valid_rows(lengths, rows):
    index = lax.axis_index("ctx") * lax.axis_size("exp") + lax.axis_index("exp")
    return lengths[0] - index * rows


def route_kernel(n_experts, sc, routes_t, dy, router_t, places, pick, w3, w3_t, full, *pay):
    places[0] = lax.rem(lax.axis_index("ctx"), 2)
    rows = dy.shape[0]
    width = dy.shape[1]
    table = jnp.concatenate(
        [router_t[...], jnp.zeros((128 - n_experts, width), f32)], axis=0
    )
    high = table.astype(bf16).astype(f32)
    mid = (table - high).astype(bf16).astype(f32)
    low = table - high - mid
    table = high + pltpu.roll(mid, n_experts, 0) + pltpu.roll(low, 2 * n_experts, 0)
    w3_t[...] = table.astype(bf16)
    w3[...] = table.T.astype(bf16)
    first, second = routes_t[0:1, :], routes_t[1:2, :]
    eight = iota((8, rows), 0)
    named = jnp.where((first == eight) | (second == eight), 1.0, 0.0)
    upper = jnp.where(iota((rows, rows), 0) < iota((rows, rows), 1), 1.0, 0.0)
    rank = dot(named.astype(bf16), upper.astype(bf16), NN)
    slot = iota((CAP, rows), 0).astype(f32)
    for e in range(n_experts):
        hit = (named[e : e + 1] > 0.5) & (rank[e : e + 1] == slot)
        pick[e * CAP : (e + 1) * CAP, :] = jnp.where(hit, 1.0, 0.0).astype(bf16)
    all_pick = pick[...].astype(f32)
    valid = iota((1, rows), 1) < valid_rows(sc, rows)
    live = jnp.where(valid, all_pick, 0.0).astype(bf16)
    full[:, :width] = dot(live, dy[...], NN).astype(bf16)
    line = iota((128, rows), 0)
    kind = jnp.where(line < 3 * n_experts, lax.rem(line, n_experts), -1)
    pair = jnp.where((first == kind) | (second == kind), 1.0, 0.0).astype(bf16)
    full[:, width:] = dot(pick[...], pair, NT).astype(bf16)
    for k, piece in enumerate(pay):
        expert = lax.rem(lax.axis_index("exp") + k, n_experts)
        piece[...] = full[pl.ds(pl.multiple_of(expert * CAP, 16), CAP), :]


def head_index(n_heads):
    index = lax.axis_index("ctx") * lax.axis_size("exp") + lax.axis_index("exp")
    return lax.rem(index, n_heads)


def bias_tiles(rel, buckets, brow, tiles):
    n_tiles, side, _ = tiles.shape
    n_heads, n_buckets = rel.shape
    head = head_index(n_heads)
    ids = buckets[...]
    row = jnp.zeros(ids.shape, f32)
    for b in range(n_buckets):
        row = jnp.where(ids == b, rel[head, b], row)
    brow[:, :side] = jnp.zeros((1, side), f32)
    brow[:, side:] = row
    for o in range(n_tiles):
        wide = jnp.broadcast_to(brow[:, o * side : (o + 2) * side], (side, 2 * side))
        tiles[o] = pltpu.roll(wide, 0, axis=1, stride=1, stride_axis=0)[:, side:]


def at_tile(index, side):
    return index * side if isinstance(index, int) else pl.multiple_of(index * side, side)


def loop(count, body, state):
    if isinstance(count, int) and count <= 4:
        for i in range(count):
            state = body(i, state)
        return state
    return lax.fori_loop(0, count, body, state)


def attn_kernel(shifts, head_dim, sc, rel, *refs):
    n_pieces = len(shifts)
    pieces = refs[:n_pieces]
    gain, w_qkv, buckets = refs[n_pieces : n_pieces + 3]
    kept, (out_t, lse) = refs[n_pieces + 3 : n_pieces + 9], refs[n_pieces + 9 : n_pieces + 11]
    h1, qa, ka, va, qt, kt, vt, brow, tiles, window, weight, sem, sems = refs[n_pieces + 11 :]
    head = head_index(rel.shape[0])
    pair_at = pl.multiple_of((head // 2) * 6 * head_dim, 128)
    fetch = pltpu.make_async_copy(w_qkv.at[:, pl.ds(pair_at, 6 * head_dim)], window, sem)
    fetch.start()
    bias_tiles(rel, buckets, brow, tiles)
    fetch.wait()
    odd = lax.rem(head, 2) == 1
    for i in range(3):
        even_part = window[:, i * head_dim : (i + 1) * head_dim]
        odd_part = window[:, (3 + i) * head_dim : (4 + i) * head_dim]
        part = jnp.where(odd, odd_part.astype(f32), even_part.astype(f32)).astype(bf16)
        pad = jnp.zeros((window.shape[0], 128 - head_dim), bf16)
        weight[:, i * 128 : (i + 1) * 128] = jnp.concatenate([part, pad], axis=1)
    n_exp = lax.axis_size("exp")
    n_x = lax.axis_size("ctx") // 2
    ctx, exp = lax.axis_index("ctx"), lax.axis_index("exp")

    def piece_start(b, o, k):
        if b < 0:
            return 0
        x_at = lax.rem(ctx // 2 + (n_x - b), n_x)
        core = lax.rem(lax.rem(ctx, 2) + o, 2)
        return ((x_at * 2 + core) * n_exp + lax.rem(exp + (n_exp - k), n_exp)) * 128

    n_tiles, side, _ = tiles.shape
    length = sc[0]

    def rows_in(x, start):
        x = x.astype(f32)
        h1[pl.ds(start, 128), :] = (x * norm_scale(x) * row_of(gain)).astype(bf16)

    def project(j, carry):
        group = 512
        start = at_tile(j, group)
        lane = iota((group, 128), 1)
        here = pl.ds(start, group)
        qkv = dot(h1[here, :], weight[...], NN).astype(bf16).astype(f32)
        q, k, v = qkv[:, :128] * 0.125, qkv[:, 128:256], qkv[:, 256:]
        live = jnp.where(start + iota((group, 128), 0) < length, 0.0, NEG)
        qa[here, :] = jnp.where(lane == head_dim, 1.0, q).astype(bf16)
        ka[here, :] = jnp.where(lane == head_dim, live, k).astype(bf16)
        va[here, :] = v.astype(bf16)
        qt[:, here] = q.T[:head_dim].astype(bf16)
        kt[:, here] = k.T[:head_dim].astype(bf16)
        vt[:, here] = v.T[:head_dim].astype(bf16)
        return carry

    for i, piece in enumerate(pieces):
        if piece.shape[0] == 128:
            rows_in(piece[...], pl.multiple_of(piece_start(*shifts[i]), 128))
        else:

            def step(j, carry, piece=piece):
                start = pl.multiple_of(j * 128, 128)
                rows_in(piece[pl.ds(start, 128), :], start)
                return carry

            lax.fori_loop(0, piece.shape[0] // 128, step, 0)
    loop(h1.shape[0] // 512, project, 0)
    leave = [
        pltpu.make_async_copy(src, dst, sems.at[i])
        for i, (src, dst) in enumerate(zip((h1, qa, ka, va, qt, kt), kept))
    ]
    for copy in leave:
        copy.start()
    blocks = side // 128

    def one_query_tile(qi, carry):
        q_start = at_tile(qi, side)
        q = qa[pl.ds(q_start, side), :]

        def fold(k_start, offset, state, diagonal):
            top, total, acc = state
            scores = dot(ka[pl.ds(k_start, side), :], q, NT) + tiles[offset]
            if diagonal:
                scores = jnp.where(iota((side, side), 0) <= iota((side, side), 1), scores, NEG)
            new_top = jnp.maximum(top, jnp.max(scores, axis=0, keepdims=True))
            probs = jnp.exp(scores - new_top)
            scale = jnp.exp(top - new_top)
            total = total * scale + jnp.sum(probs, axis=0, keepdims=True)
            acc = acc * scale + dot(vt[:, pl.ds(k_start, side)], probs.astype(bf16), NN)
            return new_top, total, acc

        state = (
            jnp.full((1, side), NEG, f32),
            jnp.zeros((1, side), f32),
            jnp.zeros((head_dim, side), f32),
        )
        state = fold(q_start, 0, state, True)

        def earlier(kj, state):
            return fold(at_tile(kj, side), qi - kj, state, False)

        top, total, acc = loop(qi, earlier, state)
        result = (acc / total).astype(bf16)
        lse[:, pl.ds(q_start, side)] = top + jnp.log(total)
        for b in range(blocks):
            out_t[qi * blocks + b] = result[:, b * 128 : (b + 1) * 128]
        return carry

    loop(n_tiles, one_query_tile, 0)
    for copy in leave:
        copy.wait()


def attn_back_kernel(head_dim, n_dp, rel, *refs):
    qa, ka, va, qt, kt, out_t, grad_t, lse, h1_far, buckets, small = refs[:11]
    pay, weight_pay = refs[11:13]
    dq, dk, dv, full, brow, tiles, sums, diag, h1, sem = refs[13:]
    fetch = pltpu.make_async_copy(h1_far, h1, sem)
    fetch.start()
    n_tiles, side, _ = tiles.shape
    blocks = side // 128
    bias_tiles(rel, buckets, brow, tiles)
    sums[...] = jnp.zeros_like(sums)
    dk[...] = jnp.zeros_like(dk)
    dv[...] = jnp.zeros_like(dv)

    def one_query_tile(qi, carry):
        q_start = at_tile(qi, side)
        q = qa[pl.ds(q_start, side), :]
        q_t = qt[:, pl.ds(q_start, side)]
        g_t = jnp.concatenate([grad_t[qi * blocks + b] for b in range(blocks)], axis=1)
        o_t = jnp.concatenate([out_t[qi * blocks + b] for b in range(blocks)], axis=1)
        row_dots = jnp.sum(g_t.astype(f32) * o_t.astype(f32), axis=0, keepdims=True)
        norm = lse[:, pl.ds(q_start, side)]

        def fold(k_start, offset, acc, diagonal):
            where_k = pl.ds(k_start, side)
            scores = dot(ka[where_k, :], q, NT) + tiles[offset]
            probs = jnp.exp(scores - norm)
            if diagonal:
                probs = jnp.where(iota((side, side), 0) <= iota((side, side), 1), probs, 0.0)
            grad_prob = dot(va[where_k, :][:, :head_dim], g_t, NN)
            grad_score = probs * (grad_prob - row_dots)
            low = grad_score.astype(bf16)
            sums[offset] = sums[offset] + grad_score
            dv[:, where_k] = dv[:, where_k] + dot(g_t, probs.astype(bf16), NT)
            dk[:, where_k] = dk[:, where_k] + dot(q_t, low, NT)
            return acc + dot(kt[:, where_k], low, NN)

        acc = fold(q_start, 0, jnp.zeros((head_dim, side), f32), True)

        def earlier(kj, acc):
            return fold(at_tile(kj, side), qi - kj, acc, False)

        dq[:, pl.ds(q_start, side)] = loop(qi, earlier, acc)
        return carry

    loop(n_tiles, one_query_tile, 0)
    full[:head_dim, :] = (dq[...] * 0.125).astype(bf16)
    full[head_dim : 2 * head_dim, :] = dk[...].astype(bf16)
    full[2 * head_dim :, :] = dv[...].astype(bf16)
    for b in range(pay.shape[0]):
        pay[b] = full[:, b * 128 : (b + 1) * 128]
    flip = jnp.where(iota((128, 128), 0) + iota((128, 128), 1) == 127, 1.0, 0.0).astype(bf16)
    diag[...] = jnp.zeros_like(diag)
    for o in range(n_tiles):
        for a in range(blocks):
            turned = dot(flip, sums[o, a * 128 : (a + 1) * 128, :].astype(bf16), NN)
            wide = jnp.concatenate([turned, jnp.zeros((128, 128), f32)], axis=1)
            lined = pltpu.roll(wide, 0, axis=1, stride=1, stride_axis=0)
            first = (o + 1) * side - (a + 1) * 128
            where_d = slice(first, first + side + 128)
            diag[:, where_d] = diag[:, where_d] + jnp.sum(lined, axis=0, keepdims=True)
    ids = jnp.concatenate([buckets[...], jnp.full((1, side), -1, jnp.int32)], axis=1)
    ids = pltpu.roll(ids, side - 1, 1)
    hot = jnp.where(ids == iota((128, ids.shape[1]), 0), 1.0, 0.0).astype(bf16)
    high, low = split2(jnp.broadcast_to(diag[...], (8, diag.shape[1])))
    rel_grad = dot(high, hot, NT) + dot(low, hot, NT)
    fetch.wait()
    grad_w = dot(full[...], h1[...], NN).astype(bf16)
    n_pay, pay_rows, lanes = weight_pay.shape
    n_ctx = n_pay // n_dp
    rows = grad_w.shape[0] // n_ctx
    rel_row = jnp.concatenate([rel_grad, jnp.zeros((8, lanes - 128), f32)], axis=1)
    line = iota((16, lanes), 0)
    for d in range(n_dp):
        for c in range(n_ctx):
            here = slice(d * lanes, (d + 1) * lanes)
            weight_pay[d * n_ctx + c, :rows, :] = grad_w[c * rows : (c + 1) * rows, here]
            extra = jnp.where(line == 0, rel_row[0:1], 0.0)
            if c < 4:
                for r in range(2):
                    row = small[2 * c + r : 2 * c + r + 1, here]
                    extra = jnp.where(line == 8 + r, row, extra)
            weight_pay[d * n_ctx + c, rows:, :] = extra.astype(bf16)


def middle_kernel(n_heads, sc, recv, w_out, x, gain, pick, middle, *send):
    rows, width = x.shape
    attn_t = jnp.concatenate([recv[h] for h in range(n_heads)], axis=0)
    branch = dot(attn_t, w_out[...], TN)
    valid = iota((rows, 1), 0) < valid_rows(sc, rows)
    mid = x[...].astype(f32) + jnp.where(valid, branch, 0.0)
    middle[...] = mid
    h2 = (mid * norm_scale(mid) * row_of(gain)).astype(bf16)
    for k, piece in enumerate(send):
        expert = lax.rem(lax.axis_index("exp") + k, len(send))
        chosen = pick[pl.ds(pl.multiple_of(expert * CAP, 16), CAP), :]
        piece[...] = dot(chosen, h2, NN).astype(bf16)


def gate_of(h2, pay, width, w3, own):
    logits = dot(h2, w3, NN)
    sel = 2.0 * own - pay[:, width:].astype(f32)
    diff = jnp.sum(logits * sel, axis=1, keepdims=True)
    return 1.0 / (1.0 + jnp.exp(-diff)), sel


def own_lanes(expert, n_experts):
    lane = iota((1, 128), 1)
    return jnp.where((lane < 3 * n_experts) & (lane % n_experts == expert), 1.0, 0.0)


def expert_kernel(n_experts, h2, pay, w3, w3_t, w_up, w_down, *refs):
    mix, back = refs[:n_experts], refs[n_experts : 2 * n_experts]
    router, z_acc, in_acc, dz, gates, rows_out = refs[2 * n_experts :]
    step = pl.program_id(0)
    width = h2.shape[1]
    expert = lax.axis_index("exp")
    own = own_lanes(expert, n_experts)

    @pl.when(step == 0)
    def _():
        gate, _ = gate_of(h2[...], pay, width, w3[...], own)
        gates[...] = jnp.broadcast_to(gate, gates.shape)
        dz[...] = (gate * pay[:, :width].astype(f32)).astype(bf16)
        z_acc[...] = jnp.zeros_like(z_acc)
        in_acc[...] = jnp.zeros_like(in_acc)

    up = dot(h2[...], w_up[...], NN)
    act, slope = gelu_parts(up)
    grad_hidden = dot(dz[...], w_down[...], NT)
    grad_up = (grad_hidden * slope).astype(bf16)
    z_acc[...] += dot(act.astype(bf16), w_down[...], NN)
    in_acc[...] += dot(grad_up, w_up[...], NT)

    @pl.when(step == pl.num_programs(0) - 1)
    def _():
        gate = gates[:, 0:1]
        sel = 2.0 * own - pay[:, width:].astype(f32)
        z = z_acc[...].astype(bf16).astype(f32)
        rows_out[...] = (gate * z).astype(bf16)
        for k in range(n_experts):
            mix[k][...] = rows_out[k * CAP : (k + 1) * CAP, :]
        grad_gate = jnp.sum(pay[:, :width].astype(f32) * z, axis=1, keepdims=True)
        high, low = split2((gate * (1.0 - gate) * grad_gate) * sel)
        total = in_acc[...] + dot(high, w3_t[...], NN) + dot(low, w3_t[...], NN)
        rows_out[...] = total.astype(bf16)
        for k in range(n_experts):
            back[k][...] = rows_out[k * CAP : (k + 1) * CAP, :]
        router[...] = (dot(high, h2[...], TN) + dot(low, h2[...], TN))[:8]


def collect(pieces, pick):
    n_experts = len(pieces)
    total = None
    for k, piece in enumerate(pieces):
        expert = lax.rem(lax.axis_index("exp") + k, n_experts)
        chosen = pick[pl.ds(pl.multiple_of(expert * CAP, 16), CAP), :]
        part = dot(chosen, piece[...], TN)
        total = part if total is None else total + part
    return total


def middle_back_kernel(n_heads, n_experts, sc, *refs):
    back = refs[:n_experts]
    pick, middle, dy, gain, recv, w_out, router, dmid, grad_t, red, small = refs[n_experts:]
    rows, width = middle.shape
    grad_h2 = collect(back, pick)
    grad_in, xhat = norm_back(middle[...], row_of(gain), grad_h2)
    grad_mid = dy[...].astype(f32) + grad_in
    dmid[...] = grad_mid
    valid = iota((rows, 1), 0) < valid_rows(sc, rows)
    branch = jnp.where(valid, grad_mid, 0.0).astype(bf16)
    attn_t = jnp.concatenate([recv[h] for h in range(n_heads)], axis=0)
    heads = dot(w_out[...], branch, NT).astype(bf16)
    head_dim = width // n_heads
    for h in range(n_heads):
        grad_t[h] = heads[h * head_dim : (h + 1) * head_dim]
    for h in range(n_heads, grad_t.shape[0]):
        grad_t[h] = jnp.zeros((head_dim, rows), bf16)
    red[...] = dot(attn_t, branch, NN).astype(bf16)
    gains = jnp.sum(grad_h2 * xhat, axis=0, keepdims=True)
    line = iota((8, width), 0)
    moved = pltpu.roll(router[...], 1, 0)
    small[...] = jnp.where(line == 0, gains, jnp.where(line < 5, moved, 0.0))


def output_kernel(n_experts, sc, *refs):
    mix = refs[:n_experts]
    pick, middle, out = refs[n_experts:]
    rows = middle.shape[0]
    valid = iota((rows, 1), 0) < valid_rows(sc, rows)
    total = collect(mix, pick)
    out[...] = (middle[...] + jnp.where(valid, total, 0.0)).astype(bf16)


def token_grad_kernel(n_heads, recv, w_qkv, x, gain, dmid, out):
    grad_t = jnp.concatenate([recv[h] for h in range(n_heads)], axis=0)
    grad_h1 = dot(w_qkv[...], grad_t, NN).T
    grad_in, _ = norm_back(x[...].astype(f32), row_of(gain), grad_h1)
    out[...] = dmid[...] + grad_in


def load_rows(h_pieces, where, pays, h2, pay, sem):
    rows = h_pieces[0].shape[0]
    copies = []
    for i, piece in enumerate(h_pieces):
        here = pl.ds(i * rows, rows)
        source = pays[i] if len(pays) > 1 else pays[0].at[
            pl.ds(pl.multiple_of(where[i] * rows, 16), rows), :
        ]
        copies.append(pltpu.make_async_copy(piece, h2.at[here, :], sem.at[0, i]))
        copies.append(pltpu.make_async_copy(source, pay.at[here, :], sem.at[1, i]))
    return copies


def chip_index(a, b, o):
    n_dp = lax.axis_size("dp")
    n_x = lax.axis_size("ctx") // 2
    dp, ctx = lax.axis_index("dp"), lax.axis_index("ctx")
    core = lax.rem(lax.rem(ctx, 2) + o, 2)
    x_at = lax.rem(ctx // 2 + (n_x - b), n_x)
    return (lax.rem(dp + (n_dp - a), n_dp) * n_x + x_at) * 2 + core


def weight_grad_kernel(n_experts, keys, together, last, sc, *refs):
    n_pieces = len(keys)
    h_pieces = refs[:n_pieces]
    n_in = n_pieces + (1 if last else n_pieces)
    pays = refs[n_pieces:n_in]
    w3, w_up, w_down = refs[n_in : n_in + 3]
    if last:
        up_base, down_base, up_out, down_out, low = refs[n_in + 3 : n_in + 8]
    else:
        up_out, down_out = refs[n_in + 3 : n_in + 5]
    h2, pay, dz, hid_t, dup_t, sem = refs[-6:]
    step = pl.program_id(0)
    rows = h_pieces[0].shape[0]
    width = h2.shape[1]
    block = w_down.shape[0]
    copies = load_rows(h_pieces, [chip_index(*key) for key in keys], pays, h2, pay, sem)

    @pl.when(step == 0)
    def _():
        for copy in copies:
            copy.start()

    own = own_lanes(lax.axis_index("exp"), n_experts)
    up_t = w_up[...].T
    down = w_down[...]
    chunk = together * rows
    for i in range(n_pieces // together):
        here = slice(i * chunk, (i + 1) * chunk)

        @pl.when(step == 0)
        def _(i=i, here=here):
            for copy in copies[2 * together * i : 2 * together * (i + 1)]:
                copy.wait()
            part = pay[here, :]
            gate, _ = gate_of(h2[here, :], part, width, w3[...], own)
            dz[here, :] = (gate * part[:, :width].astype(f32)).astype(bf16)

        act, slope = gelu_parts(dot(up_t, h2[here, :], NT))
        hid_t[:, here] = act.astype(bf16)
        dup_t[:, here] = (dot(down, dz[here, :], NT) * slope).astype(bf16)
    grad_up = dot(dup_t[...], h2[...], NN)
    grad_down = dot(hid_t[...], dz[...], NN)
    if last:
        grad_up = grad_up + up_base[...]
        grad_down = grad_down + down_base[...]
        low[:block, :] = grad_up.astype(bf16)
        low[block:, :] = grad_down.astype(bf16)
        up_out[...] = grad_up.T
    else:
        up_out[...] = grad_up
    down_out[...] = grad_down


def fill_kernel(sc, low, *refs):
    up_out, down_out = refs[-2:]
    block = down_out.shape[0]
    up_out[...] = low[:block, :].astype(f32).T
    down_out[...] = low[block:, :].astype(f32)


def assemble_kernel(keys, rows, n_groups, head_cols, *refs):
    n_pieces = len(keys)
    pieces = refs[:n_pieces]
    w_qkv, gain, grad, gain_grad, rel_grad, gain2_grad, router_grad = refs[
        n_pieces : n_pieces + 7
    ]
    turned, rel_t, stage, acc, sem = refs[n_pieces + 7 :]
    lanes = pieces[0].shape[-1]
    acc[...] = jnp.zeros_like(acc)
    n_dp, n_exp = lax.axis_size("dp"), lax.axis_size("exp")
    n_x = lax.axis_size("ctx") // 2
    dp, ctx, exp = (lax.axis_index(name) for name in ("dp", "ctx", "exp"))
    rel_t[...] = jnp.zeros_like(rel_t)
    for piece, ids in zip(pieces, keys):
        for i, (a, b, o, k) in enumerate(ids):
            d = lax.rem(dp + (n_dp - a), n_dp)
            c = lax.rem(ctx // 2 + (n_x - b), n_x) * 2 + lax.rem(lax.rem(ctx, 2) + o, 2)
            e = lax.rem(exp + (n_exp - k), n_exp)
            lane_at = pl.multiple_of(d * lanes, 128)
            for g in range(n_groups):
                head = g * n_exp + e
                row_at = pl.multiple_of(head * head_cols + c * rows, 16)
                turned[pl.ds(row_at, rows), pl.ds(lane_at, lanes)] = piece[
                    i, g * rows : (g + 1) * rows, :
                ]
                rel_t[pl.ds(head, 1), :] = piece[
                    i, n_groups * rows + g : n_groups * rows + g + 1, :128
                ].astype(f32)
            first = n_groups * rows + 8
            where_s = pl.ds(lane_at, lanes)
            small = piece[i, first : first + 8, :].astype(f32)
            acc[c, :, where_s] = acc[c, :, where_s] + small
    rel_grad[...] = rel_t[: rel_grad.shape[0], : rel_grad.shape[1]]
    width, columns = grad.shape
    gain2_grad[...] = acc[0, 0:1, :].reshape(width)
    for e in range(router_grad.shape[0]):
        router_grad[e : e + 1, :] = acc[(e + 1) // 2, (e + 1) % 2 : (e + 1) % 2 + 1, :]
    copies = []
    for i, a in enumerate(range(0, width, 128)):
        total = jnp.zeros((128, 128), f32)
        for b in range(0, columns, 128):
            tile = turned[b : b + 128, a : a + 128].astype(f32).T
            stage[a : a + 128, b : b + 128] = tile
            total = total + tile * w_qkv[a : a + 128, b : b + 128].astype(f32)
        where_a = pl.ds(a, 128)
        copy = pltpu.make_async_copy(stage.at[where_a, :], grad.at[where_a, :], sem.at[i])
        copy.start()
        copies.append(copy)
        sums = jnp.sum(total.T, axis=0, keepdims=True)
        sums = sums / gain[a : a + 128].reshape(1, 128)
        gain_grad[a : a + 128] = sums.reshape(128)
    for copy in copies:
        copy.wait()


def shard_kernel(n_dp, n_groups, summed, shard):
    n_ctx = summed.shape[0] // n_dp
    part = summed.shape[1] - 16
    line = iota((16, summed.shape[2]), 0)
    extra = jnp.zeros(line.shape, f32)
    for i in range(summed.shape[0]):
        extra = extra + summed[i, part:, :].astype(f32)
    extra = jnp.where(line >= 8, extra, 0.0)
    for g in range(n_groups):
        total = summed[g].astype(f32)
        for d in range(1, n_dp):
            total = total + summed[d * n_ctx + g].astype(f32)
        shard[0, g * part : (g + 1) * part, :] = total[:part].astype(bf16)
        extra = jnp.where(line == g, total[part : part + 1], extra)
    shard[0, n_groups * part :, :] = extra.astype(bf16)


def reduced_kernel(red, attn_out):
    attn_out[...] = red[...].astype(f32)


def after(value, *others):
    return lax.optimization_barrier((value, others))[0]


def on_device(
    n_dp,
    n_ctx,
    n_exp,
    tokens,
    lengths,
    routes,
    buckets,
    cotangent,
    attn_gain,
    w_qkv,
    w_attn_out,
    rel_bias,
    ffn_gain,
    w_router,
    w_up,
    w_down,
):
    x = tokens[0]
    dy = cotangent[0]
    rows, width = x.shape
    seq = buckets.shape[0]
    n_buckets, n_heads = rel_bias.shape
    head_dim = width // n_heads
    n_experts = w_router.shape[1]
    ff = w_up.shape[2]
    n_slot = n_ctx * n_exp
    n_groups = n_heads // n_exp
    n_x = n_ctx // 2
    small = n_x == 2 and n_dp == 2
    side = 512 if seq <= 2048 else 256
    n_tiles = seq // side
    slot_rows = n_experts * CAP
    slot_axes, all_chips = ("ctx", "exp"), ("dp", "ctx")

    def ring(v, shift):
        return lax.ppermute(v, "exp", [(i, (i + shift) % n_exp) for i in range(n_exp)])

    def swap(v):
        return lax.ppermute(v, "ctx", [(i, i ^ 1) for i in range(n_ctx)])

    def chips(v, a, b):
        perm = []
        for d in range(n_dp):
            for c in range(n_ctx):
                to = ((d + a) % n_dp) * n_ctx + ((c // 2 + b) % n_x) * 2 + c % 2
                perm.append((d * n_ctx + c, to))
        return lax.ppermute(v, all_chips, perm)

    def exchange(v, axes):
        return lax.all_to_all(v, axes, split_axis=0, concat_axis=0, tiled=True)

    def to_experts(parts):
        return [parts[0]] + [ring(parts[k], k) for k in range(1, n_exp)]

    def from_experts(parts):
        return [parts[0]] + [ring(parts[k], n_exp - k) for k in range(1, n_exp)]

    keys = [(a, b, o) for o in (0, 1) for a, b in ((0, 0), (0, 1), (1, 0), (1, 1))]

    with jax.named_scope("routing"):
        places, pick, w3, w3_t, _, *pay = call(
            functools.partial(route_kernel, n_experts),
            [
                sds((1,), jnp.int32),
                sds((slot_rows, rows), bf16),
                sds((width, 128), bf16),
                sds((128, width), bf16),
                sds((slot_rows, width + 128), bf16),
            ]
            + [sds((CAP, width + 128), bf16)] * n_experts,
            [smem()] + [vmem()] * 3,
            name="routing",
        )(lengths, routes[0].T, dy, w_router.T)

    with jax.named_scope("gather_tokens"):
        if small:
            column = [(x, 0, 0), (ring(after(x, pick), 1), 0, 1)]
            column += [(ring(x, k), 0, k) for k in range(2, n_exp)]
            onward = [v for v, _, _ in column]
            onward[-1] = after(onward[-1], pay)
            pieces = column + [(chips(v, 0, 1), 1, k) for k, v in enumerate(onward)]
            pieces = [(v, b, 0, k) for v, b, k in pieces]
            arrived = to_experts(after(pay, pieces[-1][0]))
            pieces = pieces + [(swap(v), b, 1, k) for v, b, _, k in pieces]
            blocks = [v for v, _, _, _ in pieces]
            shifts = [ids for _, *ids in pieces]
        else:
            blocks = [lax.all_gather(x, slot_axes, axis=0, tiled=True)]
            shifts = [(-1, 0, 0)]
            arrived = to_experts(pay)

    with jax.named_scope("attention"):
        bucket_row = buckets.reshape(1, seq)
        blocks[-1] = after(blocks[-1], bucket_row)
        attn_outs = (
            sds((seq, width), bf16),
            sds((seq, 128), bf16),
            sds((seq, 128), bf16),
            sds((seq, 128), bf16),
            sds((head_dim, seq), bf16),
            sds((head_dim, seq), bf16),
            sds((n_slot, head_dim, 128), bf16),
            sds((1, seq), f32),
        )
        any_spec = pl.BlockSpec(memory_space=pl.ANY)
        h1, qa, ka, va, qt, kt, out_t, lse = call(
            functools.partial(attn_kernel, shifts, head_dim),
            attn_outs,
            [smem(), smem()] + [vmem()] * (len(blocks) + 1) + [any_spec, vmem()],
            [pltpu.VMEM(o.shape, o.dtype) for o in attn_outs[:6]]
            + [
                pltpu.VMEM((head_dim, seq), bf16),
                pltpu.VMEM((1, seq + side), f32),
                pltpu.VMEM((n_tiles, side, side), f32),
                pltpu.VMEM((width, 6 * head_dim), bf16),
                pltpu.VMEM((width, 384), bf16),
                pltpu.SemaphoreType.DMA,
                pltpu.SemaphoreType.DMA((6,)),
            ],
            micros=10,
            name="attention",
            limit=58,
            out_specs=(any_spec,) * 6 + (vmem(),) * 2,
        )(lengths, rel_bias.T, *blocks, attn_gain, w_qkv, bucket_row)
        attn_in = exchange(out_t, slot_axes)
        pay_in = jnp.concatenate([arrived[0]] + [after(v, out_t) for v in arrived[1:]])

    with jax.named_scope("middle"):
        piece_shape = sds((CAP, width), bf16)
        middle, *send = call(
            functools.partial(middle_kernel, n_heads),
            [sds((rows, width), f32)] + [piece_shape] * n_experts,
            [smem()] + [vmem()] * 5,
            name="middle",
        )(lengths, attn_in, w_attn_out, x, ffn_gain, pick)
        h2_in = jnp.concatenate(to_experts(send))

    with jax.named_scope("experts"):
        block = 1024
        row_spec = pl.BlockSpec((slot_rows, width), lambda i: (0, 0))
        piece_spec = pl.BlockSpec((CAP, width), lambda i: (0, 0))
        *parts, router = pl.pallas_call(
            functools.partial(expert_kernel, n_experts),
            out_shape=[piece_shape] * (2 * n_experts)
            + [sds((8, width), f32)],
            grid_spec=pltpu.PrefetchScalarGridSpec(
                num_scalar_prefetch=0,
                grid=(ff // block,),
                in_specs=[
                    row_spec,
                    pl.BlockSpec((slot_rows, width + 128), lambda i: (0, 0)),
                    pl.BlockSpec((width, 128), lambda i: (0, 0)),
                    pl.BlockSpec((128, width), lambda i: (0, 0)),
                    pl.BlockSpec((width, block), lambda i: (0, i)),
                    pl.BlockSpec((block, width), lambda i: (i, 0)),
                ],
                out_specs=[piece_spec] * (2 * n_experts)
                + [pl.BlockSpec((8, width), lambda i: (0, 0))],
                scratch_shapes=[
                    pltpu.VMEM((slot_rows, width), f32),
                    pltpu.VMEM((slot_rows, width), f32),
                    pltpu.VMEM((slot_rows, width), bf16),
                    pltpu.VMEM((slot_rows, 128), f32),
                    pltpu.VMEM((slot_rows, width), bf16),
                ],
            ),
            compiler_params=params(),
            cost_estimate=cost_of(12),
            name="experts",
        )(h2_in, pay_in, w3, w3_t, w_up[0], w_down[0])
        mix_parts, back_parts = parts[:n_experts], parts[n_experts:]
        back_in = from_experts(back_parts)

    shares = n_dp * n_ctx
    with jax.named_scope("expert_weight_grads"):
        if small:
            pay_all = lax.all_gather(pay_in, all_chips, axis=0, tiled=True)
            beside = [chips(h2_in, a, b) for a, b in ((0, 1), (1, 0), (1, 1))]
            block = 512
            n_parts = ff // (2 * block)
            full_shapes = [sds((width, ff), f32), sds((ff, width), f32)]

            def half_specs(other):
                def at(i, s):
                    return (1 - s[0] if other else s[0]) * n_parts + i

                return (
                    pl.BlockSpec((width, block), lambda i, s: (0, at(i, s))),
                    pl.BlockSpec((block, width), lambda i, s: (at(i, s), 0)),
                )

            low_spec = pl.BlockSpec((2 * block, width), lambda i, s: (i, 0))

            base_spec = pl.BlockSpec((block, width), lambda i, s: (i, 0))
            base_shape = sds((ff // 2, width), f32)

            def weight_half(pieces, pays, keys, base, micros):
                specs = half_specs(False)
                count = len(pieces) * slot_rows
                shapes, outs = [base_shape] * 2, [base_spec] * 2
                if base:
                    shapes, outs = full_shapes + [sds((ff, width), bf16)], [*specs, low_spec]
                return pl.pallas_call(
                    functools.partial(weight_grad_kernel, n_experts, keys, 2, bool(base)),
                    out_shape=shapes,
                    grid_spec=pltpu.PrefetchScalarGridSpec(
                        num_scalar_prefetch=1,
                        grid=(n_parts,),
                        in_specs=[any_spec] * (len(pieces) + len(pays))
                        + [pl.BlockSpec((width, 128), lambda i, s: (0, 0)), *specs]
                        + [base_spec] * len(base),
                        out_specs=outs,
                        scratch_shapes=[
                            pltpu.VMEM((count, width), bf16),
                            pltpu.VMEM((count, width + 128), bf16),
                            pltpu.VMEM((count, width), bf16),
                            pltpu.VMEM((block, count), bf16),
                            pltpu.VMEM((block, count), bf16),
                            pltpu.SemaphoreType.DMA((2, len(pieces))),
                        ],
                    ),
                    compiler_params=params(),
                    cost_estimate=cost_of(micros),
                    name="weight_grads",
                )(places, *pieces, *pays, w3, w_up[0], w_down[0], *base)

            def weight_fill(low, grads):
                return pl.pallas_call(
                    fill_kernel,
                    out_shape=full_shapes,
                    grid_spec=pltpu.PrefetchScalarGridSpec(
                        num_scalar_prefetch=1,
                        grid=(n_parts,),
                        in_specs=[low_spec, any_spec, any_spec],
                        out_specs=half_specs(True),
                    ),
                    input_output_aliases={2: 0, 3: 1},
                    compiler_params=params(),
                    cost_estimate=cost_of(8),
                    name="fill",
                )(places, low, *grads)


            pays = [pay_in, swap(pay_in)]
            base = weight_half([h2_in, swap(h2_in)], pays, keys[::4], (), 11)
            back_in[0] = after(back_in[0], beside, base, pay_all)

    with jax.named_scope("middle_back"):
        dmid, grad_t, red, sums = call(
            functools.partial(middle_back_kernel, n_heads, n_experts),
            (
                sds((rows, width), f32),
                sds((n_slot, head_dim, rows), bf16),
                sds((width, width), bf16),
                sds((8, width), f32),
            ),
            [smem()] + [vmem()] * (7 + n_experts),
            name="middle_back",
        )(lengths, *back_in, pick, middle, dy, ffn_gain, attn_in, w_attn_out, router)
        grad_in = exchange(grad_t, slot_axes)

    if small:
        with jax.named_scope("expert_weight_grads"):
            beside = [after(v, grad_t) for v in beside]
            pieces = beside + [swap(v) for v in beside]
            *grads, low = weight_half(pieces, [pay_all], keys[1:4] + keys[5:], base, 8)
            share = lax.psum_scatter(red, all_chips, scatter_dimension=0, tiled=True)
            grad_in = after(grad_in, low, share)
            others = [ring(share, k) for k in range(1, n_exp)]

    with jax.named_scope("attention_back"):
        part = 3 * head_dim // n_ctx
        lanes = width // n_dp
        dqkv, weight_pay = call(
            functools.partial(attn_back_kernel, head_dim, n_dp),
            (sds((n_slot, 3 * head_dim, rows), bf16), sds((shares, part + 16, lanes), bf16)),
            [smem()] + [vmem()] * 8 + [any_spec, vmem(), vmem()],
            [
                pltpu.VMEM((head_dim, seq), f32),
                pltpu.VMEM((head_dim, seq), f32),
                pltpu.VMEM((head_dim, seq), f32),
                pltpu.VMEM((3 * head_dim, seq), bf16),
                pltpu.VMEM((1, seq + side), f32),
                pltpu.VMEM((n_tiles, side, side), f32),
                pltpu.VMEM((n_tiles, side, side), f32),
                pltpu.VMEM((1, seq + side), f32),
                pltpu.VMEM((seq, width), bf16),
                pltpu.SemaphoreType.DMA,
            ],
            micros=11,
            name="attention_back",
            limit=58,
        )(rel_bias.T, qa, ka, va, qt, kt, out_t, grad_in, lse, h1, bucket_row, sums)
        if small:
            weight_pay = after(weight_pay, others)
            share = share.astype(f32) + others[0] + others[1] + others[2]
            share = after(share, weight_pay).astype(bf16)
        else:
            mix_in = from_experts(mix_parts)
        summed = exchange(weight_pay, all_chips)
        if small:
            summed = after(summed, share)

    with jax.named_scope("projection_grad"):
        shard = call(
            functools.partial(shard_kernel, n_dp, n_groups),
            sds((1, n_groups * part + 16, lanes), bf16),
            [vmem()],
            name="shard",
        )(summed)
        if small:
            column = [ring(shard, k) for k in range(1, n_exp)]
            column = jnp.concatenate([shard] + column)
            low_in = swap(after(low, weight_pay))
            column = after(column, low_in)
            mix_in = from_experts([after(v, column) for v in mix_parts])


    if small:
        with jax.named_scope("expert_weight_grads"):
            grad_up, grad_down = weight_fill(low_in, grads)
    else:
        with jax.named_scope("expert_weight_grads"):
            own = own_lanes(lax.axis_index("exp"), n_experts)
            gate, _ = gate_of(h2_in, pay_in, width, w3, own)
            dz = (gate * pay_in[:, :width].astype(f32)).astype(bf16)
            act, slope = gelu_parts(dot(h2_in, w_up[0], NN))
            dup = (dot(dz, w_down[0], NT) * slope).astype(bf16)
            grad_up = lax.psum(dot(h2_in, dup, TN).astype(bf16), all_chips).astype(f32)
            grad_down = lax.psum(dot(act.astype(bf16), dz, TN).astype(bf16), all_chips)
            grad_down = grad_down.astype(f32)

    with jax.named_scope("output"):
        output = call(
            functools.partial(output_kernel, n_experts),
            sds((rows, width), bf16),
            [smem()] + [vmem()] * (2 + n_experts),
            micros=0.2,
            name="output",
        )(lengths, *mix_in, pick, middle)

    with jax.named_scope("token_grads"):
        if small:
            beside_x = chips(column, 0, 1)
            dqkv = after(dqkv, beside_x)
        dqkv_in = exchange(dqkv, slot_axes)
        grad_tokens = call(
            functools.partial(token_grad_kernel, n_heads),
            sds((rows, width), f32),
            [vmem()] * 5,
            name="token_grads",
        )(dqkv_in, w_qkv, x, attn_gain, dmid)

    with jax.named_scope("output_projection_grad"):
        if small:
            reduced = lax.all_gather(share, all_chips, axis=0, tiled=True)
        else:
            reduced = lax.psum(red, ("dp", "ctx", "exp"))
            sums = lax.psum(sums, ("dp", "ctx", "exp"))
            grad_ffn_gain, grad_router = sums[0], sums[1 : 1 + n_experts].T
        grad_attn_out = call(
            reduced_kernel,
            sds((width, width), f32),
            [vmem()],
            micros=0.2,
            name="reduced",
        )(reduced)

    with jax.named_scope("projection_grad"):
        if small:
            wide = [(column, 0, 0, range(n_exp))]
            wide.append((beside_x, 0, 1, range(n_exp)))
            wide.append((chips(column, 1, 0), 1, 0, range(n_exp)))
            wide.append((chips(beside_x, 1, 0), 1, 1, range(n_exp)))
            early = (grad_up, grad_down, grad_attn_out, mix_in)
            wide = [(after(v, early), a, b, ks) for v, a, b, ks in wide]
            final = [v for v, _, _, _ in wide] + [swap(v) for v, _, _, _ in wide]
            keys = [[(a, b, o, k) for k in ks] for o in (0, 1) for _, a, b, ks in wide]
            grad_qkv, grad_attn_gain, grad_rel, grad_ffn_gain, grad_router = call(
                functools.partial(assemble_kernel, keys, part, n_groups, 3 * head_dim),
                (
                    sds((width, 3 * width), f32),
                    sds((width,), f32),
                    sds((n_heads, n_buckets), f32),
                    sds((width,), f32),
                    sds((n_experts, width), f32),
                ),
                [vmem()] * (len(final) + 2),
                [
                    pltpu.VMEM((3 * width, width), bf16),
                    pltpu.VMEM((128, 128), f32),
                    pltpu.VMEM((width, 3 * width), f32),
                    pltpu.VMEM((n_ctx, 8, width), f32),
                    pltpu.SemaphoreType.DMA((width // 128,)),
                ],
                micros=6,
                name="assemble",
                limit=32,
                out_specs=(any_spec,) + (vmem(),) * 4,
            )(*final, w_qkv, attn_gain)
            grad_rel, grad_router = grad_rel.T, grad_router.T
        else:
            every = lax.all_gather(shard[0], ("dp", "ctx", "exp"), axis=0, tiled=False)
            every = every.reshape(n_dp, n_ctx, n_exp, n_groups * part + 16, lanes).astype(f32)
            main = every[:, :, :, : n_groups * part]
            main = main.reshape(n_dp, n_ctx, n_exp, n_groups, part, lanes)
            grad_qkv = main.transpose(0, 5, 3, 2, 1, 4).reshape(width, 3 * width)
            rel_rows = every[0, 0, :, n_groups * part : n_groups * (part + 1), :n_buckets]
            grad_rel = rel_rows.transpose(2, 1, 0).reshape(n_buckets, n_heads)
            grad_attn_gain = jnp.sum(grad_qkv * w_qkv.astype(f32), axis=1) / attn_gain

    return (
        output[None],
        grad_tokens[None],
        grad_attn_gain,
        grad_qkv,
        grad_attn_out,
        grad_rel,
        grad_ffn_gain,
        grad_router,
        grad_up[None],
        grad_down[None],
    )


def solution(mesh):
    sizes = dict(mesh.shape)
    by_token = P("dp", ("ctx", "exp"), None)
    by_expert = P("exp", None, None)
    return jax.shard_map(
        functools.partial(on_device, sizes["dp"], sizes["ctx"], sizes["exp"]),
        mesh=mesh,
        in_specs=(
            by_token,
            P("dp"),
            by_token,
            P(),
            by_token,
            P(),
            P(),
            P(),
            P(),
            P(),
            P(),
            by_expert,
            by_expert,
        ),
        out_specs=(
            by_token,
            by_token,
            P(),
            P(),
            P(),
            P(),
            P(),
            P(),
            by_expert,
            by_expert,
        ),
        check_vma=False,
    )
```

```python
import functools

import jax
import jax.numpy as jnp
from jax import lax
from jax.experimental import pallas as pl
from jax.experimental.pallas import tpu as pltpu
from jax.sharding import PartitionSpec as P

CAP = 80
EPS = 1e-06
NEG = -1e30
VMEM_LIMIT = 58 << 20
bf16 = jnp.bfloat16
f32 = jnp.float32
NN = ((1,), (0,))
NT = ((1,), (1,))
TN = ((0,), (0,))
GELU_C = 0.7978845608028654
GELU_A = 0.044715


def dot(left, right, dims):
    return lax.dot_general(left, right, (dims, ((), ())), preferred_element_type=f32)


def iota(shape, axis):
    return lax.broadcasted_iota(jnp.int32, shape, axis)


def norm_scale(values):
    return lax.rsqrt(jnp.mean(values * values, axis=-1, keepdims=True) + EPS)


def row_of(ref):
    return ref[...].reshape(1, ref.shape[0])


def norm_back(values, gain, grad):
    scale = norm_scale(values)
    xhat = values * scale
    gxhat = grad * gain
    grad_in = scale * (gxhat - xhat * jnp.mean(gxhat * xhat, axis=-1, keepdims=True))
    return grad_in, xhat


def gelu_parts(u):
    square = u * u
    t = jnp.tanh(u * (GELU_C + (GELU_C * GELU_A) * square))
    half = 0.5 * (1.0 + t)
    slope = half + (0.5 * u) * (1.0 - t * t) * (GELU_C + (3.0 * GELU_C * GELU_A) * square)
    return u * half, slope


def split2(values):
    high = values.astype(bf16)
    return high, (values - high.astype(f32)).astype(bf16)


def params(limit=VMEM_LIMIT):
    return pltpu.CompilerParams(vmem_limit_bytes=limit)


def vmem():
    return pl.BlockSpec(memory_space=pltpu.VMEM)


def smem():
    return pl.BlockSpec(memory_space=pltpu.SMEM)


def cost_of(micros):
    return pl.CostEstimate(
        flops=int(micros * 1e9), bytes_accessed=int(micros * 1e5), transcendentals=0
    )


def call(kernel, outs, ins, scratch=(), micros=3, name=None, limit=24, out_specs=None):
    return pl.pallas_call(
        kernel,
        out_shape=outs,
        in_specs=ins,
        out_specs=out_specs
        or jax.tree.map(lambda o: smem() if o.dtype == jnp.int32 else vmem(), outs),
        scratch_shapes=list(scratch),
        compiler_params=params(limit << 20),
        cost_estimate=cost_of(micros),
        name=name,
    )


def sds(shape, dtype):
    return jax.ShapeDtypeStruct(shape, dtype)


def valid_rows(lengths, rows):
    index = lax.axis_index("ctx") * lax.axis_size("exp") + lax.axis_index("exp")
    return lengths[0] - index * rows


def route_kernel(n_experts, sc, routes_t, dy, router_t, places, pick, w3, w3_t, full, *pay):
    places[0] = lax.rem(lax.axis_index("ctx"), 2)
    rows = dy.shape[0]
    width = dy.shape[1]
    table = jnp.concatenate(
        [router_t[...], jnp.zeros((128 - n_experts, width), f32)], axis=0
    )
    high = table.astype(bf16).astype(f32)
    mid = (table - high).astype(bf16).astype(f32)
    low = table - high - mid
    table = high + pltpu.roll(mid, n_experts, 0) + pltpu.roll(low, 2 * n_experts, 0)
    w3_t[...] = table.astype(bf16)
    w3[...] = table.T.astype(bf16)
    first, second = routes_t[0:1, :], routes_t[1:2, :]
    eight = iota((8, rows), 0)
    named = jnp.where((first == eight) | (second == eight), 1.0, 0.0)
    upper = jnp.where(iota((rows, rows), 0) < iota((rows, rows), 1), 1.0, 0.0)
    rank = dot(named.astype(bf16), upper.astype(bf16), NN)
    slot = iota((CAP, rows), 0).astype(f32)
    for e in range(n_experts):
        hit = (named[e : e + 1] > 0.5) & (rank[e : e + 1] == slot)
        pick[e * CAP : (e + 1) * CAP, :] = jnp.where(hit, 1.0, 0.0).astype(bf16)
    all_pick = pick[...].astype(f32)
    valid = iota((1, rows), 1) < valid_rows(sc, rows)
    live = jnp.where(valid, all_pick, 0.0).astype(bf16)
    full[:, :width] = dot(live, dy[...], NN).astype(bf16)
    line = iota((128, rows), 0)
    kind = jnp.where(line < 3 * n_experts, lax.rem(line, n_experts), -1)
    pair = jnp.where((first == kind) | (second == kind), 1.0, 0.0).astype(bf16)
    full[:, width:] = dot(pick[...], pair, NT).astype(bf16)
    for k, piece in enumerate(pay):
        expert = lax.rem(lax.axis_index("exp") + k, n_experts)
        piece[...] = full[pl.ds(pl.multiple_of(expert * CAP, 16), CAP), :]


def head_index(n_heads):
    index = lax.axis_index("ctx") * lax.axis_size("exp") + lax.axis_index("exp")
    return lax.rem(index, n_heads)


def bias_tiles(rel, buckets, brow, tiles):
    n_tiles, side, _ = tiles.shape
    n_heads, n_buckets = rel.shape
    head = head_index(n_heads)
    ids = buckets[...]
    row = jnp.zeros(ids.shape, f32)
    for b in range(n_buckets):
        row = jnp.where(ids == b, rel[head, b], row)
    brow[:, :side] = jnp.zeros((1, side), f32)
    brow[:, side:] = row
    for o in range(n_tiles):
        wide = jnp.broadcast_to(brow[:, o * side : (o + 2) * side], (side, 2 * side))
        tiles[o] = pltpu.roll(wide, 0, axis=1, stride=1, stride_axis=0)[:, side:]


def at_tile(index, side):
    return index * side if isinstance(index, int) else pl.multiple_of(index * side, side)


def loop(count, body, state):
    if isinstance(count, int) and count <= 4:
        for i in range(count):
            state = body(i, state)
        return state
    return lax.fori_loop(0, count, body, state)


def attn_kernel(shifts, head_dim, sc, rel, *refs):
    n_pieces = len(shifts)
    pieces = refs[:n_pieces]
    gain, w_qkv, buckets = refs[n_pieces : n_pieces + 3]
    kept, (out_t, lse) = refs[n_pieces + 3 : n_pieces + 9], refs[n_pieces + 9 : n_pieces + 11]
    h1, qa, ka, va, qt, kt, vt, brow, tiles, window, weight, sem, sems = refs[n_pieces + 11 :]
    head = head_index(rel.shape[0])
    pair_at = pl.multiple_of((head // 2) * 6 * head_dim, 128)
    fetch = pltpu.make_async_copy(w_qkv.at[:, pl.ds(pair_at, 6 * head_dim)], window, sem)
    fetch.start()
    bias_tiles(rel, buckets, brow, tiles)
    n_exp = lax.axis_size("exp")
    n_x = lax.axis_size("ctx") // 2
    ctx, exp = lax.axis_index("ctx"), lax.axis_index("exp")

    def piece_start(b, o, k):
        if b < 0:
            return 0
        x_at = lax.rem(ctx // 2 + (n_x - b), n_x)
        core = lax.rem(lax.rem(ctx, 2) + o, 2)
        return ((x_at * 2 + core) * n_exp + lax.rem(exp + (n_exp - k), n_exp)) * 128

    n_tiles, side, _ = tiles.shape
    length = sc[0]

    def rows_in(x, start):
        x = x.astype(f32)
        h1[pl.ds(start, 128), :] = (x * norm_scale(x) * row_of(gain)).astype(bf16)

    def project(j, carry):
        group = 512
        start = at_tile(j, group)
        lane = iota((group, 128), 1)
        here = pl.ds(start, group)
        qkv = dot(h1[here, :], weight[...], NN).astype(bf16).astype(f32)
        q, k, v = qkv[:, :128] * 0.125, qkv[:, 128:256], qkv[:, 256:]
        live = jnp.where(start + iota((group, 128), 0) < length, 0.0, NEG)
        qa[here, :] = jnp.where(lane == head_dim, 1.0, q).astype(bf16)
        ka[here, :] = jnp.where(lane == head_dim, live, k).astype(bf16)
        va[here, :] = v.astype(bf16)
        qt[:, here] = q.T[:head_dim].astype(bf16)
        kt[:, here] = k.T[:head_dim].astype(bf16)
        vt[:, here] = v.T[:head_dim].astype(bf16)
        return carry

    for i, piece in enumerate(pieces):
        if piece.shape[0] == 128:
            rows_in(piece[...], pl.multiple_of(piece_start(*shifts[i]), 128))
        else:

            def step(j, carry, piece=piece):
                start = pl.multiple_of(j * 128, 128)
                rows_in(piece[pl.ds(start, 128), :], start)
                return carry

            lax.fori_loop(0, piece.shape[0] // 128, step, 0)
    fetch.wait()
    odd = lax.rem(head, 2) == 1
    for i in range(3):
        even_part = window[:, i * head_dim : (i + 1) * head_dim]
        odd_part = window[:, (3 + i) * head_dim : (4 + i) * head_dim]
        part = jnp.where(odd, odd_part.astype(f32), even_part.astype(f32)).astype(bf16)
        pad = jnp.zeros((window.shape[0], 128 - head_dim), bf16)
        weight[:, i * 128 : (i + 1) * 128] = jnp.concatenate([part, pad], axis=1)
    loop(h1.shape[0] // 512, project, 0)
    leave = [
        pltpu.make_async_copy(src, dst, sems.at[i])
        for i, (src, dst) in enumerate(zip((h1, qa, ka, va, qt, kt), kept))
    ]
    for copy in leave:
        copy.start()
    blocks = side // 128

    def one_query_tile(qi, carry):
        q_start = at_tile(qi, side)
        q = qa[pl.ds(q_start, side), :]

        def fold(k_start, offset, state, diagonal):
            top, total, acc = state
            scores = dot(ka[pl.ds(k_start, side), :], q, NT) + tiles[offset]
            if diagonal:
                scores = jnp.where(iota((side, side), 0) <= iota((side, side), 1), scores, NEG)
            new_top = jnp.maximum(top, jnp.max(scores, axis=0, keepdims=True))
            probs = jnp.exp(scores - new_top)
            scale = jnp.exp(top - new_top)
            total = total * scale + jnp.sum(probs, axis=0, keepdims=True)
            acc = acc * scale + dot(vt[:, pl.ds(k_start, side)], probs.astype(bf16), NN)
            return new_top, total, acc

        state = (
            jnp.full((1, side), NEG, f32),
            jnp.zeros((1, side), f32),
            jnp.zeros((head_dim, side), f32),
        )
        state = fold(q_start, 0, state, True)

        def earlier(kj, state):
            return fold(at_tile(kj, side), qi - kj, state, False)

        top, total, acc = loop(qi, earlier, state)
        result = (acc / total).astype(bf16)
        lse[:, pl.ds(q_start, side)] = top + jnp.log(total)
        for b in range(blocks):
            out_t[qi * blocks + b] = result[:, b * 128 : (b + 1) * 128]
        return carry

    loop(n_tiles, one_query_tile, 0)
    for copy in leave:
        copy.wait()


def attn_back_kernel(head_dim, n_dp, rel, *refs):
    qa, ka, va, qt, kt, out_t, grad_t, lse, h1_far, buckets, small = refs[:11]
    pay, weight_pay = refs[11:13]
    dq, dk, dv, full, brow, tiles, sums, diag, h1, sem = refs[13:]
    fetch = pltpu.make_async_copy(h1_far, h1, sem)
    fetch.start()
    n_tiles, side, _ = tiles.shape
    blocks = side // 128
    bias_tiles(rel, buckets, brow, tiles)
    sums[...] = jnp.zeros_like(sums)
    dk[...] = jnp.zeros_like(dk)
    dv[...] = jnp.zeros_like(dv)

    def one_query_tile(qi, carry):
        q_start = at_tile(qi, side)
        q = qa[pl.ds(q_start, side), :]
        q_t = qt[:, pl.ds(q_start, side)]
        g_t = jnp.concatenate([grad_t[qi * blocks + b] for b in range(blocks)], axis=1)
        o_t = jnp.concatenate([out_t[qi * blocks + b] for b in range(blocks)], axis=1)
        row_dots = jnp.sum(g_t.astype(f32) * o_t.astype(f32), axis=0, keepdims=True)
        norm = lse[:, pl.ds(q_start, side)]

        def fold(k_start, offset, acc, diagonal):
            where_k = pl.ds(k_start, side)
            scores = dot(ka[where_k, :], q, NT) + tiles[offset]
            probs = jnp.exp(scores - norm)
            if diagonal:
                probs = jnp.where(iota((side, side), 0) <= iota((side, side), 1), probs, 0.0)
            grad_prob = dot(va[where_k, :][:, :head_dim], g_t, NN)
            grad_score = probs * (grad_prob - row_dots)
            low = grad_score.astype(bf16)
            sums[offset] = sums[offset] + grad_score
            dv[:, where_k] = dv[:, where_k] + dot(g_t, probs.astype(bf16), NT)
            dk[:, where_k] = dk[:, where_k] + dot(q_t, low, NT)
            return acc + dot(kt[:, where_k], low, NN)

        acc = fold(q_start, 0, jnp.zeros((head_dim, side), f32), True)

        def earlier(kj, acc):
            return fold(at_tile(kj, side), qi - kj, acc, False)

        dq[:, pl.ds(q_start, side)] = loop(qi, earlier, acc)
        return carry

    loop(n_tiles, one_query_tile, 0)
    full[:head_dim, :] = (dq[...] * 0.125).astype(bf16)
    full[head_dim : 2 * head_dim, :] = dk[...].astype(bf16)
    full[2 * head_dim :, :] = dv[...].astype(bf16)
    for b in range(pay.shape[0]):
        pay[b] = full[:, b * 128 : (b + 1) * 128]
    flip = jnp.where(iota((128, 128), 0) + iota((128, 128), 1) == 127, 1.0, 0.0).astype(bf16)
    diag[...] = jnp.zeros_like(diag)
    for o in range(n_tiles):
        for a in range(blocks):
            turned = dot(flip, sums[o, a * 128 : (a + 1) * 128, :].astype(bf16), NN)
            wide = jnp.concatenate([turned, jnp.zeros((128, 128), f32)], axis=1)
            lined = pltpu.roll(wide, 0, axis=1, stride=1, stride_axis=0)
            first = (o + 1) * side - (a + 1) * 128
            where_d = slice(first, first + side + 128)
            diag[:, where_d] = diag[:, where_d] + jnp.sum(lined, axis=0, keepdims=True)
    ids = jnp.concatenate([buckets[...], jnp.full((1, side), -1, jnp.int32)], axis=1)
    ids = pltpu.roll(ids, side - 1, 1)
    hot = jnp.where(ids == iota((128, ids.shape[1]), 0), 1.0, 0.0).astype(bf16)
    high, low = split2(jnp.broadcast_to(diag[...], (8, diag.shape[1])))
    rel_grad = dot(high, hot, NT) + dot(low, hot, NT)
    fetch.wait()
    grad_w = dot(full[...], h1[...], NN).astype(bf16)
    n_pay, pay_rows, lanes = weight_pay.shape
    n_ctx = n_pay // n_dp
    rows = grad_w.shape[0] // n_ctx
    rel_row = jnp.concatenate([rel_grad, jnp.zeros((8, lanes - 128), f32)], axis=1)
    line = iota((16, lanes), 0)
    for d in range(n_dp):
        for c in range(n_ctx):
            here = slice(d * lanes, (d + 1) * lanes)
            weight_pay[d * n_ctx + c, :rows, :] = grad_w[c * rows : (c + 1) * rows, here]
            extra = jnp.where(line == 0, rel_row[0:1], 0.0)
            if c < 4:
                for r in range(2):
                    row = small[2 * c + r : 2 * c + r + 1, here]
                    extra = jnp.where(line == 8 + r, row, extra)
            weight_pay[d * n_ctx + c, rows:, :] = extra.astype(bf16)


def middle_kernel(n_heads, sc, recv, w_out, x, gain, pick, middle, *send):
    rows, width = x.shape
    attn_t = jnp.concatenate([recv[h] for h in range(n_heads)], axis=0)
    branch = dot(attn_t, w_out[...], TN)
    valid = iota((rows, 1), 0) < valid_rows(sc, rows)
    mid = x[...].astype(f32) + jnp.where(valid, branch, 0.0)
    middle[...] = mid
    h2 = (mid * norm_scale(mid) * row_of(gain)).astype(bf16)
    for k, piece in enumerate(send):
        expert = lax.rem(lax.axis_index("exp") + k, len(send))
        chosen = pick[pl.ds(pl.multiple_of(expert * CAP, 16), CAP), :]
        piece[...] = dot(chosen, h2, NN).astype(bf16)


def gate_of(h2, pay, width, w3, own):
    logits = dot(h2, w3, NN)
    sel = 2.0 * own - pay[:, width:].astype(f32)
    diff = jnp.sum(logits * sel, axis=1, keepdims=True)
    return 1.0 / (1.0 + jnp.exp(-diff)), sel


def own_lanes(expert, n_experts):
    lane = iota((1, 128), 1)
    return jnp.where((lane < 3 * n_experts) & (lane % n_experts == expert), 1.0, 0.0)


def expert_kernel(n_experts, h2, pay, w3, w3_t, w_up, w_down, *refs):
    mix, back = refs[:n_experts], refs[n_experts : 2 * n_experts]
    router, z_acc, in_acc, dz, gates, rows_out = refs[2 * n_experts :]
    step = pl.program_id(0)
    width = h2.shape[1]
    expert = lax.axis_index("exp")
    own = own_lanes(expert, n_experts)

    @pl.when(step == 0)
    def _():
        gate, _ = gate_of(h2[...], pay, width, w3[...], own)
        gates[...] = jnp.broadcast_to(gate, gates.shape)
        dz[...] = (gate * pay[:, :width].astype(f32)).astype(bf16)
        z_acc[...] = jnp.zeros_like(z_acc)
        in_acc[...] = jnp.zeros_like(in_acc)

    up = dot(h2[...], w_up[...], NN)
    act, slope = gelu_parts(up)
    grad_hidden = dot(dz[...], w_down[...], NT)
    grad_up = (grad_hidden * slope).astype(bf16)
    z_acc[...] += dot(act.astype(bf16), w_down[...], NN)
    in_acc[...] += dot(grad_up, w_up[...], NT)

    @pl.when(step == pl.num_programs(0) - 1)
    def _():
        gate = gates[:, 0:1]
        sel = 2.0 * own - pay[:, width:].astype(f32)
        z = z_acc[...].astype(bf16).astype(f32)
        rows_out[...] = (gate * z).astype(bf16)
        for k in range(n_experts):
            mix[k][...] = rows_out[k * CAP : (k + 1) * CAP, :]
        grad_gate = jnp.sum(pay[:, :width].astype(f32) * z, axis=1, keepdims=True)
        high, low = split2((gate * (1.0 - gate) * grad_gate) * sel)
        total = in_acc[...] + dot(high, w3_t[...], NN) + dot(low, w3_t[...], NN)
        rows_out[...] = total.astype(bf16)
        for k in range(n_experts):
            back[k][...] = rows_out[k * CAP : (k + 1) * CAP, :]
        router[...] = (dot(high, h2[...], TN) + dot(low, h2[...], TN))[:8]


def collect(pieces, pick):
    n_experts = len(pieces)
    total = None
    for k, piece in enumerate(pieces):
        expert = lax.rem(lax.axis_index("exp") + k, n_experts)
        chosen = pick[pl.ds(pl.multiple_of(expert * CAP, 16), CAP), :]
        part = dot(chosen, piece[...], TN)
        total = part if total is None else total + part
    return total


def middle_back_kernel(n_heads, n_experts, sc, *refs):
    back = refs[:n_experts]
    pick, middle, dy, gain, recv, w_out, router, dmid, grad_t, red, small = refs[n_experts:]
    rows, width = middle.shape
    grad_h2 = collect(back, pick)
    grad_in, xhat = norm_back(middle[...], row_of(gain), grad_h2)
    grad_mid = dy[...].astype(f32) + grad_in
    dmid[...] = grad_mid
    valid = iota((rows, 1), 0) < valid_rows(sc, rows)
    branch = jnp.where(valid, grad_mid, 0.0).astype(bf16)
    attn_t = jnp.concatenate([recv[h] for h in range(n_heads)], axis=0)
    heads = dot(w_out[...], branch, NT).astype(bf16)
    head_dim = width // n_heads
    for h in range(n_heads):
        grad_t[h] = heads[h * head_dim : (h + 1) * head_dim]
    for h in range(n_heads, grad_t.shape[0]):
        grad_t[h] = jnp.zeros((head_dim, rows), bf16)
    red[...] = dot(attn_t, branch, NN).astype(bf16)
    gains = jnp.sum(grad_h2 * xhat, axis=0, keepdims=True)
    line = iota((8, width), 0)
    moved = pltpu.roll(router[...], 1, 0)
    small[...] = jnp.where(line == 0, gains, jnp.where(line < 5, moved, 0.0))


def output_kernel(n_experts, sc, *refs):
    mix = refs[:n_experts]
    pick, middle, out = refs[n_experts:]
    rows = middle.shape[0]
    valid = iota((rows, 1), 0) < valid_rows(sc, rows)
    total = collect(mix, pick)
    out[...] = (middle[...] + jnp.where(valid, total, 0.0)).astype(bf16)


def token_grad_kernel(n_heads, recv, w_qkv, x, gain, dmid, out):
    grad_t = jnp.concatenate([recv[h] for h in range(n_heads)], axis=0)
    grad_h1 = dot(w_qkv[...], grad_t, NN).T
    grad_in, _ = norm_back(x[...].astype(f32), row_of(gain), grad_h1)
    out[...] = dmid[...] + grad_in


def load_rows(h_pieces, where, pays, h2, pay, sem):
    rows = h_pieces[0].shape[0]
    copies = []
    for i, piece in enumerate(h_pieces):
        here = pl.ds(i * rows, rows)
        source = pays[i] if len(pays) > 1 else pays[0].at[
            pl.ds(pl.multiple_of(where[i] * rows, 16), rows), :
        ]
        copies.append(pltpu.make_async_copy(piece, h2.at[here, :], sem.at[0, i]))
        copies.append(pltpu.make_async_copy(source, pay.at[here, :], sem.at[1, i]))
    return copies


def chip_index(a, b, o):
    n_dp = lax.axis_size("dp")
    n_x = lax.axis_size("ctx") // 2
    dp, ctx = lax.axis_index("dp"), lax.axis_index("ctx")
    core = lax.rem(lax.rem(ctx, 2) + o, 2)
    x_at = lax.rem(ctx // 2 + (n_x - b), n_x)
    return (lax.rem(dp + (n_dp - a), n_dp) * n_x + x_at) * 2 + core


def weight_grad_kernel(n_experts, keys, together, last, sc, *refs):
    n_pieces = len(keys)
    h_pieces = refs[:n_pieces]
    n_in = n_pieces + (1 if last else n_pieces)
    pays = refs[n_pieces:n_in]
    w3, w_up, w_down = refs[n_in : n_in + 3]
    if last:
        up_base, down_base, up_out, down_out, low = refs[n_in + 3 : n_in + 8]
    else:
        up_out, down_out = refs[n_in + 3 : n_in + 5]
    h2, pay, dz, hid_t, dup_t, sem = refs[-6:]
    step = pl.program_id(0)
    rows = h_pieces[0].shape[0]
    width = h2.shape[1]
    block = w_down.shape[0]
    copies = load_rows(h_pieces, [chip_index(*key) for key in keys], pays, h2, pay, sem)

    @pl.when(step == 0)
    def _():
        for copy in copies:
            copy.start()

    own = own_lanes(lax.axis_index("exp"), n_experts)
    up_t = w_up[...].T
    down = w_down[...]
    chunk = together * rows
    for i in range(n_pieces // together):
        here = slice(i * chunk, (i + 1) * chunk)

        @pl.when(step == 0)
        def _(i=i, here=here):
            for copy in copies[2 * together * i : 2 * together * (i + 1)]:
                copy.wait()
            part = pay[here, :]
            gate, _ = gate_of(h2[here, :], part, width, w3[...], own)
            dz[here, :] = (gate * part[:, :width].astype(f32)).astype(bf16)

        act, slope = gelu_parts(dot(up_t, h2[here, :], NT))
        hid_t[:, here] = act.astype(bf16)
        dup_t[:, here] = (dot(down, dz[here, :], NT) * slope).astype(bf16)
    grad_up = dot(dup_t[...], h2[...], NN)
    grad_down = dot(hid_t[...], dz[...], NN)
    if last:
        grad_up = grad_up + up_base[...]
        grad_down = grad_down + down_base[...]
        low[:block, :] = grad_up.astype(bf16)
        low[block:, :] = grad_down.astype(bf16)
        up_out[...] = grad_up.T
    else:
        up_out[...] = grad_up
    down_out[...] = grad_down


def fill_kernel(sc, low, *refs):
    up_out, down_out = refs[-2:]
    block = down_out.shape[0]
    up_out[...] = low[:block, :].astype(f32).T
    down_out[...] = low[block:, :].astype(f32)


def assemble_kernel(keys, rows, n_groups, head_cols, *refs):
    n_pieces = len(keys)
    pieces = refs[:n_pieces]
    w_qkv, gain, grad, gain_grad, rel_grad, gain2_grad, router_grad = refs[
        n_pieces : n_pieces + 7
    ]
    turned, rel_t, stage, acc, sem = refs[n_pieces + 7 :]
    lanes = pieces[0].shape[-1]
    acc[...] = jnp.zeros_like(acc)
    n_dp, n_exp = lax.axis_size("dp"), lax.axis_size("exp")
    n_x = lax.axis_size("ctx") // 2
    dp, ctx, exp = (lax.axis_index(name) for name in ("dp", "ctx", "exp"))
    rel_t[...] = jnp.zeros_like(rel_t)
    for piece, ids in zip(pieces, keys):
        for i, (a, b, o, k) in enumerate(ids):
            d = lax.rem(dp + (n_dp - a), n_dp)
            c = lax.rem(ctx // 2 + (n_x - b), n_x) * 2 + lax.rem(lax.rem(ctx, 2) + o, 2)
            e = lax.rem(exp + (n_exp - k), n_exp)
            lane_at = pl.multiple_of(d * lanes, 128)
            for g in range(n_groups):
                head = g * n_exp + e
                row_at = pl.multiple_of(head * head_cols + c * rows, 16)
                turned[pl.ds(row_at, rows), pl.ds(lane_at, lanes)] = piece[
                    i, g * rows : (g + 1) * rows, :
                ]
                rel_t[pl.ds(head, 1), :] = piece[
                    i, n_groups * rows + g : n_groups * rows + g + 1, :128
                ].astype(f32)
            first = n_groups * rows + 8
            where_s = pl.ds(lane_at, lanes)
            small = piece[i, first : first + 8, :].astype(f32)
            acc[c, :, where_s] = acc[c, :, where_s] + small
    rel_grad[...] = rel_t[: rel_grad.shape[0], : rel_grad.shape[1]]
    width, columns = grad.shape
    gain2_grad[...] = acc[0, 0:1, :].reshape(width)
    for e in range(router_grad.shape[0]):
        router_grad[e : e + 1, :] = acc[(e + 1) // 2, (e + 1) % 2 : (e + 1) % 2 + 1, :]
    copies = []
    for i, a in enumerate(range(0, width, 128)):
        total = jnp.zeros((128, 128), f32)
        for b in range(0, columns, 128):
            tile = turned[b : b + 128, a : a + 128].astype(f32).T
            stage[a : a + 128, b : b + 128] = tile
            total = total + tile * w_qkv[a : a + 128, b : b + 128].astype(f32)
        where_a = pl.ds(a, 128)
        copy = pltpu.make_async_copy(stage.at[where_a, :], grad.at[where_a, :], sem.at[i])
        copy.start()
        copies.append(copy)
        sums = jnp.sum(total.T, axis=0, keepdims=True)
        sums = sums / gain[a : a + 128].reshape(1, 128)
        gain_grad[a : a + 128] = sums.reshape(128)
    for copy in copies:
        copy.wait()


def shard_kernel(n_dp, n_groups, summed, shard):
    n_ctx = summed.shape[0] // n_dp
    part = summed.shape[1] - 16
    line = iota((16, summed.shape[2]), 0)
    extra = jnp.zeros(line.shape, f32)
    for i in range(summed.shape[0]):
        extra = extra + summed[i, part:, :].astype(f32)
    extra = jnp.where(line >= 8, extra, 0.0)
    for g in range(n_groups):
        total = summed[g].astype(f32)
        for d in range(1, n_dp):
            total = total + summed[d * n_ctx + g].astype(f32)
        shard[0, g * part : (g + 1) * part, :] = total[:part].astype(bf16)
        extra = jnp.where(line == g, total[part : part + 1], extra)
    shard[0, n_groups * part :, :] = extra.astype(bf16)


def reduced_kernel(red, attn_out):
    attn_out[...] = red[...].astype(f32)


def after(value, *others):
    return lax.optimization_barrier((value, others))[0]


def on_device(
    n_dp,
    n_ctx,
    n_exp,
    tokens,
    lengths,
    routes,
    buckets,
    cotangent,
    attn_gain,
    w_qkv,
    w_attn_out,
    rel_bias,
    ffn_gain,
    w_router,
    w_up,
    w_down,
):
    x = tokens[0]
    dy = cotangent[0]
    rows, width = x.shape
    seq = buckets.shape[0]
    n_buckets, n_heads = rel_bias.shape
    head_dim = width // n_heads
    n_experts = w_router.shape[1]
    ff = w_up.shape[2]
    n_slot = n_ctx * n_exp
    n_groups = n_heads // n_exp
    n_x = n_ctx // 2
    small = n_x == 2 and n_dp == 2
    side = 512 if seq <= 2048 else 256
    n_tiles = seq // side
    slot_rows = n_experts * CAP
    slot_axes, all_chips = ("ctx", "exp"), ("dp", "ctx")

    def ring(v, shift):
        return lax.ppermute(v, "exp", [(i, (i + shift) % n_exp) for i in range(n_exp)])

    def swap(v):
        return lax.ppermute(v, "ctx", [(i, i ^ 1) for i in range(n_ctx)])

    def chips(v, a, b):
        perm = []
        for d in range(n_dp):
            for c in range(n_ctx):
                to = ((d + a) % n_dp) * n_ctx + ((c // 2 + b) % n_x) * 2 + c % 2
                perm.append((d * n_ctx + c, to))
        return lax.ppermute(v, all_chips, perm)

    def exchange(v, axes):
        return lax.all_to_all(v, axes, split_axis=0, concat_axis=0, tiled=True)

    def to_experts(parts):
        return [parts[0]] + [ring(parts[k], k) for k in range(1, n_exp)]

    def from_experts(parts):
        return [parts[0]] + [ring(parts[k], n_exp - k) for k in range(1, n_exp)]

    keys = [(a, b, o) for o in (0, 1) for a, b in ((0, 0), (0, 1), (1, 0), (1, 1))]

    with jax.named_scope("routing"):
        places, pick, w3, w3_t, _, *pay = call(
            functools.partial(route_kernel, n_experts),
            [
                sds((1,), jnp.int32),
                sds((slot_rows, rows), bf16),
                sds((width, 128), bf16),
                sds((128, width), bf16),
                sds((slot_rows, width + 128), bf16),
            ]
            + [sds((CAP, width + 128), bf16)] * n_experts,
            [smem()] + [vmem()] * 3,
            name="routing",
        )(lengths, routes[0].T, dy, w_router.T)

    with jax.named_scope("gather_tokens"):
        if small:
            column = [(x, 0, 0), (ring(after(x, pick), 1), 0, 1)]
            column += [(ring(x, k), 0, k) for k in range(2, n_exp)]
            onward = [v for v, _, _ in column]
            onward[-1] = after(onward[-1], pay)
            pieces = column + [(chips(v, 0, 1), 1, k) for k, v in enumerate(onward)]
            pieces = [(v, b, 0, k) for v, b, k in pieces]
            arrived = to_experts(after(pay, pieces[-1][0]))
            pieces = pieces + [(swap(v), b, 1, k) for v, b, _, k in pieces]
            blocks = [v for v, _, _, _ in pieces]
            shifts = [ids for _, *ids in pieces]
        else:
            blocks = [lax.all_gather(x, slot_axes, axis=0, tiled=True)]
            shifts = [(-1, 0, 0)]
            arrived = to_experts(pay)

    with jax.named_scope("attention"):
        bucket_row = buckets.reshape(1, seq)
        blocks[-1] = after(blocks[-1], bucket_row)
        attn_outs = (
            sds((seq, width), bf16),
            sds((seq, 128), bf16),
            sds((seq, 128), bf16),
            sds((seq, 128), bf16),
            sds((head_dim, seq), bf16),
            sds((head_dim, seq), bf16),
            sds((n_slot, head_dim, 128), bf16),
            sds((1, seq), f32),
        )
        any_spec = pl.BlockSpec(memory_space=pl.ANY)
        h1, qa, ka, va, qt, kt, out_t, lse = call(
            functools.partial(attn_kernel, shifts, head_dim),
            attn_outs,
            [smem(), smem()] + [vmem()] * (len(blocks) + 1) + [any_spec, vmem()],
            [pltpu.VMEM(o.shape, o.dtype) for o in attn_outs[:6]]
            + [
                pltpu.VMEM((head_dim, seq), bf16),
                pltpu.VMEM((1, seq + side), f32),
                pltpu.VMEM((n_tiles, side, side), f32),
                pltpu.VMEM((width, 6 * head_dim), bf16),
                pltpu.VMEM((width, 384), bf16),
                pltpu.SemaphoreType.DMA,
                pltpu.SemaphoreType.DMA((6,)),
            ],
            micros=10,
            name="attention",
            limit=58,
            out_specs=(any_spec,) * 6 + (vmem(),) * 2,
        )(lengths, rel_bias.T, *blocks, attn_gain, w_qkv, bucket_row)
        attn_in = exchange(out_t, slot_axes)
        pay_in = jnp.concatenate([arrived[0]] + [after(v, out_t) for v in arrived[1:]])

    with jax.named_scope("middle"):
        piece_shape = sds((CAP, width), bf16)
        middle, *send = call(
            functools.partial(middle_kernel, n_heads),
            [sds((rows, width), f32)] + [piece_shape] * n_experts,
            [smem()] + [vmem()] * 5,
            name="middle",
        )(lengths, attn_in, w_attn_out, x, ffn_gain, pick)
        h2_in = jnp.concatenate(to_experts(send))

    with jax.named_scope("experts"):
        block = 1024
        row_spec = pl.BlockSpec((slot_rows, width), lambda i: (0, 0))
        piece_spec = pl.BlockSpec((CAP, width), lambda i: (0, 0))
        *parts, router = pl.pallas_call(
            functools.partial(expert_kernel, n_experts),
            out_shape=[piece_shape] * (2 * n_experts)
            + [sds((8, width), f32)],
            grid_spec=pltpu.PrefetchScalarGridSpec(
                num_scalar_prefetch=0,
                grid=(ff // block,),
                in_specs=[
                    row_spec,
                    pl.BlockSpec((slot_rows, width + 128), lambda i: (0, 0)),
                    pl.BlockSpec((width, 128), lambda i: (0, 0)),
                    pl.BlockSpec((128, width), lambda i: (0, 0)),
                    pl.BlockSpec((width, block), lambda i: (0, i)),
                    pl.BlockSpec((block, width), lambda i: (i, 0)),
                ],
                out_specs=[piece_spec] * (2 * n_experts)
                + [pl.BlockSpec((8, width), lambda i: (0, 0))],
                scratch_shapes=[
                    pltpu.VMEM((slot_rows, width), f32),
                    pltpu.VMEM((slot_rows, width), f32),
                    pltpu.VMEM((slot_rows, width), bf16),
                    pltpu.VMEM((slot_rows, 128), f32),
                    pltpu.VMEM((slot_rows, width), bf16),
                ],
            ),
            compiler_params=params(),
            cost_estimate=cost_of(12),
            name="experts",
        )(h2_in, pay_in, w3, w3_t, w_up[0], w_down[0])
        mix_parts, back_parts = parts[:n_experts], parts[n_experts:]
        back_in = from_experts(back_parts)

    shares = n_dp * n_ctx
    with jax.named_scope("expert_weight_grads"):
        if small:
            pay_all = lax.all_gather(pay_in, all_chips, axis=0, tiled=True)
            beside = [chips(h2_in, a, b) for a, b in ((0, 1), (1, 0), (1, 1))]
            block = 512
            n_parts = ff // (2 * block)
            full_shapes = [sds((width, ff), f32), sds((ff, width), f32)]

            def half_specs(other):
                def at(i, s):
                    return (1 - s[0] if other else s[0]) * n_parts + i

                return (
                    pl.BlockSpec((width, block), lambda i, s: (0, at(i, s))),
                    pl.BlockSpec((block, width), lambda i, s: (at(i, s), 0)),
                )

            low_spec = pl.BlockSpec((2 * block, width), lambda i, s: (i, 0))

            base_spec = pl.BlockSpec((block, width), lambda i, s: (i, 0))
            base_shape = sds((ff // 2, width), f32)

            def weight_half(pieces, pays, keys, base, micros):
                specs = half_specs(False)
                count = len(pieces) * slot_rows
                shapes, outs = [base_shape] * 2, [base_spec] * 2
                if base:
                    shapes, outs = full_shapes + [sds((ff, width), bf16)], [*specs, low_spec]
                return pl.pallas_call(
                    functools.partial(weight_grad_kernel, n_experts, keys, 2, bool(base)),
                    out_shape=shapes,
                    grid_spec=pltpu.PrefetchScalarGridSpec(
                        num_scalar_prefetch=1,
                        grid=(n_parts,),
                        in_specs=[any_spec] * (len(pieces) + len(pays))
                        + [pl.BlockSpec((width, 128), lambda i, s: (0, 0)), *specs]
                        + [base_spec] * len(base),
                        out_specs=outs,
                        scratch_shapes=[
                            pltpu.VMEM((count, width), bf16),
                            pltpu.VMEM((count, width + 128), bf16),
                            pltpu.VMEM((count, width), bf16),
                            pltpu.VMEM((block, count), bf16),
                            pltpu.VMEM((block, count), bf16),
                            pltpu.SemaphoreType.DMA((2, len(pieces))),
                        ],
                    ),
                    compiler_params=params(),
                    cost_estimate=cost_of(micros),
                    name="weight_grads",
                )(places, *pieces, *pays, w3, w_up[0], w_down[0], *base)

            def weight_fill(low, grads):
                return pl.pallas_call(
                    fill_kernel,
                    out_shape=full_shapes,
                    grid_spec=pltpu.PrefetchScalarGridSpec(
                        num_scalar_prefetch=1,
                        grid=(n_parts,),
                        in_specs=[low_spec, any_spec, any_spec],
                        out_specs=half_specs(True),
                    ),
                    input_output_aliases={2: 0, 3: 1},
                    compiler_params=params(),
                    cost_estimate=cost_of(8),
                    name="fill",
                )(places, low, *grads)


            pays = [pay_in, swap(pay_in)]
            base = weight_half([h2_in, swap(h2_in)], pays, keys[::4], (), 11)
            back_in[0] = after(back_in[0], beside, base, pay_all)

    with jax.named_scope("middle_back"):
        dmid, grad_t, red, sums = call(
            functools.partial(middle_back_kernel, n_heads, n_experts),
            (
                sds((rows, width), f32),
                sds((n_slot, head_dim, rows), bf16),
                sds((width, width), bf16),
                sds((8, width), f32),
            ),
            [smem()] + [vmem()] * (7 + n_experts),
            name="middle_back",
        )(lengths, *back_in, pick, middle, dy, ffn_gain, attn_in, w_attn_out, router)
        grad_in = exchange(grad_t, slot_axes)

    if small:
        with jax.named_scope("expert_weight_grads"):
            beside = [after(v, grad_t) for v in beside]
            pieces = beside + [swap(v) for v in beside]
            *grads, low = weight_half(pieces, [pay_all], keys[1:4] + keys[5:], base, 8)
            share = lax.psum_scatter(red, all_chips, scatter_dimension=0, tiled=True)
            grad_in = after(grad_in, low, share)
            others = [ring(share, k) for k in range(1, n_exp)]

    with jax.named_scope("attention_back"):
        part = 3 * head_dim // n_ctx
        lanes = width // n_dp
        dqkv, weight_pay = call(
            functools.partial(attn_back_kernel, head_dim, n_dp),
            (sds((n_slot, 3 * head_dim, rows), bf16), sds((shares, part + 16, lanes), bf16)),
            [smem()] + [vmem()] * 8 + [any_spec, vmem(), vmem()],
            [
                pltpu.VMEM((head_dim, seq), f32),
                pltpu.VMEM((head_dim, seq), f32),
                pltpu.VMEM((head_dim, seq), f32),
                pltpu.VMEM((3 * head_dim, seq), bf16),
                pltpu.VMEM((1, seq + side), f32),
                pltpu.VMEM((n_tiles, side, side), f32),
                pltpu.VMEM((n_tiles, side, side), f32),
                pltpu.VMEM((1, seq + side), f32),
                pltpu.VMEM((seq, width), bf16),
                pltpu.SemaphoreType.DMA,
            ],
            micros=11,
            name="attention_back",
            limit=58,
        )(rel_bias.T, qa, ka, va, qt, kt, out_t, grad_in, lse, h1, bucket_row, sums)
        if small:
            weight_pay = after(weight_pay, others)
            share = share.astype(f32) + others[0] + others[1] + others[2]
            share = after(share, weight_pay).astype(bf16)
        else:
            mix_in = from_experts(mix_parts)
        summed = exchange(weight_pay, all_chips)
        if small:
            summed = after(summed, share)

    with jax.named_scope("projection_grad"):
        shard = call(
            functools.partial(shard_kernel, n_dp, n_groups),
            sds((1, n_groups * part + 16, lanes), bf16),
            [vmem()],
            name="shard",
        )(summed)
        if small:
            column = [ring(shard, k) for k in range(1, n_exp)]
            column = jnp.concatenate([shard] + column)
            low_in = swap(after(low, weight_pay))
            column = after(column, low_in)
            mix_in = from_experts([after(v, column) for v in mix_parts])


    if small:
        with jax.named_scope("expert_weight_grads"):
            grad_up, grad_down = weight_fill(low_in, grads)
    else:
        with jax.named_scope("expert_weight_grads"):
            own = own_lanes(lax.axis_index("exp"), n_experts)
            gate, _ = gate_of(h2_in, pay_in, width, w3, own)
            dz = (gate * pay_in[:, :width].astype(f32)).astype(bf16)
            act, slope = gelu_parts(dot(h2_in, w_up[0], NN))
            dup = (dot(dz, w_down[0], NT) * slope).astype(bf16)
            grad_up = lax.psum(dot(h2_in, dup, TN).astype(bf16), all_chips).astype(f32)
            grad_down = lax.psum(dot(act.astype(bf16), dz, TN).astype(bf16), all_chips)
            grad_down = grad_down.astype(f32)

    with jax.named_scope("output"):
        output = call(
            functools.partial(output_kernel, n_experts),
            sds((rows, width), bf16),
            [smem()] + [vmem()] * (2 + n_experts),
            micros=0.2,
            name="output",
        )(lengths, *mix_in, pick, middle)

    with jax.named_scope("token_grads"):
        if small:
            beside_x = chips(column, 0, 1)
            dqkv = after(dqkv, beside_x)
        dqkv_in = exchange(dqkv, slot_axes)
        grad_tokens = call(
            functools.partial(token_grad_kernel, n_heads),
            sds((rows, width), f32),
            [vmem()] * 5,
            name="token_grads",
        )(dqkv_in, w_qkv, x, attn_gain, dmid)

    with jax.named_scope("output_projection_grad"):
        if small:
            reduced = lax.all_gather(share, all_chips, axis=0, tiled=True)
        else:
            reduced = lax.psum(red, ("dp", "ctx", "exp"))
            sums = lax.psum(sums, ("dp", "ctx", "exp"))
            grad_ffn_gain, grad_router = sums[0], sums[1 : 1 + n_experts].T
        grad_attn_out = call(
            reduced_kernel,
            sds((width, width), f32),
            [vmem()],
            micros=0.2,
            name="reduced",
        )(reduced)

    with jax.named_scope("projection_grad"):
        if small:
            wide = [(column, 0, 0, range(n_exp))]
            wide.append((beside_x, 0, 1, range(n_exp)))
            wide.append((chips(column, 1, 0), 1, 0, range(n_exp)))
            wide.append((chips(beside_x, 1, 0), 1, 1, range(n_exp)))
            early = (grad_up, grad_down, grad_attn_out, mix_in)
            wide = [(after(v, early), a, b, ks) for v, a, b, ks in wide]
            final = [v for v, _, _, _ in wide] + [swap(v) for v, _, _, _ in wide]
            keys = [[(a, b, o, k) for k in ks] for o in (0, 1) for _, a, b, ks in wide]
            grad_qkv, grad_attn_gain, grad_rel, grad_ffn_gain, grad_router = call(
                functools.partial(assemble_kernel, keys, part, n_groups, 3 * head_dim),
                (
                    sds((width, 3 * width), f32),
                    sds((width,), f32),
                    sds((n_heads, n_buckets), f32),
                    sds((width,), f32),
                    sds((n_experts, width), f32),
                ),
                [vmem()] * (len(final) + 2),
                [
                    pltpu.VMEM((3 * width, width), bf16),
                    pltpu.VMEM((128, 128), f32),
                    pltpu.VMEM((width, 3 * width), f32),
                    pltpu.VMEM((n_ctx, 8, width), f32),
                    pltpu.SemaphoreType.DMA((width // 128,)),
                ],
                micros=6,
                name="assemble",
                limit=32,
                out_specs=(any_spec,) + (vmem(),) * 4,
            )(*final, w_qkv, attn_gain)
            grad_rel, grad_router = grad_rel.T, grad_router.T
        else:
            every = lax.all_gather(shard[0], ("dp", "ctx", "exp"), axis=0, tiled=False)
            every = every.reshape(n_dp, n_ctx, n_exp, n_groups * part + 16, lanes).astype(f32)
            main = every[:, :, :, : n_groups * part]
            main = main.reshape(n_dp, n_ctx, n_exp, n_groups, part, lanes)
            grad_qkv = main.transpose(0, 5, 3, 2, 1, 4).reshape(width, 3 * width)
            rel_rows = every[0, 0, :, n_groups * part : n_groups * (part + 1), :n_buckets]
            grad_rel = rel_rows.transpose(2, 1, 0).reshape(n_buckets, n_heads)
            grad_attn_gain = jnp.sum(grad_qkv * w_qkv.astype(f32), axis=1) / attn_gain

    return (
        output[None],
        grad_tokens[None],
        grad_attn_gain,
        grad_qkv,
        grad_attn_out,
        grad_rel,
        grad_ffn_gain,
        grad_router,
        grad_up[None],
        grad_down[None],
    )


def solution(mesh):
    sizes = dict(mesh.shape)
    by_token = P("dp", ("ctx", "exp"), None)
    by_expert = P("exp", None, None)
    return jax.shard_map(
        functools.partial(on_device, sizes["dp"], sizes["ctx"], sizes["exp"]),
        mesh=mesh,
        in_specs=(
            by_token,
            P("dp"),
            by_token,
            P(),
            by_token,
            P(),
            P(),
            P(),
            P(),
            P(),
            P(),
            by_expert,
            by_expert,
        ),
        out_specs=(
            by_token,
            by_token,
            P(),
            P(),
            P(),
            P(),
            P(),
            P(),
            by_expert,
            by_expert,
        ),
        check_vma=False,
    )
```

```python
import functools

import jax
import jax.numpy as jnp
from jax import lax
from jax.experimental import pallas as pl
from jax.experimental.pallas import tpu as pltpu
from jax.sharding import PartitionSpec as P

CAP = 80
EPS = 1e-06
NEG = -1e30
VMEM_LIMIT = 58 << 20
bf16 = jnp.bfloat16
f32 = jnp.float32
NN = ((1,), (0,))
NT = ((1,), (1,))
TN = ((0,), (0,))
GELU_C = 0.7978845608028654
GELU_A = 0.044715


def dot(left, right, dims):
    return lax.dot_general(left, right, (dims, ((), ())), preferred_element_type=f32)


def iota(shape, axis):
    return lax.broadcasted_iota(jnp.int32, shape, axis)


def norm_scale(values):
    return lax.rsqrt(jnp.mean(values * values, axis=-1, keepdims=True) + EPS)


def row_of(ref):
    return ref[...].reshape(1, ref.shape[0])


def norm_back(values, gain, grad):
    scale = norm_scale(values)
    xhat = values * scale
    gxhat = grad * gain
    grad_in = scale * (gxhat - xhat * jnp.mean(gxhat * xhat, axis=-1, keepdims=True))
    return grad_in, xhat


def gelu_parts(u):
    square = u * u
    t = jnp.tanh(u * (GELU_C + (GELU_C * GELU_A) * square))
    half = 0.5 * (1.0 + t)
    slope = half + (0.5 * u) * (1.0 - t * t) * (GELU_C + (3.0 * GELU_C * GELU_A) * square)
    return u * half, slope


def split2(values):
    high = values.astype(bf16)
    return high, (values - high.astype(f32)).astype(bf16)


def params(limit=VMEM_LIMIT):
    return pltpu.CompilerParams(vmem_limit_bytes=limit)


def vmem():
    return pl.BlockSpec(memory_space=pltpu.VMEM)


def smem():
    return pl.BlockSpec(memory_space=pltpu.SMEM)


def cost_of(micros):
    return pl.CostEstimate(
        flops=int(micros * 1e9), bytes_accessed=int(micros * 1e5), transcendentals=0
    )


def call(kernel, outs, ins, scratch=(), micros=3, name=None, limit=24, out_specs=None):
    return pl.pallas_call(
        kernel,
        out_shape=outs,
        in_specs=ins,
        out_specs=out_specs
        or jax.tree.map(lambda o: smem() if o.dtype == jnp.int32 else vmem(), outs),
        scratch_shapes=list(scratch),
        compiler_params=params(limit << 20),
        cost_estimate=cost_of(micros),
        name=name,
    )


def sds(shape, dtype):
    return jax.ShapeDtypeStruct(shape, dtype)


def valid_rows(lengths, rows):
    index = lax.axis_index("ctx") * lax.axis_size("exp") + lax.axis_index("exp")
    return lengths[0] - index * rows


def route_kernel(n_experts, sc, routes_t, dy, router_t, places, pick, w3, w3_t, full, *pay):
    places[0] = lax.rem(lax.axis_index("ctx"), 2)
    rows = dy.shape[0]
    width = dy.shape[1]
    table = jnp.concatenate(
        [router_t[...], jnp.zeros((128 - n_experts, width), f32)], axis=0
    )
    high = table.astype(bf16).astype(f32)
    mid = (table - high).astype(bf16).astype(f32)
    low = table - high - mid
    table = high + pltpu.roll(mid, n_experts, 0) + pltpu.roll(low, 2 * n_experts, 0)
    w3_t[...] = table.astype(bf16)
    w3[...] = table.T.astype(bf16)
    first, second = routes_t[0:1, :], routes_t[1:2, :]
    eight = iota((8, rows), 0)
    named = jnp.where((first == eight) | (second == eight), 1.0, 0.0)
    upper = jnp.where(iota((rows, rows), 0) < iota((rows, rows), 1), 1.0, 0.0)
    rank = dot(named.astype(bf16), upper.astype(bf16), NN)
    slot = iota((CAP, rows), 0).astype(f32)
    for e in range(n_experts):
        hit = (named[e : e + 1] > 0.5) & (rank[e : e + 1] == slot)
        pick[e * CAP : (e + 1) * CAP, :] = jnp.where(hit, 1.0, 0.0).astype(bf16)
    all_pick = pick[...].astype(f32)
    valid = iota((1, rows), 1) < valid_rows(sc, rows)
    live = jnp.where(valid, all_pick, 0.0).astype(bf16)
    full[:, :width] = dot(live, dy[...], NN).astype(bf16)
    line = iota((128, rows), 0)
    kind = jnp.where(line < 3 * n_experts, lax.rem(line, n_experts), -1)
    pair = jnp.where((first == kind) | (second == kind), 1.0, 0.0).astype(bf16)
    full[:, width:] = dot(pick[...], pair, NT).astype(bf16)
    for k, piece in enumerate(pay):
        expert = lax.rem(lax.axis_index("exp") + k, n_experts)
        piece[...] = full[pl.ds(pl.multiple_of(expert * CAP, 16), CAP), :]


def head_index(n_heads):
    index = lax.axis_index("ctx") * lax.axis_size("exp") + lax.axis_index("exp")
    return lax.rem(index, n_heads)


def bias_tiles(rel, buckets, brow, tiles):
    n_tiles, side, _ = tiles.shape
    n_heads, n_buckets = rel.shape
    head = head_index(n_heads)
    ids = buckets[...]
    row = jnp.zeros(ids.shape, f32)
    for b in range(n_buckets):
        row = jnp.where(ids == b, rel[head, b], row)
    brow[:, :side] = jnp.zeros((1, side), f32)
    brow[:, side:] = row
    for o in range(n_tiles):
        wide = jnp.broadcast_to(brow[:, o * side : (o + 2) * side], (side, 2 * side))
        tiles[o] = pltpu.roll(wide, 0, axis=1, stride=1, stride_axis=0)[:, side:]


def at_tile(index, side):
    return index * side if isinstance(index, int) else pl.multiple_of(index * side, side)


def loop(count, body, state):
    if isinstance(count, int) and count <= 4:
        for i in range(count):
            state = body(i, state)
        return state
    return lax.fori_loop(0, count, body, state)


def attn_kernel(shifts, head_dim, sc, rel, *refs):
    n_pieces = len(shifts)
    pieces = refs[:n_pieces]
    gain, w_qkv, buckets = refs[n_pieces : n_pieces + 3]
    kept, (out_t, lse) = refs[n_pieces + 3 : n_pieces + 9], refs[n_pieces + 9 : n_pieces + 11]
    h1, qa, ka, va, qt, kt, vt, brow, tiles, window, weight, sem, sems = refs[n_pieces + 11 :]
    head = head_index(rel.shape[0])
    pair_at = pl.multiple_of((head // 2) * 6 * head_dim, 128)
    fetch = pltpu.make_async_copy(w_qkv.at[:, pl.ds(pair_at, 6 * head_dim)], window, sem)
    fetch.start()
    bias_tiles(rel, buckets, brow, tiles)
    n_exp = lax.axis_size("exp")
    n_x = lax.axis_size("ctx") // 2
    ctx, exp = lax.axis_index("ctx"), lax.axis_index("exp")

    def piece_start(b, o, k):
        if b < 0:
            return 0
        x_at = lax.rem(ctx // 2 + (n_x - b), n_x)
        core = lax.rem(lax.rem(ctx, 2) + o, 2)
        return ((x_at * 2 + core) * n_exp + lax.rem(exp + (n_exp - k), n_exp)) * 128

    n_tiles, side, _ = tiles.shape
    length = sc[0]

    def rows_in(x, start):
        x = x.astype(f32)
        h1[pl.ds(start, 128), :] = (x * norm_scale(x) * row_of(gain)).astype(bf16)

    def project(j, carry):
        group = 512
        start = at_tile(j, group)
        lane = iota((group, 128), 1)
        here = pl.ds(start, group)
        qkv = dot(h1[here, :], weight[...], NN).astype(bf16).astype(f32)
        q, k, v = qkv[:, :128] * 0.125, qkv[:, 128:256], qkv[:, 256:]
        live = jnp.where(start + iota((group, 128), 0) < length, 0.0, NEG)
        qa[here, :] = jnp.where(lane == head_dim, 1.0, q).astype(bf16)
        ka[here, :] = jnp.where(lane == head_dim, live, k).astype(bf16)
        va[here, :] = v.astype(bf16)
        qt[:, here] = q.T[:head_dim].astype(bf16)
        kt[:, here] = k.T[:head_dim].astype(bf16)
        vt[:, here] = v.T[:head_dim].astype(bf16)
        return carry

    for i, piece in enumerate(pieces):
        if piece.shape[0] == 128:
            rows_in(piece[...], pl.multiple_of(piece_start(*shifts[i]), 128))
        else:

            def step(j, carry, piece=piece):
                start = pl.multiple_of(j * 128, 128)
                rows_in(piece[pl.ds(start, 128), :], start)
                return carry

            lax.fori_loop(0, piece.shape[0] // 128, step, 0)
    fetch.wait()
    odd = lax.rem(head, 2) == 1
    for i in range(3):
        even_part = window[:, i * head_dim : (i + 1) * head_dim]
        odd_part = window[:, (3 + i) * head_dim : (4 + i) * head_dim]
        part = jnp.where(odd, odd_part.astype(f32), even_part.astype(f32)).astype(bf16)
        pad = jnp.zeros((window.shape[0], 128 - head_dim), bf16)
        weight[:, i * 128 : (i + 1) * 128] = jnp.concatenate([part, pad], axis=1)
    loop(h1.shape[0] // 512, project, 0)
    leave = [
        pltpu.make_async_copy(src, dst, sems.at[i])
        for i, (src, dst) in enumerate(zip((h1, qa, ka, va, qt, kt), kept))
    ]
    for copy in leave:
        copy.start()
    blocks = side // 128

    def one_query_tile(qi, carry):
        q_start = at_tile(qi, side)
        q = qa[pl.ds(q_start, side), :]

        def fold(k_start, offset, state, diagonal):
            top, total, acc = state
            scores = dot(ka[pl.ds(k_start, side), :], q, NT) + tiles[offset]
            if diagonal:
                scores = jnp.where(iota((side, side), 0) <= iota((side, side), 1), scores, NEG)
            new_top = jnp.maximum(top, jnp.max(scores, axis=0, keepdims=True))
            probs = jnp.exp(scores - new_top)
            scale = jnp.exp(top - new_top)
            total = total * scale + jnp.sum(probs, axis=0, keepdims=True)
            acc = acc * scale + dot(vt[:, pl.ds(k_start, side)], probs.astype(bf16), NN)
            return new_top, total, acc

        state = (
            jnp.full((1, side), NEG, f32),
            jnp.zeros((1, side), f32),
            jnp.zeros((head_dim, side), f32),
        )
        state = fold(q_start, 0, state, True)

        def earlier(kj, state):
            return fold(at_tile(kj, side), qi - kj, state, False)

        top, total, acc = loop(qi, earlier, state)
        result = (acc / total).astype(bf16)
        lse[:, pl.ds(q_start, side)] = top + jnp.log(total)
        for b in range(blocks):
            out_t[qi * blocks + b] = result[:, b * 128 : (b + 1) * 128]
        return carry

    loop(n_tiles, one_query_tile, 0)
    for copy in leave:
        copy.wait()


def attn_back_kernel(head_dim, n_dp, rel, *refs):
    qa, ka, va, qt, kt, out_t, grad_t, lse, h1_far, buckets, small = refs[:11]
    pay, weight_pay = refs[11:13]
    dq, dk, dv, full, brow, tiles, sums, diag, h1, sem = refs[13:]
    fetch = pltpu.make_async_copy(h1_far, h1, sem)
    fetch.start()
    n_tiles, side, _ = tiles.shape
    blocks = side // 128
    bias_tiles(rel, buckets, brow, tiles)
    sums[...] = jnp.zeros_like(sums)
    dk[...] = jnp.zeros_like(dk)
    dv[...] = jnp.zeros_like(dv)

    def one_query_tile(qi, carry):
        q_start = at_tile(qi, side)
        q = qa[pl.ds(q_start, side), :]
        q_t = qt[:, pl.ds(q_start, side)]
        g_t = jnp.concatenate([grad_t[qi * blocks + b] for b in range(blocks)], axis=1)
        o_t = jnp.concatenate([out_t[qi * blocks + b] for b in range(blocks)], axis=1)
        row_dots = jnp.sum(g_t.astype(f32) * o_t.astype(f32), axis=0, keepdims=True)
        norm = lse[:, pl.ds(q_start, side)]

        def fold(k_start, offset, acc, diagonal):
            where_k = pl.ds(k_start, side)
            scores = dot(ka[where_k, :], q, NT) + tiles[offset]
            probs = jnp.exp(scores - norm)
            if diagonal:
                probs = jnp.where(iota((side, side), 0) <= iota((side, side), 1), probs, 0.0)
            grad_prob = dot(va[where_k, :][:, :head_dim], g_t, NN)
            grad_score = probs * (grad_prob - row_dots)
            low = grad_score.astype(bf16)
            sums[offset] = sums[offset] + grad_score
            dv[:, where_k] = dv[:, where_k] + dot(g_t, probs.astype(bf16), NT)
            dk[:, where_k] = dk[:, where_k] + dot(q_t, low, NT)
            return acc + dot(kt[:, where_k], low, NN)

        acc = fold(q_start, 0, jnp.zeros((head_dim, side), f32), True)

        def earlier(kj, acc):
            return fold(at_tile(kj, side), qi - kj, acc, False)

        dq[:, pl.ds(q_start, side)] = loop(qi, earlier, acc)
        return carry

    loop(n_tiles, one_query_tile, 0)
    full[:head_dim, :] = (dq[...] * 0.125).astype(bf16)
    full[head_dim : 2 * head_dim, :] = dk[...].astype(bf16)
    full[2 * head_dim :, :] = dv[...].astype(bf16)
    for b in range(pay.shape[0]):
        pay[b] = full[:, b * 128 : (b + 1) * 128]
    flip = jnp.where(iota((128, 128), 0) + iota((128, 128), 1) == 127, 1.0, 0.0).astype(bf16)
    diag[...] = jnp.zeros_like(diag)
    for o in range(n_tiles):
        for a in range(blocks):
            turned = dot(flip, sums[o, a * 128 : (a + 1) * 128, :].astype(bf16), NN)
            wide = jnp.concatenate([turned, jnp.zeros((128, 128), f32)], axis=1)
            lined = pltpu.roll(wide, 0, axis=1, stride=1, stride_axis=0)
            first = (o + 1) * side - (a + 1) * 128
            where_d = slice(first, first + side + 128)
            diag[:, where_d] = diag[:, where_d] + jnp.sum(lined, axis=0, keepdims=True)
    ids = jnp.concatenate([buckets[...], jnp.full((1, side), -1, jnp.int32)], axis=1)
    ids = pltpu.roll(ids, side - 1, 1)
    hot = jnp.where(ids == iota((128, ids.shape[1]), 0), 1.0, 0.0).astype(bf16)
    high, low = split2(jnp.broadcast_to(diag[...], (8, diag.shape[1])))
    rel_grad = dot(high, hot, NT) + dot(low, hot, NT)
    fetch.wait()
    grad_w = dot(full[...], h1[...], NN).astype(bf16)
    n_pay, pay_rows, lanes = weight_pay.shape
    n_ctx = n_pay // n_dp
    rows = grad_w.shape[0] // n_ctx
    rel_row = jnp.concatenate([rel_grad, jnp.zeros((8, lanes - 128), f32)], axis=1)
    line = iota((16, lanes), 0)
    for d in range(n_dp):
        for c in range(n_ctx):
            here = slice(d * lanes, (d + 1) * lanes)
            weight_pay[d * n_ctx + c, :rows, :] = grad_w[c * rows : (c + 1) * rows, here]
            extra = jnp.where(line == 0, rel_row[0:1], 0.0)
            if c < 4:
                for r in range(2):
                    row = small[2 * c + r : 2 * c + r + 1, here]
                    extra = jnp.where(line == 8 + r, row, extra)
            weight_pay[d * n_ctx + c, rows:, :] = extra.astype(bf16)


def middle_kernel(n_heads, sc, recv, w_out, x, gain, pick, middle, *send):
    rows, width = x.shape
    attn_t = jnp.concatenate([recv[h] for h in range(n_heads)], axis=0)
    branch = dot(attn_t, w_out[...], TN)
    valid = iota((rows, 1), 0) < valid_rows(sc, rows)
    mid = x[...].astype(f32) + jnp.where(valid, branch, 0.0)
    middle[...] = mid
    h2 = (mid * norm_scale(mid) * row_of(gain)).astype(bf16)
    for k, piece in enumerate(send):
        expert = lax.rem(lax.axis_index("exp") + k, len(send))
        chosen = pick[pl.ds(pl.multiple_of(expert * CAP, 16), CAP), :]
        piece[...] = dot(chosen, h2, NN).astype(bf16)


def gate_of(h2, pay, width, w3, own):
    logits = dot(h2, w3, NN)
    sel = 2.0 * own - pay[:, width:].astype(f32)
    diff = jnp.sum(logits * sel, axis=1, keepdims=True)
    return 1.0 / (1.0 + jnp.exp(-diff)), sel


def own_lanes(expert, n_experts):
    lane = iota((1, 128), 1)
    return jnp.where((lane < 3 * n_experts) & (lane % n_experts == expert), 1.0, 0.0)


def expert_kernel(n_experts, h2, pay, w3, w3_t, w_up, w_down, *refs):
    mix, back = refs[:n_experts], refs[n_experts : 2 * n_experts]
    router, z_acc, in_acc, dz, gates, rows_out = refs[2 * n_experts :]
    step = pl.program_id(0)
    width = h2.shape[1]
    expert = lax.axis_index("exp")
    own = own_lanes(expert, n_experts)

    @pl.when(step == 0)
    def _():
        gate, _ = gate_of(h2[...], pay, width, w3[...], own)
        gates[...] = jnp.broadcast_to(gate, gates.shape)
        dz[...] = (gate * pay[:, :width].astype(f32)).astype(bf16)
        z_acc[...] = jnp.zeros_like(z_acc)
        in_acc[...] = jnp.zeros_like(in_acc)

    up = dot(h2[...], w_up[...], NN)
    act, slope = gelu_parts(up)
    grad_hidden = dot(dz[...], w_down[...], NT)
    grad_up = (grad_hidden * slope).astype(bf16)
    z_acc[...] += dot(act.astype(bf16), w_down[...], NN)
    in_acc[...] += dot(grad_up, w_up[...], NT)

    @pl.when(step == pl.num_programs(0) - 1)
    def _():
        gate = gates[:, 0:1]
        sel = 2.0 * own - pay[:, width:].astype(f32)
        z = z_acc[...].astype(bf16).astype(f32)
        rows_out[...] = (gate * z).astype(bf16)
        for k in range(n_experts):
            mix[k][...] = rows_out[k * CAP : (k + 1) * CAP, :]
        grad_gate = jnp.sum(pay[:, :width].astype(f32) * z, axis=1, keepdims=True)
        high, low = split2((gate * (1.0 - gate) * grad_gate) * sel)
        total = in_acc[...] + dot(high, w3_t[...], NN) + dot(low, w3_t[...], NN)
        rows_out[...] = total.astype(bf16)
        for k in range(n_experts):
            back[k][...] = rows_out[k * CAP : (k + 1) * CAP, :]
        router[...] = (dot(high, h2[...], TN) + dot(low, h2[...], TN))[:8]


def collect(pieces, pick):
    n_experts = len(pieces)
    total = None
    for k, piece in enumerate(pieces):
        expert = lax.rem(lax.axis_index("exp") + k, n_experts)
        chosen = pick[pl.ds(pl.multiple_of(expert * CAP, 16), CAP), :]
        part = dot(chosen, piece[...], TN)
        total = part if total is None else total + part
    return total


def middle_back_kernel(n_heads, n_experts, sc, *refs):
    back = refs[:n_experts]
    pick, middle, dy, gain, recv, w_out, router, dmid, grad_t, red, small = refs[n_experts:]
    rows, width = middle.shape
    grad_h2 = collect(back, pick)
    grad_in, xhat = norm_back(middle[...], row_of(gain), grad_h2)
    grad_mid = dy[...].astype(f32) + grad_in
    dmid[...] = grad_mid
    valid = iota((rows, 1), 0) < valid_rows(sc, rows)
    branch = jnp.where(valid, grad_mid, 0.0).astype(bf16)
    attn_t = jnp.concatenate([recv[h] for h in range(n_heads)], axis=0)
    heads = dot(w_out[...], branch, NT).astype(bf16)
    head_dim = width // n_heads
    for h in range(n_heads):
        grad_t[h] = heads[h * head_dim : (h + 1) * head_dim]
    for h in range(n_heads, grad_t.shape[0]):
        grad_t[h] = jnp.zeros((head_dim, rows), bf16)
    red[...] = dot(attn_t, branch, NN).astype(bf16)
    gains = jnp.sum(grad_h2 * xhat, axis=0, keepdims=True)
    line = iota((8, width), 0)
    moved = pltpu.roll(router[...], 1, 0)
    small[...] = jnp.where(line == 0, gains, jnp.where(line < 5, moved, 0.0))


def output_kernel(n_experts, sc, *refs):
    mix = refs[:n_experts]
    pick, middle, out = refs[n_experts:]
    rows = middle.shape[0]
    valid = iota((rows, 1), 0) < valid_rows(sc, rows)
    total = collect(mix, pick)
    out[...] = (middle[...] + jnp.where(valid, total, 0.0)).astype(bf16)


def token_grad_kernel(n_heads, recv, w_qkv, x, gain, dmid, out):
    grad_t = jnp.concatenate([recv[h] for h in range(n_heads)], axis=0)
    grad_h1 = dot(w_qkv[...], grad_t, NN).T
    grad_in, _ = norm_back(x[...].astype(f32), row_of(gain), grad_h1)
    out[...] = dmid[...] + grad_in


def load_rows(h_pieces, where, pays, h2, pay, sem):
    rows = h_pieces[0].shape[0]
    copies = []
    for i, piece in enumerate(h_pieces):
        here = pl.ds(i * rows, rows)
        source = pays[i] if len(pays) > 1 else pays[0].at[
            pl.ds(pl.multiple_of(where[i] * rows, 16), rows), :
        ]
        copies.append(pltpu.make_async_copy(piece, h2.at[here, :], sem.at[0, i]))
        copies.append(pltpu.make_async_copy(source, pay.at[here, :], sem.at[1, i]))
    return copies


def chip_index(a, b, o):
    n_dp = lax.axis_size("dp")
    n_x = lax.axis_size("ctx") // 2
    dp, ctx = lax.axis_index("dp"), lax.axis_index("ctx")
    core = lax.rem(lax.rem(ctx, 2) + o, 2)
    x_at = lax.rem(ctx // 2 + (n_x - b), n_x)
    return (lax.rem(dp + (n_dp - a), n_dp) * n_x + x_at) * 2 + core


def weight_grad_kernel(n_experts, keys, together, last, sc, *refs):
    n_pieces = len(keys)
    h_pieces = refs[:n_pieces]
    n_in = n_pieces + (1 if last else n_pieces)
    pays = refs[n_pieces:n_in]
    w3, w_up, w_down = refs[n_in : n_in + 3]
    if last:
        up_base, down_base, up_out, down_out, low = refs[n_in + 3 : n_in + 8]
    else:
        up_out, down_out = refs[n_in + 3 : n_in + 5]
    h2, pay, dz, hid_t, dup_t, sem = refs[-6:]
    step = pl.program_id(0)
    rows = h_pieces[0].shape[0]
    width = h2.shape[1]
    block = w_down.shape[0]
    copies = load_rows(h_pieces, [chip_index(*key) for key in keys], pays, h2, pay, sem)

    @pl.when(step == 0)
    def _():
        for copy in copies:
            copy.start()

    own = own_lanes(lax.axis_index("exp"), n_experts)
    up_t = w_up[...].T
    down = w_down[...]
    chunk = together * rows
    for i in range(n_pieces // together):
        here = slice(i * chunk, (i + 1) * chunk)

        @pl.when(step == 0)
        def _(i=i, here=here):
            for copy in copies[2 * together * i : 2 * together * (i + 1)]:
                copy.wait()
            part = pay[here, :]
            gate, _ = gate_of(h2[here, :], part, width, w3[...], own)
            dz[here, :] = (gate * part[:, :width].astype(f32)).astype(bf16)

        act, slope = gelu_parts(dot(up_t, h2[here, :], NT))
        hid_t[:, here] = act.astype(bf16)
        dup_t[:, here] = (dot(down, dz[here, :], NT) * slope).astype(bf16)
    grad_up = dot(dup_t[...], h2[...], NN)
    grad_down = dot(hid_t[...], dz[...], NN)
    if last:
        grad_up = grad_up + up_base[...]
        grad_down = grad_down + down_base[...]
        low[:block, :] = grad_up.astype(bf16)
        low[block:, :] = grad_down.astype(bf16)
        up_out[...] = grad_up.T
    else:
        up_out[...] = grad_up
    down_out[...] = grad_down


def fill_kernel(sc, low, *refs):
    up_out, down_out = refs[-2:]
    block = down_out.shape[0]
    up_out[...] = low[:block, :].astype(f32).T
    down_out[...] = low[block:, :].astype(f32)


def assemble_kernel(keys, rows, n_groups, head_cols, *refs):
    n_pieces = len(keys)
    pieces = refs[:n_pieces]
    w_qkv, gain, grad, gain_grad, rel_grad, gain2_grad, router_grad = refs[
        n_pieces : n_pieces + 7
    ]
    turned, rel_t, stage, acc, sem = refs[n_pieces + 7 :]
    lanes = pieces[0].shape[-1]
    acc[...] = jnp.zeros_like(acc)
    n_dp, n_exp = lax.axis_size("dp"), lax.axis_size("exp")
    n_x = lax.axis_size("ctx") // 2
    dp, ctx, exp = (lax.axis_index(name) for name in ("dp", "ctx", "exp"))
    rel_t[...] = jnp.zeros_like(rel_t)
    for piece, ids in zip(pieces, keys):
        for i, (a, b, o, k) in enumerate(ids):
            d = lax.rem(dp + (n_dp - a), n_dp)
            c = lax.rem(ctx // 2 + (n_x - b), n_x) * 2 + lax.rem(lax.rem(ctx, 2) + o, 2)
            e = lax.rem(exp + (n_exp - k), n_exp)
            lane_at = pl.multiple_of(d * lanes, 128)
            for g in range(n_groups):
                head = g * n_exp + e
                row_at = pl.multiple_of(head * head_cols + c * rows, 16)
                turned[pl.ds(row_at, rows), pl.ds(lane_at, lanes)] = piece[
                    i, g * rows : (g + 1) * rows, :
                ]
                rel_t[pl.ds(head, 1), :] = piece[
                    i, n_groups * rows + g : n_groups * rows + g + 1, :128
                ].astype(f32)
            first = n_groups * rows + 8
            where_s = pl.ds(lane_at, lanes)
            small = piece[i, first : first + 8, :].astype(f32)
            acc[c, :, where_s] = acc[c, :, where_s] + small
    rel_grad[...] = rel_t[: rel_grad.shape[0], : rel_grad.shape[1]]
    width, columns = grad.shape
    gain2_grad[...] = acc[0, 0:1, :].reshape(width)
    for e in range(router_grad.shape[0]):
        router_grad[e : e + 1, :] = acc[(e + 1) // 2, (e + 1) % 2 : (e + 1) % 2 + 1, :]
    copies = []
    for i, a in enumerate(range(0, width, 128)):
        total = jnp.zeros((128, 128), f32)
        for b in range(0, columns, 128):
            tile = turned[b : b + 128, a : a + 128].astype(f32).T
            stage[a : a + 128, b : b + 128] = tile
            total = total + tile * w_qkv[a : a + 128, b : b + 128].astype(f32)
        where_a = pl.ds(a, 128)
        copy = pltpu.make_async_copy(stage.at[where_a, :], grad.at[where_a, :], sem.at[i])
        copy.start()
        copies.append(copy)
        sums = jnp.sum(total.T, axis=0, keepdims=True)
        sums = sums / gain[a : a + 128].reshape(1, 128)
        gain_grad[a : a + 128] = sums.reshape(128)
    for copy in copies:
        copy.wait()


def shard_kernel(n_dp, n_groups, summed, shard):
    n_ctx = summed.shape[0] // n_dp
    part = summed.shape[1] - 16
    line = iota((16, summed.shape[2]), 0)
    extra = jnp.zeros(line.shape, f32)
    for i in range(summed.shape[0]):
        extra = extra + summed[i, part:, :].astype(f32)
    extra = jnp.where(line >= 8, extra, 0.0)
    for g in range(n_groups):
        total = summed[g].astype(f32)
        for d in range(1, n_dp):
            total = total + summed[d * n_ctx + g].astype(f32)
        shard[0, g * part : (g + 1) * part, :] = total[:part].astype(bf16)
        extra = jnp.where(line == g, total[part : part + 1], extra)
    shard[0, n_groups * part :, :] = extra.astype(bf16)


def reduced_kernel(red, attn_out):
    attn_out[...] = red[...].astype(f32)


def after(value, *others):
    return lax.optimization_barrier((value, others))[0]


def on_device(
    n_dp,
    n_ctx,
    n_exp,
    tokens,
    lengths,
    routes,
    buckets,
    cotangent,
    attn_gain,
    w_qkv,
    w_attn_out,
    rel_bias,
    ffn_gain,
    w_router,
    w_up,
    w_down,
):
    x = tokens[0]
    dy = cotangent[0]
    rows, width = x.shape
    seq = buckets.shape[0]
    n_buckets, n_heads = rel_bias.shape
    head_dim = width // n_heads
    n_experts = w_router.shape[1]
    ff = w_up.shape[2]
    n_slot = n_ctx * n_exp
    n_groups = n_heads // n_exp
    n_x = n_ctx // 2
    small = n_x == 2 and n_dp == 2
    side = 512 if seq <= 2048 else 256
    n_tiles = seq // side
    slot_rows = n_experts * CAP
    slot_axes, all_chips = ("ctx", "exp"), ("dp", "ctx")

    def ring(v, shift):
        return lax.ppermute(v, "exp", [(i, (i + shift) % n_exp) for i in range(n_exp)])

    def swap(v):
        return lax.ppermute(v, "ctx", [(i, i ^ 1) for i in range(n_ctx)])

    def chips(v, a, b):
        perm = []
        for d in range(n_dp):
            for c in range(n_ctx):
                to = ((d + a) % n_dp) * n_ctx + ((c // 2 + b) % n_x) * 2 + c % 2
                perm.append((d * n_ctx + c, to))
        return lax.ppermute(v, all_chips, perm)

    def exchange(v, axes):
        return lax.all_to_all(v, axes, split_axis=0, concat_axis=0, tiled=True)

    def to_experts(parts):
        return [parts[0]] + [ring(parts[k], k) for k in range(1, n_exp)]

    def from_experts(parts):
        return [parts[0]] + [ring(parts[k], n_exp - k) for k in range(1, n_exp)]

    keys = [(a, b, o) for o in (0, 1) for a, b in ((0, 0), (0, 1), (1, 0), (1, 1))]

    with jax.named_scope("routing"):
        places, pick, w3, w3_t, _, *pay = call(
            functools.partial(route_kernel, n_experts),
            [
                sds((1,), jnp.int32),
                sds((slot_rows, rows), bf16),
                sds((width, 128), bf16),
                sds((128, width), bf16),
                sds((slot_rows, width + 128), bf16),
            ]
            + [sds((CAP, width + 128), bf16)] * n_experts,
            [smem()] + [vmem()] * 3,
            name="routing",
        )(lengths, routes[0].T, dy, w_router.T)

    with jax.named_scope("gather_tokens"):
        if small:
            column = [(x, 0, 0), (ring(after(x, pick), 1), 0, 1)]
            column += [(ring(x, k), 0, k) for k in range(2, n_exp)]
            onward = [v for v, _, _ in column]
            onward[-1] = after(onward[-1], pay)
            pieces = column + [(chips(v, 0, 1), 1, k) for k, v in enumerate(onward)]
            pieces = [(v, b, 0, k) for v, b, k in pieces]
            arrived = to_experts(after(pay, pieces[-1][0]))
            pieces = pieces + [(swap(v), b, 1, k) for v, b, _, k in pieces]
            blocks = [v for v, _, _, _ in pieces]
            shifts = [ids for _, *ids in pieces]
        else:
            blocks = [lax.all_gather(x, slot_axes, axis=0, tiled=True)]
            shifts = [(-1, 0, 0)]
            arrived = to_experts(pay)

    with jax.named_scope("attention"):
        bucket_row = buckets.reshape(1, seq)
        blocks[-1] = after(blocks[-1], bucket_row)
        attn_outs = (
            sds((seq, width), bf16),
            sds((seq, 128), bf16),
            sds((seq, 128), bf16),
            sds((seq, 128), bf16),
            sds((head_dim, seq), bf16),
            sds((head_dim, seq), bf16),
            sds((n_slot, head_dim, 128), bf16),
            sds((1, seq), f32),
        )
        any_spec = pl.BlockSpec(memory_space=pl.ANY)
        h1, qa, ka, va, qt, kt, out_t, lse = call(
            functools.partial(attn_kernel, shifts, head_dim),
            attn_outs,
            [smem(), smem()] + [vmem()] * (len(blocks) + 1) + [any_spec, vmem()],
            [pltpu.VMEM(o.shape, o.dtype) for o in attn_outs[:6]]
            + [
                pltpu.VMEM((head_dim, seq), bf16),
                pltpu.VMEM((1, seq + side), f32),
                pltpu.VMEM((n_tiles, side, side), f32),
                pltpu.VMEM((width, 6 * head_dim), bf16),
                pltpu.VMEM((width, 384), bf16),
                pltpu.SemaphoreType.DMA,
                pltpu.SemaphoreType.DMA((6,)),
            ],
            micros=10,
            name="attention",
            limit=58,
            out_specs=(any_spec,) * 6 + (vmem(),) * 2,
        )(lengths, rel_bias.T, *blocks, attn_gain, w_qkv, bucket_row)
        attn_in = exchange(out_t, slot_axes)
        pay_in = jnp.concatenate([arrived[0]] + [after(v, out_t) for v in arrived[1:]])

    with jax.named_scope("middle"):
        piece_shape = sds((CAP, width), bf16)
        middle, *send = call(
            functools.partial(middle_kernel, n_heads),
            [sds((rows, width), f32)] + [piece_shape] * n_experts,
            [smem()] + [vmem()] * 5,
            name="middle",
        )(lengths, attn_in, w_attn_out, x, ffn_gain, pick)
        h2_in = jnp.concatenate(to_experts(send))

    with jax.named_scope("experts"):
        block = 1536
        row_spec = pl.BlockSpec((slot_rows, width), lambda i: (0, 0))
        piece_spec = pl.BlockSpec((CAP, width), lambda i: (0, 0))
        *parts, router = pl.pallas_call(
            functools.partial(expert_kernel, n_experts),
            out_shape=[piece_shape] * (2 * n_experts)
            + [sds((8, width), f32)],
            grid_spec=pltpu.PrefetchScalarGridSpec(
                num_scalar_prefetch=0,
                grid=(ff // block,),
                in_specs=[
                    row_spec,
                    pl.BlockSpec((slot_rows, width + 128), lambda i: (0, 0)),
                    pl.BlockSpec((width, 128), lambda i: (0, 0)),
                    pl.BlockSpec((128, width), lambda i: (0, 0)),
                    pl.BlockSpec((width, block), lambda i: (0, i)),
                    pl.BlockSpec((block, width), lambda i: (i, 0)),
                ],
                out_specs=[piece_spec] * (2 * n_experts)
                + [pl.BlockSpec((8, width), lambda i: (0, 0))],
                scratch_shapes=[
                    pltpu.VMEM((slot_rows, width), f32),
                    pltpu.VMEM((slot_rows, width), f32),
                    pltpu.VMEM((slot_rows, width), bf16),
                    pltpu.VMEM((slot_rows, 128), f32),
                    pltpu.VMEM((slot_rows, width), bf16),
                ],
            ),
            compiler_params=params(),
            cost_estimate=cost_of(12),
            name="experts",
        )(h2_in, pay_in, w3, w3_t, w_up[0], w_down[0])
        mix_parts, back_parts = parts[:n_experts], parts[n_experts:]
        back_in = from_experts(back_parts)

    shares = n_dp * n_ctx
    with jax.named_scope("expert_weight_grads"):
        if small:
            pay_all = lax.all_gather(pay_in, all_chips, axis=0, tiled=True)
            beside = [chips(h2_in, a, b) for a, b in ((0, 1), (1, 0), (1, 1))]
            block = 512
            n_parts = ff // (2 * block)
            full_shapes = [sds((width, ff), f32), sds((ff, width), f32)]

            def half_specs(other):
                def at(i, s):
                    return (1 - s[0] if other else s[0]) * n_parts + i

                return (
                    pl.BlockSpec((width, block), lambda i, s: (0, at(i, s))),
                    pl.BlockSpec((block, width), lambda i, s: (at(i, s), 0)),
                )

            low_spec = pl.BlockSpec((2 * block, width), lambda i, s: (i, 0))

            base_spec = pl.BlockSpec((block, width), lambda i, s: (i, 0))
            base_shape = sds((ff // 2, width), f32)

            def weight_half(pieces, pays, keys, base, micros):
                specs = half_specs(False)
                count = len(pieces) * slot_rows
                shapes, outs = [base_shape] * 2, [base_spec] * 2
                if base:
                    shapes, outs = full_shapes + [sds((ff, width), bf16)], [*specs, low_spec]
                return pl.pallas_call(
                    functools.partial(weight_grad_kernel, n_experts, keys, 2, bool(base)),
                    out_shape=shapes,
                    grid_spec=pltpu.PrefetchScalarGridSpec(
                        num_scalar_prefetch=1,
                        grid=(n_parts,),
                        in_specs=[any_spec] * (len(pieces) + len(pays))
                        + [pl.BlockSpec((width, 128), lambda i, s: (0, 0)), *specs]
                        + [base_spec] * len(base),
                        out_specs=outs,
                        scratch_shapes=[
                            pltpu.VMEM((count, width), bf16),
                            pltpu.VMEM((count, width + 128), bf16),
                            pltpu.VMEM((count, width), bf16),
                            pltpu.VMEM((block, count), bf16),
                            pltpu.VMEM((block, count), bf16),
                            pltpu.SemaphoreType.DMA((2, len(pieces))),
                        ],
                    ),
                    compiler_params=params(),
                    cost_estimate=cost_of(micros),
                    name="weight_grads",
                )(places, *pieces, *pays, w3, w_up[0], w_down[0], *base)

            def weight_fill(low, grads):
                return pl.pallas_call(
                    fill_kernel,
                    out_shape=full_shapes,
                    grid_spec=pltpu.PrefetchScalarGridSpec(
                        num_scalar_prefetch=1,
                        grid=(n_parts,),
                        in_specs=[low_spec, any_spec, any_spec],
                        out_specs=half_specs(True),
                    ),
                    input_output_aliases={2: 0, 3: 1},
                    compiler_params=params(),
                    cost_estimate=cost_of(8),
                    name="fill",
                )(places, low, *grads)


            pays = [pay_in, swap(pay_in)]
            base = weight_half([h2_in, swap(h2_in)], pays, keys[::4], (), 11)
            back_in[0] = after(back_in[0], beside, base, pay_all)

    with jax.named_scope("middle_back"):
        dmid, grad_t, red, sums = call(
            functools.partial(middle_back_kernel, n_heads, n_experts),
            (
                sds((rows, width), f32),
                sds((n_slot, head_dim, rows), bf16),
                sds((width, width), bf16),
                sds((8, width), f32),
            ),
            [smem()] + [vmem()] * (7 + n_experts),
            name="middle_back",
        )(lengths, *back_in, pick, middle, dy, ffn_gain, attn_in, w_attn_out, router)
        grad_in = exchange(grad_t, slot_axes)

    if small:
        with jax.named_scope("expert_weight_grads"):
            beside = [after(v, grad_t) for v in beside]
            pieces = beside + [swap(v) for v in beside]
            *grads, low = weight_half(pieces, [pay_all], keys[1:4] + keys[5:], base, 8)
            share = lax.psum_scatter(red, all_chips, scatter_dimension=0, tiled=True)
            grad_in = after(grad_in, low, share)
            others = [ring(share, k) for k in range(1, n_exp)]

    with jax.named_scope("attention_back"):
        part = 3 * head_dim // n_ctx
        lanes = width // n_dp
        dqkv, weight_pay = call(
            functools.partial(attn_back_kernel, head_dim, n_dp),
            (sds((n_slot, 3 * head_dim, rows), bf16), sds((shares, part + 16, lanes), bf16)),
            [smem()] + [vmem()] * 8 + [any_spec, vmem(), vmem()],
            [
                pltpu.VMEM((head_dim, seq), f32),
                pltpu.VMEM((head_dim, seq), f32),
                pltpu.VMEM((head_dim, seq), f32),
                pltpu.VMEM((3 * head_dim, seq), bf16),
                pltpu.VMEM((1, seq + side), f32),
                pltpu.VMEM((n_tiles, side, side), f32),
                pltpu.VMEM((n_tiles, side, side), f32),
                pltpu.VMEM((1, seq + side), f32),
                pltpu.VMEM((seq, width), bf16),
                pltpu.SemaphoreType.DMA,
            ],
            micros=11,
            name="attention_back",
            limit=58,
        )(rel_bias.T, qa, ka, va, qt, kt, out_t, grad_in, lse, h1, bucket_row, sums)
        if small:
            weight_pay = after(weight_pay, others)
            share = share.astype(f32) + others[0] + others[1] + others[2]
            share = after(share, weight_pay).astype(bf16)
        else:
            mix_in = from_experts(mix_parts)
        summed = exchange(weight_pay, all_chips)
        if small:
            summed = after(summed, share)

    with jax.named_scope("projection_grad"):
        shard = call(
            functools.partial(shard_kernel, n_dp, n_groups),
            sds((1, n_groups * part + 16, lanes), bf16),
            [vmem()],
            name="shard",
        )(summed)
        if small:
            column = [ring(shard, k) for k in range(1, n_exp)]
            column = jnp.concatenate([shard] + column)
            low_in = swap(after(low, weight_pay))
            column = after(column, low_in)
            mix_in = from_experts([after(v, column) for v in mix_parts])


    if small:
        with jax.named_scope("expert_weight_grads"):
            grad_up, grad_down = weight_fill(low_in, grads)
    else:
        with jax.named_scope("expert_weight_grads"):
            own = own_lanes(lax.axis_index("exp"), n_experts)
            gate, _ = gate_of(h2_in, pay_in, width, w3, own)
            dz = (gate * pay_in[:, :width].astype(f32)).astype(bf16)
            act, slope = gelu_parts(dot(h2_in, w_up[0], NN))
            dup = (dot(dz, w_down[0], NT) * slope).astype(bf16)
            grad_up = lax.psum(dot(h2_in, dup, TN).astype(bf16), all_chips).astype(f32)
            grad_down = lax.psum(dot(act.astype(bf16), dz, TN).astype(bf16), all_chips)
            grad_down = grad_down.astype(f32)

    with jax.named_scope("output"):
        output = call(
            functools.partial(output_kernel, n_experts),
            sds((rows, width), bf16),
            [smem()] + [vmem()] * (2 + n_experts),
            micros=0.2,
            name="output",
        )(lengths, *mix_in, pick, middle)

    with jax.named_scope("token_grads"):
        if small:
            beside_x = chips(column, 0, 1)
            dqkv = after(dqkv, beside_x)
        dqkv_in = exchange(dqkv, slot_axes)
        grad_tokens = call(
            functools.partial(token_grad_kernel, n_heads),
            sds((rows, width), f32),
            [vmem()] * 5,
            name="token_grads",
        )(dqkv_in, w_qkv, x, attn_gain, dmid)

    with jax.named_scope("output_projection_grad"):
        if small:
            reduced = lax.all_gather(share, all_chips, axis=0, tiled=True)
        else:
            reduced = lax.psum(red, ("dp", "ctx", "exp"))
            sums = lax.psum(sums, ("dp", "ctx", "exp"))
            grad_ffn_gain, grad_router = sums[0], sums[1 : 1 + n_experts].T
        grad_attn_out = call(
            reduced_kernel,
            sds((width, width), f32),
            [vmem()],
            micros=0.2,
            name="reduced",
        )(reduced)

    with jax.named_scope("projection_grad"):
        if small:
            wide = [(column, 0, 0, range(n_exp))]
            wide.append((beside_x, 0, 1, range(n_exp)))
            wide.append((chips(column, 1, 0), 1, 0, range(n_exp)))
            wide.append((chips(beside_x, 1, 0), 1, 1, range(n_exp)))
            early = (grad_up, grad_down, grad_attn_out, mix_in)
            wide = [(after(v, early), a, b, ks) for v, a, b, ks in wide]
            final = [v for v, _, _, _ in wide] + [swap(v) for v, _, _, _ in wide]
            keys = [[(a, b, o, k) for k in ks] for o in (0, 1) for _, a, b, ks in wide]
            grad_qkv, grad_attn_gain, grad_rel, grad_ffn_gain, grad_router = call(
                functools.partial(assemble_kernel, keys, part, n_groups, 3 * head_dim),
                (
                    sds((width, 3 * width), f32),
                    sds((width,), f32),
                    sds((n_heads, n_buckets), f32),
                    sds((width,), f32),
                    sds((n_experts, width), f32),
                ),
                [vmem()] * (len(final) + 2),
                [
                    pltpu.VMEM((3 * width, width), bf16),
                    pltpu.VMEM((128, 128), f32),
                    pltpu.VMEM((width, 3 * width), f32),
                    pltpu.VMEM((n_ctx, 8, width), f32),
                    pltpu.SemaphoreType.DMA((width // 128,)),
                ],
                micros=6,
                name="assemble",
                limit=32,
                out_specs=(any_spec,) + (vmem(),) * 4,
            )(*final, w_qkv, attn_gain)
            grad_rel, grad_router = grad_rel.T, grad_router.T
        else:
            every = lax.all_gather(shard[0], ("dp", "ctx", "exp"), axis=0, tiled=False)
            every = every.reshape(n_dp, n_ctx, n_exp, n_groups * part + 16, lanes).astype(f32)
            main = every[:, :, :, : n_groups * part]
            main = main.reshape(n_dp, n_ctx, n_exp, n_groups, part, lanes)
            grad_qkv = main.transpose(0, 5, 3, 2, 1, 4).reshape(width, 3 * width)
            rel_rows = every[0, 0, :, n_groups * part : n_groups * (part + 1), :n_buckets]
            grad_rel = rel_rows.transpose(2, 1, 0).reshape(n_buckets, n_heads)
            grad_attn_gain = jnp.sum(grad_qkv * w_qkv.astype(f32), axis=1) / attn_gain

    return (
        output[None],
        grad_tokens[None],
        grad_attn_gain,
        grad_qkv,
        grad_attn_out,
        grad_rel,
        grad_ffn_gain,
        grad_router,
        grad_up[None],
        grad_down[None],
    )


def solution(mesh):
    sizes = dict(mesh.shape)
    by_token = P("dp", ("ctx", "exp"), None)
    by_expert = P("exp", None, None)
    return jax.shard_map(
        functools.partial(on_device, sizes["dp"], sizes["ctx"], sizes["exp"]),
        mesh=mesh,
        in_specs=(
            by_token,
            P("dp"),
            by_token,
            P(),
            by_token,
            P(),
            P(),
            P(),
            P(),
            P(),
            P(),
            by_expert,
            by_expert,
        ),
        out_specs=(
            by_token,
            by_token,
            P(),
            P(),
            P(),
            P(),
            P(),
            P(),
            by_expert,
            by_expert,
        ),
        check_vma=False,
    )
```
